32 devices in a mesh: groups: 2 (over x), tm: 16 (over z, y, core).
Axes of the slice: x: 2, y: 2, z: 4, core: 2. Of those that a mesh axis runs over, the one named last changes fastest.
Arguments:
- receptance: bfloat16 [4096, 1024], P(('groups', 'tm')), parts along dimension 0, may hold values from -0.75 to 0.75
- key_input: bfloat16 [4096, 1024], P(('groups', 'tm')), parts along dimension 0, may hold values from -6 to 6
- values: bfloat16 [4096, 1024], P(('groups', 'tm')), parts along dimension 0, may hold values from -6 to 6
- log_decay: bfloat16 [4096, 1024], P(('groups', 'tm')), parts along dimension 0, may hold values from -1 to 0
- kappa_raw: bfloat16 [4096, 1024], P(('groups', 'tm')), parts along dimension 0, may hold values from -6 to 6
- removal: bfloat16 [4096, 1024], P(('groups', 'tm')), parts along dimension 0, may hold values from 0 to 1
- initial_state: float32 [32, 64, 64], P('groups'), parts along dimension 0, may hold values from -3 to 3
- out_weight: bfloat16 [1024, 1024], replicated, may hold values from -0.1875 to 0.1875
- grad_output: bfloat16 [1024, 4096], P('tm', 'groups'), parts along dimension 1, may hold values from -6 to 6
Outputs:
- grad_receptance: bfloat16 [4096, 1024], P(('groups', 'tm')), parts along dimension 0
- grad_keys: bfloat16 [4096, 1024], P(('groups', 'tm')), parts along dimension 0
- grad_values: bfloat16 [4096, 1024], P(('groups', 'tm')), parts along dimension 0
- grad_weight: float32 [2048, 1024], P(('groups', 'tm')), parts along dimension 0
The draws below stay inside these ranges and needn't reach their ends.
There are 2 independent parts, one for each index of `groups`. The reference program is written for one: setup_inputs(seed, part) draws one part's arguments, and reference() takes and returns one part's arrays. A program takes and returns all parts, laid end to end along the dimension named above; an argument that names none is the same for every part. Nothing has to cross between parts.
All inputs are finite; a program needn't handle non-finite values.
Results may differ from the reference program's by a relative error of at most 0.0029.
Values may be sent and summed in bfloat16 or wider, within the bound.
A program may use at most 320 MiB of HBM per device.

```python
import math
import jax
import jax.numpy as jnp
from jax import lax

HEAD_COUNT = 16
HEAD_SIZE = 64
D = 1024
FRAME_COUNT = 2048


def slow_heads(key, slow_share):
    return jax.random.uniform(jax.random.fold_in(key, 17), (HEAD_COUNT,)) < slow_share


def draw_log_decay(key, part):
    key_rate, key_fast, key_rough = jax.random.split(jax.random.fold_in(key, 23), 3)
    slow_share = 0.5
    is_slow = slow_heads(key, slow_share)
    slow_rate = jax.random.uniform(key_rate, (HEAD_COUNT,), minval=0.05, maxval=0.3) * math.log(10.0) / FRAME_COUNT
    fast_rate = jax.random.uniform(key_fast, (HEAD_COUNT,), minval=1.0 / 50.0, maxval=1.0 / 30.0)
    base_rate = jnp.where(is_slow, slow_rate, fast_rate)
    roughness = jax.random.uniform(key_rough, (FRAME_COUNT, HEAD_COUNT, HEAD_SIZE), minval=0.7, maxval=1.4)
    return (-(base_rate[None, :, None] * roughness)).reshape(FRAME_COUNT, HEAD_COUNT * HEAD_SIZE).astype(jnp.bfloat16)


def draw_removal(key, part):
    key_fast, key_back, key_select_mask, key_magnitude = jax.random.split(jax.random.fold_in(key, 29), 4)
    slow_share = 0.5
    is_slow = slow_heads(key, slow_share)
    fast_level = jax.random.uniform(key_fast, (FRAME_COUNT, HEAD_COUNT, HEAD_SIZE), minval=0.05, maxval=0.6)
    ambient_level = jax.random.uniform(key_back, (FRAME_COUNT, HEAD_COUNT, HEAD_SIZE), minval=0.0, maxval=1.0) * (HEAD_SIZE / FRAME_COUNT)
    spike_mask = jax.random.uniform(key_select_mask, (FRAME_COUNT, HEAD_COUNT)) < 1.1 * HEAD_SIZE / FRAME_COUNT
    spike_level = jax.random.uniform(key_magnitude, (FRAME_COUNT, HEAD_COUNT, HEAD_SIZE), minval=0.3, maxval=0.6)
    gradual_level = jnp.where(spike_mask[:, :, None], spike_level, ambient_level)
    chosen = jnp.where(is_slow[None, :, None], gradual_level, fast_level)
    return chosen.reshape(FRAME_COUNT, HEAD_COUNT * HEAD_SIZE).astype(jnp.bfloat16)


def block_levels(stream_key, dims, cuts, smallest, largest):
    gain, own = 1.0, jax.random.fold_in(stream_key, 6)
    for dim, parts in cuts:
        heights = jnp.exp(jax.random.uniform(jax.random.fold_in(own, dim), (parts,), jnp.float32, smallest / len(cuts), largest / len(cuts)))
        gain = gain * jnp.repeat(heights, dims[dim] // parts).reshape([-1 if axis == dim else 1 for axis in range(len(dims))])
    return gain


def bell_draw(key, dims, width, bound, cuts=(), kind=jnp.bfloat16):
    result = jax.random.normal(key, dims, jnp.float32) * width
    if len(cuts) > 0:
        result = block_levels(key, dims, cuts, -0.22, 0.18) * result
    return jnp.clip(result, min=-bound, max=bound).astype(kind)


def setup_inputs(seed: int = 0, part: int = 0) -> dict:
    key_of = jax.random.split(jax.random.key(seed), 10)
    own_keys = jax.random.split(jax.random.fold_in(key_of[9], part), 10)
    return {
        "receptance": bell_draw(own_keys[0], (FRAME_COUNT, D), 0.125, 0.75, ((0, 16),)),
        "key_input": bell_draw(own_keys[1], (FRAME_COUNT, D), 1.0, 6.0, ((0, 16),)),
        "values": bell_draw(own_keys[2], (FRAME_COUNT, D), 1.0, 6.0, ((0, 16),)),
        "log_decay": draw_log_decay(jax.random.fold_in(jax.random.fold_in(key_of[9], part), 71), part),
        "kappa_raw": bell_draw(own_keys[4], (FRAME_COUNT, D), 1.0, 6.0, ((0, 16),)),
        "removal": draw_removal(jax.random.fold_in(jax.random.fold_in(key_of[9], part), 71), part),
        "initial_state": bell_draw(own_keys[6], (HEAD_COUNT, HEAD_SIZE, HEAD_SIZE), 0.5, 3.0, (), jnp.float32),
        "out_weight": bell_draw(key_of[7], (D, D), D ** -0.5, 0.1875),
        "grad_output": bell_draw(own_keys[8], (D, FRAME_COUNT), 1.0, 6.0, ((0, 16),)),
    }


def make_frames(receptance, key_input, values, log_decay, kappa_raw, removal, grad_y):
    frame_count = receptance.shape[0]
    head_shape = (frame_count, HEAD_COUNT, HEAD_SIZE)
    log_part = log_decay.astype(jnp.float32).reshape(head_shape)
    decays = jnp.exp(log_part)
    key_scale = jnp.sqrt(-jnp.expm1(log_part))
    raw_key = kappa_raw.astype(jnp.float32).reshape(head_shape)
    unit_key = raw_key / jnp.sqrt(lax.optimization_barrier(jnp.sum(raw_key * raw_key, -1, keepdims=True)) + 1e-06)
    gated_key = removal.astype(jnp.float32).reshape(head_shape) * unit_key
    keys_in = key_input.astype(jnp.float32).reshape(head_shape) * key_scale
    value_rows = values.astype(jnp.float32).reshape(head_shape)
    recept_rows = receptance.astype(jnp.float32).reshape(head_shape)
    grad_rows = grad_y.reshape(head_shape)
    return (decays, unit_key, gated_key, value_rows, keys_in, recept_rows, grad_rows, key_scale)

def advance(current, decays, unit_key, gated_key, value_rows, keys_in):
    projected = lax.optimization_barrier(jnp.sum(current * unit_key[..., None, :], -1))
    return current * decays[..., None, :] - projected[..., :, None] * gated_key[..., None, :] + value_rows[..., :, None] * keys_in[..., None, :]

def pull_back(grad_state, decays, unit_key, gated_key):
    pulled = lax.optimization_barrier(jnp.sum(grad_state * gated_key[..., None, :], -1))
    return grad_state * decays[..., None, :] - pulled[..., :, None] * unit_key[..., None, :]

def forward_step(current, frame_slice):
    decays, unit_key, gated_key, value_rows, keys_in, recept_rows, grad_rows, key_scale = frame_slice
    current = advance(current, decays, unit_key, gated_key, value_rows, keys_in)
    out_y = lax.optimization_barrier(jnp.sum(current * recept_rows[:, None, :], -1))
    grad_r = lax.optimization_barrier(jnp.sum(current * grad_rows[:, :, None], -2))
    return (current, (out_y, grad_r))

def backward_step(incoming, frame_slice):
    decays, unit_key, gated_key, value_rows, keys_in, recept_rows, grad_rows, key_scale = frame_slice
    grad_state = incoming + grad_rows[:, :, None] * recept_rows[:, None, :]
    grad_v = lax.optimization_barrier(jnp.sum(grad_state * keys_in[:, None, :], -1))
    grad_k = lax.optimization_barrier(jnp.sum(grad_state * value_rows[:, :, None], -2)) * key_scale
    return (pull_back(grad_state, decays, unit_key, gated_key), (grad_v, grad_k))

def reference(receptance, key_input, values, log_decay, kappa_raw, removal, initial_state, out_weight, grad_output):
    frame_count = receptance.shape[0]
    grad_y = lax.dot_general(grad_output, out_weight, (((0,), (1,)), ((), ())), preferred_element_type=jnp.float32)
    frames = make_frames(receptance, key_input, values, log_decay, kappa_raw, removal, grad_y)
    last_state, (out_y, grad_r) = lax.scan(forward_step, initial_state.astype(jnp.float32), frames)
    zero_state = jnp.zeros((HEAD_COUNT, HEAD_SIZE, HEAD_SIZE), jnp.float32)
    last_grad, (grad_v, grad_k) = lax.scan(backward_step, zero_state, frames, reverse=True)
    y_low = out_y.reshape(frame_count, HEAD_COUNT * HEAD_SIZE).astype(jnp.bfloat16)
    loss_scale = 1.0 / math.sqrt(frame_count)
    grad_weight = lax.dot_general(y_low, grad_output, (((0,), (1,)), ((), ())), preferred_element_type=jnp.float32) * loss_scale
    flat_shape = (frame_count, HEAD_COUNT * HEAD_SIZE)
    return (grad_r.reshape(flat_shape).astype(jnp.bfloat16), grad_k.reshape(flat_shape).astype(jnp.bfloat16), grad_v.reshape(flat_shape).astype(jnp.bfloat16), grad_weight)
```

```python
import functools
import math

import jax
import jax.numpy as jnp
from jax import lax
from jax.experimental import pallas as pl
from jax.experimental.pallas import tpu as pltpu
from jax.sharding import PartitionSpec as P

HEAD_COUNT = 16
HEAD_SIZE = 64
PAIR = 2 * HEAD_SIZE
PAIRS = HEAD_COUNT // 2
GROUP = 4
F32 = jnp.float32
BF16 = jnp.bfloat16

NN = (((1,), (0,)), ((), ()))
NT = (((1,), (1,)), ((), ()))
TN = (((0,), (0,)), ((), ()))


def split(x):
    high = x.astype(BF16)
    return high, (x - high.astype(F32)).astype(BF16)


def dot1(a, b, dims):
    return lax.dot_general(a, b, dims, preferred_element_type=F32)


def dot3(a, b, dims):
    a = (a,) if not isinstance(a, tuple) and a.dtype == BF16 else a if isinstance(a, tuple) else split(a)
    b = (b,) if not isinstance(b, tuple) and b.dtype == BF16 else b if isinstance(b, tuple) else split(b)
    out = dot1(a[0], b[0], dims)
    if len(b) > 1:
        out = out + dot1(a[0], b[1], dims)
    if len(a) > 1:
        out = out + dot1(a[1], b[0], dims)
    return out


def iota(shape, dim):
    return lax.broadcasted_iota(jnp.int32, shape, dim)


def both(f, lane_low):
    return jnp.where(lane_low, f(0), f(1))


def pack(full, lane_low):
    return jnp.where(lane_low, full[:HEAD_SIZE], full[HEAD_SIZE:])


def unpack(packed, diagonal):
    return jnp.where(diagonal, jnp.concatenate([packed, packed], 0), 0.0)


def product(a, b, dims):
    a = a if isinstance(a, tuple) else (a,) if a.dtype == BF16 else split(a)
    b = b if isinstance(b, tuple) else (b,) if b.dtype == BF16 else split(b)
    (ca,), (cb,) = dims[0]
    if len(a) == 1 and len(b) == 1:
        return dot1(a[0], b[0], dims)
    if len(b) == 1:
        return dot1(jnp.concatenate(a, ca), jnp.concatenate([b[0], b[0]], cb), dims)
    if len(a) == 1:
        return dot1(jnp.concatenate([a[0], a[0]], ca), jnp.concatenate(b, cb), dims)
    wide = b[0].shape[1 - cb]
    if wide <= PAIR:
        right = jnp.concatenate(b, 1 - cb)
        out = dot1(jnp.concatenate(a, ca), jnp.concatenate([right, right], cb), dims)
        return out[:, :wide] + out[:, wide:]
    out = dot1(jnp.concatenate(a, ca), jnp.concatenate([b[0], b[0]], cb), dims)
    return out + dot1(a[0], b[1], dims)


def inverses(lower, row, col):
    size = row.shape[0]
    eye = jnp.where(row == col, 1.0, 0.0).astype(F32)
    block = 8
    inside = row // block == col // block
    first = [jnp.where(inside, m, 0.0) for m in lower]
    halves = [split(m) for m in first]
    square = [split(product(m, m, NN)) for m in halves]
    left = [eye - m for m in first]
    tall = [tuple(jnp.concatenate(x, 0) for x in zip(split(m), s)) for m, s in zip(left, square)]
    tall = [product(m, s, NN) for m, s in zip(tall, square)]
    left = [m + t[:size] for m, t in zip(left, tall)]
    out = [m + product(m, t[size:], NN) for m, t in zip(left, tall)]
    while block < size:
        inside = (row // (4 * block) == col // (4 * block)) & (row // block != col // block)
        halves = [split(t) for t in out]
        near = [split(product(t, jnp.where(inside, m, 0.0), NN)) for t, m in zip(halves, lower)]
        both_of = [
            product(n, tuple(jnp.concatenate(x, 1) for x in zip(n, t)), NN) for n, t in zip(near, halves)
        ]
        out = [t - m[:, size:] for t, m in zip(out, both_of)]
        out = [t + product(m[:, :size], t, NN) for t, m in zip(out, both_of)]
        block *= 4
    return out


def one_less_exp(x):
    series = jnp.full_like(x, 1.0 / math.factorial(10))
    for n in range(9, 0, -1):
        series = series * x + 1.0 / math.factorial(n)
    return jnp.where(x > -0.5, -x * series, 1.0 - jnp.exp(x))


def row_scales(total):
    frames = total.shape[0]
    return total[frames // 2 - 1 : frames // 2], total[frames - 1 : frames]


def stream_kernel(count, parts, rec_ref, key_ref, val_ref, log_ref, kap_ref, rem_ref, start_ref, go_ref, w_hbm,
                  gr_out, gk_out, gv_out, mine_out,
                  w_ref, gath, gy_ref, tot_ref, ks_ref, a_ref, b_ref, k_ref, u_ref, x_ref, y_ref, yr_ref,
                  p_ref, tb_ref, gv_ref, gvk_ref, gra_ref, gka_ref, t_ref, ak_ref, rb_ref, rk_ref,
                  pay_out, pay_in, pull_out, pull_in, link_row, link_col, held, landed, ylow,
                  weight_sem, local_sem, send_sem, recv_sem):
    frames = rec_ref.shape[0]
    rows_each = HEAD_SIZE // parts
    half = rows_each // 2
    features = go_ref.shape[0]
    me = lax.axis_index("tm")
    row, col = iota((frames, frames), 0), iota((frames, frames), 1)
    lane_low = iota((frames, PAIR), 1) < HEAD_SIZE
    own = [lane_low, jnp.logical_not(lane_low)]
    low2 = jnp.concatenate([lane_low, lane_low], 1)
    own2 = [jnp.concatenate([m, m], 0) for m in own]
    pack_low = iota((HEAD_SIZE, PAIR), 1) < HEAD_SIZE
    half_low = iota((half, PAIR), 1) < HEAD_SIZE
    row_low = iota((rows_each, PAIR), 1) < HEAD_SIZE
    prow, pcol = iota((PAIR, PAIR), 0), iota((PAIR, PAIR), 1)
    ones = jnp.where((prow // HEAD_SIZE) == (pcol // HEAD_SIZE), 1.0, 0.0).astype(BF16)
    tri = jnp.where(row >= col, 1.0, 0.0).astype(BF16)
    strict, lax_tri = row > col, row >= col
    zero = jnp.zeros((), BF16)

    weight_copy = pltpu.make_async_copy(w_hbm, w_ref, weight_sem)
    weight_copy.start()

    barrier = pltpu.get_barrier_semaphore()

    def others(f):
        def step(i, carried):
            @pl.when(i != me)
            def _():
                f(i)

            return carried

        lax.fori_loop(0, count, step, 0)

    others(lambda i: pl.semaphore_signal(
        barrier, inc=1, device_id={"tm": i}, device_id_type=pl.DeviceIdType.MESH))
    pl.semaphore_wait(barrier, count - 1)

    def lanes(i):
        return pl.ds(pl.multiple_of(i * PAIR, PAIR), PAIR)

    def rows(i, n):
        return pl.ds(pl.multiple_of(i * n, n), n)

    sources = (
        lambda i: go_ref.at[:, pl.ds(pl.multiple_of(i * frames, frames), frames)],
        lambda i: pay_out.at[i],
        lambda i: pull_out.at[i],
        lambda i: held.at[i],
        lambda i: ylow.at[rows(i, features)],
    )
    places = (
        lambda i: gath.at[rows(i, features)],
        lambda i: pay_in.at[i],
        lambda i: pull_in.at[i],
        lambda i: landed.at[rows(i, rows_each)],
        lambda i: mine_out.at[i],
    )

    def remote(way, i, origin):
        return pltpu.make_async_remote_copy(
            src_ref=sources[way](i),
            dst_ref=places[way](origin),
            send_sem=send_sem.at[way, i],
            recv_sem=recv_sem.at[way, origin],
            device_id={"tm": i},
            device_id_type=pl.DeviceIdType.MESH,
        )

    def local(way):
        return pltpu.make_async_copy(sources[way](me), places[way](me), local_sem.at[way])

    def send(way, i):
        @pl.when(i != me)
        def _():
            remote(way, i, me).start()

        @pl.when(i == me)
        def _():
            local(way).start()

    def send_all(way, begin, end):
        def step(i, carried):
            send(way, i)
            return carried

        lax.fori_loop(begin, end, step, 0)

    def arrive(way):
        others(lambda i: remote(way, i, i).wait_recv())
        local(way).wait()

    send_all(0, 0, count)

    group = GROUP
    per_group = 2 * group * parts

    def first(g, carried):
        pairs = [g * group + n for n in range(group)]
        m_ab = []
        for pair in pairs:
            at = lanes(pair)
            log_low = log_ref[:, at]
            log_part = log_low.astype(F32)
            total = dot1(tri, log_low, NN)
            middle, last = row_scales(total)
            key_scale = jnp.sqrt(one_less_exp(log_part))
            raw = kap_ref[:, at].astype(F32)
            norm = product(raw * raw, ones, NN)
            a = raw / jnp.sqrt(norm + 1e-06)
            e_neg = jnp.exp(middle - total)
            a_mid = a * jnp.exp(total - log_part - middle)
            b_mid = rem_ref[:, at].astype(F32) * a * e_neg
            k_mid = key_ref[:, at].astype(F32) * key_scale * e_neg
            r_mid = rec_ref[:, at].astype(F32) * jnp.exp(total - middle)
            for ref, value in zip((tot_ref, ks_ref, a_ref, b_ref, k_ref), (total, key_scale, a_mid, b_mid, k_mid)):
                ref[pair] = value
            upper = split(jnp.concatenate([a_mid, r_mid], 0))
            rights = split(jnp.concatenate([b_mid, k_mid], 0))
            for h, m in enumerate(own2):
                gram = product(upper, tuple(jnp.where(m, x, zero) for x in rights), NT)
                m_ab.append(jnp.where(strict, gram[:frames, :frames], 0.0))
                kept = (
                    (ak_ref, jnp.where(strict, gram[:frames, frames:], 0.0)),
                    (rb_ref, jnp.where(lax_tri, gram[frames:, :frames], 0.0)),
                    (rk_ref, jnp.where(lax_tri, gram[frames:, frames:], 0.0)),
                )
                for ref, value in kept:
                    ref[0, pair * 2 + h], ref[1, pair * 2 + h] = split(value)
        inverted = inverses(m_ab, row, col)
        for n, pair in enumerate(pairs):
            at = lanes(pair)
            v = val_ref[:, at]
            total = tot_ref[pair]
            middle, last = row_scales(total)
            a_abs = a_ref[pair] * jnp.exp(middle)
            scale = jnp.exp(last - middle)
            t_inv = [split(inverted[n * 2 + h]) for h in range(2)]
            for h in range(2):
                t_ref[0, pair * 2 + h], t_ref[1, pair * 2 + h] = t_inv[h]
            on_v = both(lambda h: product((ak_ref[0, pair * 2 + h], ak_ref[1, pair * 2 + h]), v, NN), lane_low)
            given = split(jnp.concatenate([on_v, a_abs], 1))
            inner = both(lambda h: product(t_inv[h], given, NN), low2)
            u_ref[pair], x_ref[pair] = inner[:, :PAIR], inner[:, PAIR:]
            ended = product(inner, b_ref[pair] * scale, TN)
            through = pack(jnp.where(prow == pcol, jnp.exp(last), 0.0) - ended[PAIR:], pack_low)
            offset = pack(product(v, k_ref[pair] * scale, TN) - ended[:PAIR], pack_low)
            turned = pltpu.roll(through, HEAD_SIZE, 1)
            for part in range(parts):
                some = offset[part * rows_each : (part + 1) * rows_each]
                if parts > 1:
                    some = jnp.concatenate([some, jnp.zeros((HEAD_SIZE - rows_each, PAIR), F32)], 0)
                pay_out[pair * 2 * parts + part] = jnp.where(pack_low, through, pltpu.roll(some, HEAD_SIZE, 1))
                pay_out[(pair * 2 + 1) * parts + part] = jnp.where(pack_low, turned, some)
        send_all(1, g * per_group, (g + 1) * per_group)
        return carried

    lax.fori_loop(0, PAIRS // group, first, 0)

    arrive(0)
    weight_copy.wait()
    some_pairs = 2

    def project(n, carried):
        wide = some_pairs * PAIR
        weight = w_ref[rows(n, wide), :]
        out = dot1(gath[...], weight, (((0,), (1,)), ((), ())))
        for m in range(some_pairs):
            gy_ref[n * some_pairs + m] = out[:, m * PAIR : (m + 1) * PAIR]
        return carried

    lax.fori_loop(0, PAIRS // some_pairs, project, 0)

    def second(g, carried):
        for pair in [g * group + n for n in range(group)]:
            total = tot_ref[pair]
            middle, last = row_scales(total)
            scale = jnp.exp(last - middle)
            q = split(gy_ref[pair])
            r = rec_ref[:, lanes(pair)].astype(F32)
            back = both(lambda h: product((rb_ref[0, pair * 2 + h], rb_ref[1, pair * 2 + h]), q, TN), lane_low)
            given = split(jnp.concatenate([back, b_ref[pair] * scale], 1))
            pulled = both(lambda h: product((t_ref[0, pair * 2 + h], t_ref[1, pair * 2 + h]), given, TN), low2)
            p0 = pulled[:, :PAIR]
            p_ref[pair], tb_ref[pair] = p0, pulled[:, PAIR:]
            pull = product(q, r * jnp.exp(total), TN) - product(p0, a_ref[pair] * jnp.exp(middle), TN)
            pull = pack(pull, pack_low)
            for part in range(parts):
                top = pull[part * rows_each : part * rows_each + half]
                low = pull[part * rows_each + half : (part + 1) * rows_each]
                pull_out[pair * 2 * parts + part] = jnp.where(half_low, top, pltpu.roll(low, HEAD_SIZE, 1))
                pull_out[(pair * 2 + 1) * parts + part] = jnp.where(half_low, pltpu.roll(top, HEAD_SIZE, 1), low)
        send_all(2, g * per_group, (g + 1) * per_group)
        return carried

    lax.fori_loop(0, PAIRS // group, second, 0)

    def third(g, carried):
        for pair in [g * group + n for n in range(group)]:
            v = val_ref[:, lanes(pair)]
            total = tot_ref[pair]
            middle, last = row_scales(total)
            q = split(gy_ref[pair])
            inner = split(jnp.concatenate([u_ref[pair], x_ref[pair]], 1))
            minus = both(lambda h: product((rb_ref[0, pair * 2 + h], rb_ref[1, pair * 2 + h]), inner, NN), low2)
            m_rk = [(rk_ref[0, pair * 2 + h], rk_ref[1, pair * 2 + h]) for h in range(2)]
            y_ref[pair] = both(lambda h: product(m_rk[h], v, NN), lane_low) - minus[:, :PAIR]
            yr_ref[pair] = rec_ref[:, lanes(pair)].astype(F32) * jnp.exp(total) - minus[:, PAIR:]
            pulled = split(jnp.concatenate([p_ref[pair], tb_ref[pair]], 1))
            minus = both(lambda h: product((ak_ref[0, pair * 2 + h], ak_ref[1, pair * 2 + h]), pulled, TN), low2)
            gv_ref[pair] = both(lambda h: product(m_rk[h], q, TN), lane_low) - minus[:, :PAIR]
            gvk_ref[pair] = k_ref[pair] * jnp.exp(last - middle) - minus[:, PAIR:]
        return carried

    lax.fori_loop(0, PAIRS // group, third, 0)

    arrive(1)
    arrive(2)

    def ready(i, carried):
        got = pay_in[i]
        link = jnp.where(pack_low, got, pltpu.roll(got, HEAD_SIZE, 1))
        high, low = split(link)
        high, low = jnp.concatenate([high, high], 0), jnp.concatenate([low, low], 0)
        link_row[i] = jnp.concatenate([high, low], 0)
        link_col[i] = jnp.concatenate([high, low], 1)
        return carried

    lax.fori_loop(0, count, ready, 0)

    def carry_over(x):
        high, low = split(x)
        x = jnp.where(row_low, high, low)
        return jnp.concatenate([x, x], 1)

    def lap(i, carried):
        state, grad = carried
        j = count - 1 - i
        held[i, :, :HEAD_SIZE] = state[:, :HEAD_SIZE]
        held[j, :, HEAD_SIZE:] = grad[:, HEAD_SIZE:]
        got = pay_in[i, :rows_each]
        offset = jnp.where(row_low, pltpu.roll(got, HEAD_SIZE, 1), got)
        got = pull_in[j]
        turned = pltpu.roll(got, HEAD_SIZE, 1)
        pull = jnp.concatenate([jnp.where(half_low, got, turned), jnp.where(half_low, turned, got)], 0)
        state = offset + dot1(carry_over(state), link_row[i], NN)
        grad = pull + dot1(carry_over(grad), link_col[j], NT)
        return state, grad

    def lap_and_send(i, carried):
        carried = lap(i, carried)
        send(3, i)
        send(3, count - 1 - i)
        return carried

    carried = (start_ref[...], jnp.zeros((rows_each, PAIR), F32))
    carried = lax.fori_loop(0, count // 2, lap, carried)
    lax.fori_loop(count // 2, count, lap_and_send, carried)

    def fourth(g, carried):
        for pair in [g * group + n for n in range(group)]:
            v = val_ref[:, lanes(pair)]
            total = tot_ref[pair]
            middle, last = row_scales(total)
            e_pos, e_neg = jnp.exp(total - middle), jnp.exp(middle - total)
            q = split(gy_ref[pair])
            v_own = [jnp.where(m, v, zero) for m in own]
            q_own = [tuple(jnp.where(m, x, zero) for x in q) for m in own]
            k_mid, r_mid = split(k_ref[pair]), split(rec_ref[:, lanes(pair)].astype(F32) * e_pos)
            gra_ref[pair] = e_pos * both(
                lambda h: product(jnp.where(lax_tri, product(q, v_own[h], NT), 0.0), k_mid, NN), lane_low
            )
            gka_ref[pair] = ks_ref[pair] * e_neg * both(
                lambda h: product(jnp.where(row <= col, product(v, q_own[h], NT), 0.0), r_mid, NN), lane_low
            )
        return carried

    lax.fori_loop(0, PAIRS // group, fourth, 0)

    arrive(3)

    def landed_pair(pair):
        return (landed[rows(pair * 2, HEAD_SIZE)], landed[rows(pair * 2 + 1, HEAD_SIZE)])

    def state_of(pair):
        even, odd = landed_pair(pair)
        return jnp.concatenate(
            [jnp.where(pack_low, even, 0.0), jnp.where(pack_low, 0.0, pltpu.roll(odd, HEAD_SIZE, 1))], 0
        )

    def grad_of(pair):
        even, odd = landed_pair(pair)
        return jnp.concatenate(
            [jnp.where(pack_low, pltpu.roll(even, HEAD_SIZE, 1), 0.0), jnp.where(pack_low, 0.0, odd)], 0
        )

    def fifth(g, carried):
        for pair in [g * group + n for n in range(group)]:
            y = y_ref[pair] + product(yr_ref[pair], state_of(pair), NT)
            ylow[rows(pair, PAIR), :] = y.T.astype(BF16)
        return carried

    lax.fori_loop(0, PAIRS // group, fifth, 0)
    send_all(4, 0, count)

    def sixth(g, carried):
        for pair in [g * group + n for n in range(group)]:
            at = lanes(pair)
            state, grad = split(state_of(pair)), split(grad_of(pair))
            q, v = split(gy_ref[pair]), val_ref[:, at]
            u = split(u_ref[pair] + product(x_ref[pair], state, NT))
            behind = product(jnp.concatenate([tb_ref[pair], gvk_ref[pair]], 0), grad, NT)
            p = split(p_ref[pair] + behind[:frames])
            gv_out[:, at] = (gv_ref[pair] + behind[frames:]).astype(BF16)
            b_mid, a_mid = split(b_ref[pair]), split(a_ref[pair])
            total = tot_ref[pair]
            middle, last = row_scales(total)

            def removed(h):
                gram = product(q, tuple(jnp.where(own[h], x, zero) for x in u), NT)
                return product(jnp.where(lax_tri, gram, 0.0), b_mid, NN)

            def removed_back(h):
                gram = product(v, tuple(jnp.where(own[h], x, zero) for x in p), NT)
                return product(jnp.where(row < col, gram, 0.0), a_mid, NN)

            gr = jnp.exp(total) * product(q, state, NN) + gra_ref[pair]
            gr = gr - jnp.exp(total - middle) * both(removed, lane_low)
            gr_out[:, at] = gr.astype(BF16)
            gk = jnp.exp(last - total) * product(v, grad, NN) - jnp.exp(middle - total) * both(
                removed_back, lane_low
            )
            gk_out[:, at] = (gk * ks_ref[pair] + gka_ref[pair]).astype(BF16)
        return carried

    lax.fori_loop(0, PAIRS // group, sixth, 0)

    arrive(4)
    for way in range(5):
        others(lambda i: remote(way, i, me).wait_send())


def local(receptance, key_input, values, log_decay, kappa_raw, removal, initial_state, out_weight, grad_output):
    size = lax.axis_size("tm")
    frames, width = receptance.shape
    parts = size // HEAD_COUNT
    rows_each = HEAD_SIZE // parts
    features = grad_output.shape[0]
    everything = lax.all_gather(grad_output, "tm", axis=0, tiled=True)
    start = lax.dynamic_slice_in_dim(
        initial_state.reshape(HEAD_COUNT * HEAD_SIZE, HEAD_SIZE), lax.axis_index("tm") * rows_each, rows_each, 0
    )
    start = jnp.concatenate([start, start], 1)
    whole = pl.BlockSpec(memory_space=pltpu.VMEM)
    anywhere = pl.BlockSpec(memory_space=pl.ANY)
    low = jax.ShapeDtypeStruct((frames, width), BF16)
    flat = pltpu.VMEM((PAIRS, frames, PAIR), F32)
    matrix = pltpu.VMEM((2, HEAD_COUNT, frames, frames), BF16)
    grad_r, grad_k, grad_v, y_mine = pl.pallas_call(
        functools.partial(stream_kernel, size, parts),
        in_specs=[whole] * 8 + [anywhere],
        out_specs=[whole] * 4,
        out_shape=[low] * 3 + [jax.ShapeDtypeStruct((size, features, frames), BF16)],
        scratch_shapes=[
            pltpu.VMEM((width, width), BF16),
            pltpu.VMEM((width, frames), BF16),
        ]
        + [flat] * 16
        + [matrix] * 4
        + [
            pltpu.VMEM((size, HEAD_SIZE, PAIR), F32),
            pltpu.VMEM((size, HEAD_SIZE, PAIR), F32),
            pltpu.VMEM((size, rows_each // 2, PAIR), F32),
            pltpu.VMEM((size, rows_each // 2, PAIR), F32),
            pltpu.VMEM((size, 2 * PAIR, PAIR), BF16),
            pltpu.VMEM((size, PAIR, 2 * PAIR), BF16),
            pltpu.VMEM((size, rows_each, PAIR), F32),
            pltpu.VMEM((HEAD_COUNT * HEAD_SIZE, PAIR), F32),
            pltpu.VMEM((width, frames), BF16),
            pltpu.SemaphoreType.DMA,
            pltpu.SemaphoreType.DMA((5,)),
            pltpu.SemaphoreType.DMA((5, size)),
            pltpu.SemaphoreType.DMA((5, size)),
        ],
        compiler_params=pltpu.CompilerParams(
            collective_id=0, has_side_effects=True, vmem_limit_bytes=56 << 20
        ),
        name="stream",
    )(receptance, key_input, values, log_decay, kappa_raw, removal, start, grad_output, out_weight)
    loss_scale = 1.0 / math.sqrt(frames * size)
    y_mine = y_mine.swapaxes(0, 1).reshape(width // size, size * frames)
    grad_weight = (
        lax.dot_general(y_mine, everything, (((1,), (1,)), ((), ())), preferred_element_type=F32)
        * loss_scale
    )
    return grad_r, grad_k, grad_v, grad_weight


def solution(mesh):
    rows = P(("groups", "tm"), None)
    return jax.shard_map(
        local,
        mesh=mesh,
        in_specs=(rows,) * 6 + (P("groups", None, None), P(), P("tm", "groups")),
        out_specs=(rows,) * 4,
        check_vma=False,
    )
```

```python
import functools
import math

import jax
import jax.numpy as jnp
from jax import lax
from jax.experimental import pallas as pl
from jax.experimental.pallas import tpu as pltpu
from jax.sharding import PartitionSpec as P

HEAD_COUNT = 16
HEAD_SIZE = 64
PAIR = 2 * HEAD_SIZE
PAIRS = HEAD_COUNT // 2
GROUP = 4
F32 = jnp.float32
BF16 = jnp.bfloat16

NN = (((1,), (0,)), ((), ()))
NT = (((1,), (1,)), ((), ()))
TN = (((0,), (0,)), ((), ()))


def split(x):
    high = x.astype(BF16)
    return high, (x - high.astype(F32)).astype(BF16)


def dot1(a, b, dims):
    return lax.dot_general(a, b, dims, preferred_element_type=F32)


def dot3(a, b, dims):
    a = (a,) if not isinstance(a, tuple) and a.dtype == BF16 else a if isinstance(a, tuple) else split(a)
    b = (b,) if not isinstance(b, tuple) and b.dtype == BF16 else b if isinstance(b, tuple) else split(b)
    out = dot1(a[0], b[0], dims)
    if len(b) > 1:
        out = out + dot1(a[0], b[1], dims)
    if len(a) > 1:
        out = out + dot1(a[1], b[0], dims)
    return out


def iota(shape, dim):
    return lax.broadcasted_iota(jnp.int32, shape, dim)


def both(f, lane_low):
    return jnp.where(lane_low, f(0), f(1))


def pack(full, lane_low):
    return jnp.where(lane_low, full[:HEAD_SIZE], full[HEAD_SIZE:])


def unpack(packed, diagonal):
    return jnp.where(diagonal, jnp.concatenate([packed, packed], 0), 0.0)


def product(a, b, dims):
    a = a if isinstance(a, tuple) else (a,) if a.dtype == BF16 else split(a)
    b = b if isinstance(b, tuple) else (b,) if b.dtype == BF16 else split(b)
    (ca,), (cb,) = dims[0]
    if len(a) == 1 and len(b) == 1:
        return dot1(a[0], b[0], dims)
    if len(b) == 1:
        return dot1(jnp.concatenate(a, ca), jnp.concatenate([b[0], b[0]], cb), dims)
    if len(a) == 1:
        return dot1(jnp.concatenate([a[0], a[0]], ca), jnp.concatenate(b, cb), dims)
    wide = b[0].shape[1 - cb]
    if wide <= PAIR:
        right = jnp.concatenate(b, 1 - cb)
        out = dot1(jnp.concatenate(a, ca), jnp.concatenate([right, right], cb), dims)
        return out[:, :wide] + out[:, wide:]
    out = dot1(jnp.concatenate(a, ca), jnp.concatenate([b[0], b[0]], cb), dims)
    return out + dot1(a[0], b[1], dims)


def inverses(lower, row, col):
    size = row.shape[0]
    eye = jnp.where(row == col, 1.0, 0.0).astype(F32)
    block = 8
    inside = row // block == col // block
    first = [jnp.where(inside, m, 0.0) for m in lower]
    halves = [split(m) for m in first]
    square = [split(product(m, m, NN)) for m in halves]
    left = [eye - m for m in first]
    tall = [tuple(jnp.concatenate(x, 0) for x in zip(split(m), s)) for m, s in zip(left, square)]
    tall = [product(m, s, NN) for m, s in zip(tall, square)]
    left = [m + t[:size] for m, t in zip(left, tall)]
    out = [m + product(m, t[size:], NN) for m, t in zip(left, tall)]
    while block < size:
        inside = (row // (4 * block) == col // (4 * block)) & (row // block != col // block)
        halves = [split(t) for t in out]
        near = [split(product(t, jnp.where(inside, m, 0.0), NN)) for t, m in zip(halves, lower)]
        both_of = [
            product(n, tuple(jnp.concatenate(x, 1) for x in zip(n, t)), NN) for n, t in zip(near, halves)
        ]
        out = [t - m[:, size:] for t, m in zip(out, both_of)]
        out = [t + product(m[:, :size], t, NN) for t, m in zip(out, both_of)]
        block *= 4
    return out


def one_less_exp(x):
    series = jnp.full_like(x, 1.0 / math.factorial(10))
    for n in range(9, 0, -1):
        series = series * x + 1.0 / math.factorial(n)
    return jnp.where(x > -0.5, -x * series, 1.0 - jnp.exp(x))


def row_scales(total):
    frames = total.shape[0]
    return total[frames // 2 - 1 : frames // 2], total[frames - 1 : frames]


def stream_kernel(count, parts, rec_ref, key_ref, val_ref, log_ref, kap_ref, rem_ref, start_ref, go_ref, w_hbm,
                  gr_out, gk_out, gv_out, gw_out,
                  w_ref, gath, gy_ref, tot_ref, ks_ref, a_ref, b_ref, k_ref, u_ref, x_ref, y_ref, yr_ref,
                  p_ref, tb_ref, gv_ref, gvk_ref, gra_ref, gka_ref, t_ref, ak_ref, rb_ref, rk_ref,
                  pay_out, pay_in, pull_out, pull_in, link_row, link_col, held, landed, ylow, mine, half_go,
                  cross_out, cross_in, part_ref, part_out, part_in,
                  copy_sem, local_sem, send_sem, recv_sem, cross_send, cross_recv,
                  ring_send, ring_recv, twin_send, twin_recv):
    frames = rec_ref.shape[0]
    rows_each = HEAD_SIZE // parts
    features = go_ref.shape[0]
    near = count // 2
    wide = near * frames
    me = lax.axis_index("tm")
    side, here = me // near, lax.rem(me, near)
    partner = lax.rem(me + near, count)
    row, col = iota((frames, frames), 0), iota((frames, frames), 1)
    lane_low = iota((frames, PAIR), 1) < HEAD_SIZE
    own = [lane_low, jnp.logical_not(lane_low)]
    low2 = jnp.concatenate([lane_low, lane_low], 1)
    own2 = [jnp.concatenate([m, m], 0) for m in own]
    pack_low = iota((HEAD_SIZE, PAIR), 1) < HEAD_SIZE
    prow, pcol = iota((PAIR, PAIR), 0), iota((PAIR, PAIR), 1)
    diagonal = (prow // HEAD_SIZE) == (pcol // HEAD_SIZE)
    ones = jnp.where(diagonal, 1.0, 0.0).astype(BF16)
    tri = jnp.where(row >= col, 1.0, 0.0).astype(BF16)
    strict, lax_tri = row > col, row >= col
    zero = jnp.zeros((), BF16)

    weight_copy = pltpu.make_async_copy(w_hbm, w_ref, copy_sem.at[0])
    weight_copy.start()

    barrier = pltpu.get_barrier_semaphore()

    def greet(i):
        pl.semaphore_signal(barrier, inc=1, device_id={"tm": i}, device_id_type=pl.DeviceIdType.MESH)

    def others(f):
        def step(i, carried):
            @pl.when(i != here)
            def _():
                f(i)

            return carried

        lax.fori_loop(0, near, step, 0)

    others(lambda i: greet(side * near + i))
    greet(partner)
    pl.semaphore_wait(barrier, near)

    def lanes(i):
        return pl.ds(pl.multiple_of(i * PAIR, PAIR), PAIR)

    def rows(i, n):
        return pl.ds(pl.multiple_of(i * n, n), n)

    sources = (
        lambda i: go_ref.at[:, rows(side * near + i, frames)],
        lambda i: half_go.at[1 - side, here, :, rows(i, frames)],
        lambda i: pay_out.at[i],
        lambda i: pull_out.at[i],
        lambda i: held.at[i],
        lambda i: ylow.at[:, i],
    )
    places = (
        lambda i: gath.at[rows(side * near + i, features)],
        lambda i: gath.at[rows((1 - side) * near + i, features)],
        lambda i: pay_in.at[i],
        lambda i: pull_in.at[i],
        lambda i: landed.at[:, rows(i, rows_each)],
        lambda i: mine.at[:, :, rows(i, frames)],
    )
    ways = len(sources)

    def remote(way, i, origin):
        return pltpu.make_async_remote_copy(
            src_ref=sources[way](i),
            dst_ref=places[way](origin),
            send_sem=send_sem.at[way, i],
            recv_sem=recv_sem.at[way, origin],
            device_id={"tm": side * near + i},
            device_id_type=pl.DeviceIdType.MESH,
        )

    def local(way):
        return pltpu.make_async_copy(sources[way](here), places[way](here), local_sem.at[way])

    def send(way, i):
        @pl.when(i != here)
        def _():
            remote(way, i, here).start()

        @pl.when(i == here)
        def _():
            local(way).start()

    def send_all(way, begin, many):
        def step(i, carried):
            send(way, begin + lax.rem(here + many // 2 + i, many))
            return carried

        lax.fori_loop(0, many, step, 0)

    def arrive(way):
        others(lambda i: remote(way, i, i).wait_recv())
        local(way).wait()

    def cross(way):
        source, place = (
            (go_ref.at[:, rows(1 - side, wide)], half_go.at[side, here]),
            (cross_out, cross_in),
            (part_out, part_in),
        )[way]
        return pltpu.make_async_remote_copy(
            src_ref=source,
            dst_ref=place,
            send_sem=cross_send.at[way],
            recv_sem=cross_recv.at[way],
            device_id={"tm": partner},
            device_id_type=pl.DeviceIdType.MESH,
        )

    chips = near // 2
    hops = chips // 2
    core = lax.rem(here, 2)
    chip = here // 2
    spot = jnp.where(lax.rem(chip, 2) == 0, chip // 2, chips - 1 - chip // 2)

    def place_at(spot):
        spot = lax.rem(spot + 2 * chips, chips)
        return 2 * jnp.where(spot < hops, 2 * spot, 2 * (chips - 1 - spot) + 1) + core

    def ring(way, step, part):
        toward = 1 - 2 * way
        block = half_go.at[:, place_at(spot - toward * (step - 1))]
        if part:
            block = half_go.at[:, place_at(spot - toward * (step - 1)), :, pl.ds(way * (wide // 2), wide // 2)]
        return pltpu.make_async_remote_copy(
            src_ref=block,
            dst_ref=block,
            send_sem=ring_send.at[way, step - 1],
            recv_sem=ring_recv.at[way, step - 1],
            device_id={"tm": side * near + place_at(spot + toward)},
            device_id_type=pl.DeviceIdType.MESH,
        )

    def twin(way, step):
        block = half_go.at[:, place_at(spot - (1 - 2 * way) * step)]
        return pltpu.make_async_remote_copy(
            src_ref=block,
            dst_ref=block,
            send_sem=twin_send.at[way, step],
            recv_sem=twin_recv.at[way, step],
            device_id={"tm": me + 1 - 2 * core},
            device_id_type=pl.DeviceIdType.MESH,
        )

    def ring_begin():
        for way in range(2):
            ring(way, 1, hops == 1).start()
        twin(0, 0).start()

    def ring_steps():
        def body(step, carried):
            for way in range(2):
                ring(way, step, False).wait_recv()
            for way in range(2):
                ring(way, step + 1, False).start()
            for way in range(2):
                twin(way, step).start()
            return carried

        lax.fori_loop(1, hops - 1, body, 0)
        for way in range(2):
            ring(way, hops - 1, False).wait_recv()
        for way in range(2):
            ring(way, hops, True).start()
        for way in range(2):
            twin(way, hops - 1).start()

    def ring_end():
        for way in range(2):
            ring(way, hops, True).wait_recv()
        twin(0, hops).start()

    def ring_done():
        def body(step, carried):
            for way in range(2):
                ring(way, step, False).wait_send()
                twin(way, step).wait()
            return carried

        lax.fori_loop(1, hops, body, 0)
        for way in range(2):
            ring(way, hops, True).wait_send()
        twin(0, 0).wait()
        twin(0, hops).wait()

    cross(0).start()
    send_all(0, 0, near)
    own_half = pltpu.make_async_copy(go_ref.at[:, rows(side, wide)], half_go.at[side, here], copy_sem.at[1])
    own_half.start()
    own_half.wait()

    group = GROUP
    groups = PAIRS // group
    per_group = group * parts

    def far_first(n):
        return lax.rem(n + 1 + here * groups // near, groups)

    def first(n, carried):
        g = far_first(n)
        pairs = [g * group + m for m in range(group)]
        m_ab = []
        for pair in pairs:
            at = lanes(pair)
            log_low = log_ref[:, at]
            log_part = log_low.astype(F32)
            total = dot1(tri, log_low, NN)
            middle, last = row_scales(total)
            key_scale = jnp.sqrt(one_less_exp(log_part))
            raw = kap_ref[:, at].astype(F32)
            norm = product(raw * raw, ones, NN)
            a = raw / jnp.sqrt(norm + 1e-06)
            e_neg = jnp.exp(middle - total)
            a_mid = a * jnp.exp(total - log_part - middle)
            b_mid = rem_ref[:, at].astype(F32) * a * e_neg
            k_mid = key_ref[:, at].astype(F32) * key_scale * e_neg
            r_mid = rec_ref[:, at].astype(F32) * jnp.exp(total - middle)
            for ref, value in zip((tot_ref, ks_ref, a_ref, b_ref, k_ref), (total, key_scale, a_mid, b_mid, k_mid)):
                ref[pair] = value
            upper = split(jnp.concatenate([a_mid, r_mid], 0))
            rights = split(jnp.concatenate([b_mid, k_mid], 0))
            for h, m in enumerate(own2):
                gram = product(upper, tuple(jnp.where(m, x, zero) for x in rights), NT)
                m_ab.append(jnp.where(strict, gram[:frames, :frames], 0.0))
                kept = (
                    (ak_ref, jnp.where(strict, gram[:frames, frames:], 0.0)),
                    (rb_ref, jnp.where(lax_tri, gram[frames:, :frames], 0.0)),
                    (rk_ref, jnp.where(lax_tri, gram[frames:, frames:], 0.0)),
                )
                for ref, value in kept:
                    ref[0, pair * 2 + h], ref[1, pair * 2 + h] = split(value)
        inverted = inverses(m_ab, row, col)
        for m, pair in enumerate(pairs):
            at = lanes(pair)
            v = val_ref[:, at]
            total = tot_ref[pair]
            middle, last = row_scales(total)
            a_abs = a_ref[pair] * jnp.exp(middle)
            scale = jnp.exp(last - middle)
            t_inv = [split(inverted[m * 2 + h]) for h in range(2)]
            for h in range(2):
                t_ref[0, pair * 2 + h], t_ref[1, pair * 2 + h] = t_inv[h]
            on_v = both(lambda h: product((ak_ref[0, pair * 2 + h], ak_ref[1, pair * 2 + h]), v, NN), lane_low)
            given = split(jnp.concatenate([on_v, a_abs], 1))
            inner = both(lambda h: product(t_inv[h], given, NN), low2)
            u_ref[pair], x_ref[pair] = inner[:, :PAIR], inner[:, PAIR:]
            ended = product(inner, b_ref[pair] * scale, TN)
            through = pack(jnp.where(prow == pcol, jnp.exp(last), 0.0) - ended[PAIR:], pack_low)
            offset = pack(product(v, k_ref[pair] * scale, TN) - ended[:PAIR], pack_low)
            for part in range(parts):
                pay_out[pair * parts + part, :HEAD_SIZE] = through
                pay_out[pair * parts + part, HEAD_SIZE:] = offset[part * rows_each : (part + 1) * rows_each]
        send_all(2, g * per_group, per_group)

        @pl.when(n == 0)
        def _():
            cross(0).wait_recv()
            send_all(1, 0, near)

        return carried

    lax.fori_loop(0, PAIRS // group, first, 0)
    ring_begin()

    arrive(0)
    arrive(1)
    weight_copy.wait()
    some_pairs = 2

    def project(n, carried):
        wide = some_pairs * PAIR
        weight = w_ref[rows(n, wide), :]
        out = dot1(gath[...], weight, (((0,), (1,)), ((), ())))
        for m in range(some_pairs):
            gy_ref[n * some_pairs + m] = out[:, m * PAIR : (m + 1) * PAIR]
        return carried

    lax.fori_loop(0, PAIRS // some_pairs, project, 0)

    def second(n, carried):
        g = far_first(n)
        for pair in [g * group + m for m in range(group)]:
            total = tot_ref[pair]
            middle, last = row_scales(total)
            scale = jnp.exp(last - middle)
            q = split(gy_ref[pair])
            r = rec_ref[:, lanes(pair)].astype(F32)
            back = both(lambda h: product((rb_ref[0, pair * 2 + h], rb_ref[1, pair * 2 + h]), q, TN), lane_low)
            given = split(jnp.concatenate([back, b_ref[pair] * scale], 1))
            pulled = both(lambda h: product((t_ref[0, pair * 2 + h], t_ref[1, pair * 2 + h]), given, TN), low2)
            p0 = pulled[:, :PAIR]
            p_ref[pair], tb_ref[pair] = p0, pulled[:, PAIR:]
            pull = product(q, r * jnp.exp(total), TN) - product(p0, a_ref[pair] * jnp.exp(middle), TN)
            pull = pack(pull, pack_low)
            for part in range(parts):
                pull_out[pair * parts + part] = pull[part * rows_each : (part + 1) * rows_each]
        send_all(3, g * per_group, per_group)
        return carried

    lax.fori_loop(0, PAIRS // group, second, 0)

    def third(g, carried):
        for pair in [g * group + n for n in range(group)]:
            v = val_ref[:, lanes(pair)]
            total = tot_ref[pair]
            middle, last = row_scales(total)
            q = split(gy_ref[pair])
            inner = split(jnp.concatenate([u_ref[pair], x_ref[pair]], 1))
            minus = both(lambda h: product((rb_ref[0, pair * 2 + h], rb_ref[1, pair * 2 + h]), inner, NN), low2)
            m_rk = [(rk_ref[0, pair * 2 + h], rk_ref[1, pair * 2 + h]) for h in range(2)]
            y_ref[pair] = both(lambda h: product(m_rk[h], v, NN), lane_low) - minus[:, :PAIR]
            yr_ref[pair] = rec_ref[:, lanes(pair)].astype(F32) * jnp.exp(total) - minus[:, PAIR:]
            pulled = split(jnp.concatenate([p_ref[pair], tb_ref[pair]], 1))
            minus = both(lambda h: product((ak_ref[0, pair * 2 + h], ak_ref[1, pair * 2 + h]), pulled, TN), low2)
            gv_ref[pair] = both(lambda h: product(m_rk[h], q, TN), lane_low) - minus[:, :PAIR]
            gvk_ref[pair] = k_ref[pair] * jnp.exp(last - middle) - minus[:, PAIR:]
        return carried

    lax.fori_loop(0, PAIRS // group, third, 0)
    ring_steps()

    arrive(2)
    arrive(3)

    def ready(i, carried):
        link = split(unpack(pay_in[i, :HEAD_SIZE], diagonal))
        down, across = jnp.concatenate(link, 0), jnp.concatenate(link, 1)
        link_row[i] = jnp.concatenate([across, across], 0)
        link_col[i] = jnp.concatenate([down, down], 1)
        return carried

    lax.fori_loop(0, near, ready, 0)

    def carry_over(x, link, dims):
        out = dot1(jnp.concatenate(split(x), 1), link, dims)
        return out[:, :PAIR] + out[:, PAIR:]

    def ahead(i, state):
        held[i, 0] = state
        return pay_in[i, HEAD_SIZE:] + carry_over(state, link_row[i], NN)

    def astern(i, grad):
        j = near - 1 - i
        held[j, 1] = grad
        return pull_in[j] + carry_over(grad, link_col[j], NT)

    @pl.when(side == 0)
    def _():
        cross_out[...] = lax.fori_loop(0, near, ahead, start_ref[...], unroll=near <= 8)

    @pl.when(side == 1)
    def _():
        cross_out[...] = lax.fori_loop(0, near, astern, jnp.zeros((rows_each, PAIR), F32), unroll=near <= 8)

    cross(1).start()

    def fourth(g, carried):
        for pair in [g * group + n for n in range(group)]:
            v = val_ref[:, lanes(pair)]
            total = tot_ref[pair]
            middle, last = row_scales(total)
            e_pos, e_neg = jnp.exp(total - middle), jnp.exp(middle - total)
            q = split(gy_ref[pair])
            v_own = [jnp.where(m, v, zero) for m in own]
            q_own = [tuple(jnp.where(m, x, zero) for x in q) for m in own]
            k_mid, r_mid = split(k_ref[pair]), split(rec_ref[:, lanes(pair)].astype(F32) * e_pos)
            gra_ref[pair] = e_pos * both(
                lambda h: product(jnp.where(lax_tri, product(q, v_own[h], NT), 0.0), k_mid, NN), lane_low
            )
            gka_ref[pair] = ks_ref[pair] * e_neg * both(
                lambda h: product(jnp.where(row <= col, product(v, q_own[h], NT), 0.0), r_mid, NN), lane_low
            )
        return carried

    lax.fori_loop(0, groups // 2, fourth, 0)
    cross(1).wait_recv()

    @pl.when(side == 0)
    def _():
        lax.fori_loop(0, near, astern, cross_in[...], unroll=near <= 8)

    @pl.when(side == 1)
    def _():
        lax.fori_loop(0, near, ahead, cross_in[...], unroll=near <= 8)

    send_all(4, 0, near)
    lax.fori_loop(groups // 2, groups, fourth, 0)
    ring_end()

    arrive(4)

    def state_of(pair):
        return unpack(landed[0, rows(pair, HEAD_SIZE)], diagonal)

    def grad_of(pair):
        return unpack(landed[1, rows(pair, HEAD_SIZE)], diagonal)

    def fifth(g, carried):
        for pair in [g * group + n for n in range(group)]:
            y = y_ref[pair] + product(yr_ref[pair], state_of(pair), NT)
            y = y.T.astype(BF16)
            for m in range(PAIR // features):
                block = pair * (PAIR // features) + m
                ylow[block // near, lax.rem(block, near)] = y[m * features : (m + 1) * features]
        return carried

    lax.fori_loop(0, PAIRS // group, fifth, 0)
    send_all(5, 0, near)

    def sixth(g, carried):
        for pair in [g * group + n for n in range(group)]:
            at = lanes(pair)
            state, grad = split(state_of(pair)), split(grad_of(pair))
            q, v = split(gy_ref[pair]), val_ref[:, at]
            u = split(u_ref[pair] + product(x_ref[pair], state, NT))
            behind = product(jnp.concatenate([tb_ref[pair], gvk_ref[pair]], 0), grad, NT)
            p = split(p_ref[pair] + behind[:frames])
            gv_out[:, at] = (gv_ref[pair] + behind[frames:]).astype(BF16)
            b_mid, a_mid = split(b_ref[pair]), split(a_ref[pair])
            total = tot_ref[pair]
            middle, last = row_scales(total)

            def removed(h):
                gram = product(q, tuple(jnp.where(own[h], x, zero) for x in u), NT)
                return product(jnp.where(lax_tri, gram, 0.0), b_mid, NN)

            def removed_back(h):
                gram = product(v, tuple(jnp.where(own[h], x, zero) for x in p), NT)
                return product(jnp.where(row < col, gram, 0.0), a_mid, NN)

            gr = jnp.exp(total) * product(q, state, NN) + gra_ref[pair]
            gr = gr - jnp.exp(total - middle) * both(removed, lane_low)
            gr_out[:, at] = gr.astype(BF16)
            gk = jnp.exp(last - total) * product(v, grad, NN) - jnp.exp(middle - total) * both(
                removed_back, lane_low
            )
            gk_out[:, at] = (gk * ks_ref[pair] + gka_ref[pair]).astype(BF16)
        return carried

    lax.fori_loop(0, groups // 2, sixth, 0)
    ring_done()
    arrive(5)
    per = 2 * PAIR // features
    loss_scale = 1.0 / math.sqrt(frames * count)

    def weigh(n, carried):
        blocks = half_go[n * per // near, pl.ds(lax.rem(n * per, near), per)].reshape(per * features, wide)
        out = dot1(mine[...].reshape(2 * features, wide), blocks, NT) * loss_scale
        part_ref[0, :, rows(n, 2 * PAIR)] = out[:features]
        part_ref[1, :, rows(n, 2 * PAIR)] = out[features:]
        return carried

    lax.fori_loop(0, count // per, weigh, 0)
    part_out[...] = part_ref[1 - side].astype(BF16)
    cross(2).start()
    lax.fori_loop(groups // 2, groups, sixth, 0)
    cross(2).wait_recv()
    gw_out[...] = part_ref[side] + part_in[...].astype(F32)
    for way in range(ways):
        others(lambda i: remote(way, i, here).wait_send())
    for way in range(3):
        cross(way).wait_send()


def local(receptance, key_input, values, log_decay, kappa_raw, removal, initial_state, out_weight, grad_output):
    size = lax.axis_size("tm")
    frames, width = receptance.shape
    near = size // 2
    parts = near // PAIRS
    rows_each = HEAD_SIZE // parts
    features = grad_output.shape[0]
    here = lax.rem(lax.axis_index("tm"), near)
    start = lax.dynamic_slice_in_dim(
        initial_state.reshape(PAIRS, 2, parts, rows_each, HEAD_SIZE).swapaxes(1, 2).reshape(near, 2, rows_each, HEAD_SIZE),
        here, 1, 0,
    )
    start = jnp.concatenate([start[0, 0], start[0, 1]], 1)
    whole = pl.BlockSpec(memory_space=pltpu.VMEM)
    anywhere = pl.BlockSpec(memory_space=pl.ANY)
    low = jax.ShapeDtypeStruct((frames, width), BF16)
    flat = pltpu.VMEM((PAIRS, frames, PAIR), F32)
    matrix = pltpu.VMEM((2, HEAD_COUNT, frames, frames), BF16)
    return tuple(pl.pallas_call(
        functools.partial(stream_kernel, size, parts),
        in_specs=[whole] * 8 + [anywhere],
        out_specs=[whole] * 4,
        out_shape=[low] * 3 + [jax.ShapeDtypeStruct((features, width), F32)],
        scratch_shapes=[
            pltpu.VMEM((width, width), BF16),
            pltpu.VMEM((width, frames), BF16),
        ]
        + [flat] * 16
        + [matrix] * 4
        + [
            pltpu.VMEM((near, HEAD_SIZE + rows_each, PAIR), F32),
            pltpu.VMEM((near, HEAD_SIZE + rows_each, PAIR), F32),
            pltpu.VMEM((near, rows_each, PAIR), F32),
            pltpu.VMEM((near, rows_each, PAIR), F32),
            pltpu.VMEM((near, 2 * PAIR, 2 * PAIR), BF16),
            pltpu.VMEM((near, 2 * PAIR, 2 * PAIR), BF16),
            pltpu.VMEM((near, 2, rows_each, PAIR), F32),
            pltpu.VMEM((2, PAIRS * HEAD_SIZE, PAIR), F32),
            pltpu.VMEM((2, near, features, frames), BF16),
            pltpu.VMEM((2, features, near * frames), BF16),
            pltpu.VMEM((2, near, features, near * frames), BF16),
            pltpu.VMEM((rows_each, PAIR), F32),
            pltpu.VMEM((rows_each, PAIR), F32),
            pltpu.VMEM((2, features, width), F32),
            pltpu.VMEM((features, width), BF16),
            pltpu.VMEM((features, width), BF16),
            pltpu.SemaphoreType.DMA((2,)),
            pltpu.SemaphoreType.DMA((6,)),
            pltpu.SemaphoreType.DMA((6, near)),
            pltpu.SemaphoreType.DMA((6, near)),
            pltpu.SemaphoreType.DMA((3,)),
            pltpu.SemaphoreType.DMA((3,)),
            pltpu.SemaphoreType.DMA((2, near // 4)),
            pltpu.SemaphoreType.DMA((2, near // 4)),
            pltpu.SemaphoreType.DMA((2, near // 4 + 1)),
            pltpu.SemaphoreType.DMA((2, near // 4 + 1)),
        ],
        compiler_params=pltpu.CompilerParams(
            collective_id=0, has_side_effects=True, vmem_limit_bytes=56 << 20
        ),
        name="stream",
    )(receptance, key_input, values, log_decay, kappa_raw, removal, start, grad_output, out_weight))


def solution(mesh):
    rows = P(("groups", "tm"), None)
    return jax.shard_map(
        local,
        mesh=mesh,
        in_specs=(rows,) * 6 + (P("groups", None, None), P(), P("tm", "groups")),
        out_specs=(rows,) * 4,
        check_vma=False,
    )
```

```python
import functools
import math

import jax
import jax.numpy as jnp
from jax import lax
from jax.experimental import pallas as pl
from jax.experimental.pallas import tpu as pltpu
from jax.sharding import PartitionSpec as P

HEAD_COUNT = 16
HEAD_SIZE = 64
PAIR = 2 * HEAD_SIZE
PAIRS = HEAD_COUNT // 2
GROUP = 4
F32 = jnp.float32
BF16 = jnp.bfloat16

NN = (((1,), (0,)), ((), ()))
NT = (((1,), (1,)), ((), ()))
TN = (((0,), (0,)), ((), ()))


def split(x):
    high = x.astype(BF16)
    return high, (x - high.astype(F32)).astype(BF16)


def dot1(a, b, dims):
    return lax.dot_general(a, b, dims, preferred_element_type=F32)


def dot3(a, b, dims):
    a = (a,) if not isinstance(a, tuple) and a.dtype == BF16 else a if isinstance(a, tuple) else split(a)
    b = (b,) if not isinstance(b, tuple) and b.dtype == BF16 else b if isinstance(b, tuple) else split(b)
    out = dot1(a[0], b[0], dims)
    if len(b) > 1:
        out = out + dot1(a[0], b[1], dims)
    if len(a) > 1:
        out = out + dot1(a[1], b[0], dims)
    return out


def iota(shape, dim):
    return lax.broadcasted_iota(jnp.int32, shape, dim)


def both(f, lane_low):
    return jnp.where(lane_low, f(0), f(1))


def pack(full, lane_low):
    return jnp.where(lane_low, full[:HEAD_SIZE], full[HEAD_SIZE:])


def unpack(packed, diagonal):
    return jnp.where(diagonal, jnp.concatenate([packed, packed], 0), 0.0)


def product(a, b, dims):
    a = a if isinstance(a, tuple) else (a,) if a.dtype == BF16 else split(a)
    b = b if isinstance(b, tuple) else (b,) if b.dtype == BF16 else split(b)
    (ca,), (cb,) = dims[0]
    if len(a) == 1 and len(b) == 1:
        return dot1(a[0], b[0], dims)
    if len(b) == 1:
        return dot1(jnp.concatenate(a, ca), jnp.concatenate([b[0], b[0]], cb), dims)
    if len(a) == 1:
        return dot1(jnp.concatenate([a[0], a[0]], ca), jnp.concatenate(b, cb), dims)
    wide = b[0].shape[1 - cb]
    if wide <= PAIR:
        right = jnp.concatenate(b, 1 - cb)
        out = dot1(jnp.concatenate(a, ca), jnp.concatenate([right, right], cb), dims)
        return out[:, :wide] + out[:, wide:]
    out = dot1(jnp.concatenate(a, ca), jnp.concatenate([b[0], b[0]], cb), dims)
    return out + dot1(a[0], b[1], dims)


def inverses(lower, row, col):
    size = row.shape[0]
    eye = jnp.where(row == col, 1.0, 0.0).astype(F32)
    block = 8
    inside = row // block == col // block
    first = [jnp.where(inside, m, 0.0) for m in lower]
    halves = [split(m) for m in first]
    square = [split(product(m, m, NN)) for m in halves]
    left = [eye - m for m in first]
    tall = [tuple(jnp.concatenate(x, 0) for x in zip(split(m), s)) for m, s in zip(left, square)]
    tall = [product(m, s, NN) for m, s in zip(tall, square)]
    left = [m + t[:size] for m, t in zip(left, tall)]
    out = [m + product(m, t[size:], NN) for m, t in zip(left, tall)]
    while block < size:
        inside = (row // (4 * block) == col // (4 * block)) & (row // block != col // block)
        halves = [split(t) for t in out]
        near = [split(product(t, jnp.where(inside, m, 0.0), NN)) for t, m in zip(halves, lower)]
        both_of = [
            product(n, tuple(jnp.concatenate(x, 1) for x in zip(n, t)), NN) for n, t in zip(near, halves)
        ]
        out = [t - m[:, size:] for t, m in zip(out, both_of)]
        out = [t + product(m[:, :size], t, NN) for t, m in zip(out, both_of)]
        block *= 4
    return out


def one_less_exp(x):
    series = jnp.full_like(x, 1.0 / math.factorial(10))
    for n in range(9, 0, -1):
        series = series * x + 1.0 / math.factorial(n)
    return jnp.where(x > -0.5, -x * series, 1.0 - jnp.exp(x))


def row_scales(total):
    frames = total.shape[0]
    return total[frames // 2 - 1 : frames // 2], total[frames - 1 : frames]


def stream_kernel(count, parts, rec_hbm, key_hbm, val_hbm, log_hbm, kap_hbm, rem_hbm, start_hbm, go_hbm, w_hbm,
                  all_out, gw_out,
                  rec_ref, key_ref, val_ref, log_ref, kap_ref, rem_ref, start_ref, go_ref, w_ref, gath, gy_ref, tot_ref, ks_ref, a_ref, b_ref, k_ref, u_ref, x_ref, y_ref, yr_ref,
                  p_ref, tb_ref, gv_ref, gvk_ref, gra_ref, gka_ref, t_ref, ak_ref, rb_ref, rk_ref,
                  pay_out, pay_in, pull_out, pull_in, link_row, link_col, held, landed, ylow, mine, half_go,
                  cross_out, cross_in, part_ref, part_out, part_in,
                  copy_sem, local_sem, send_sem, recv_sem, cross_send, cross_recv,
                  ring_send, ring_recv, twin_send, twin_recv):
    frames = rec_hbm.shape[0]
    rows_each = HEAD_SIZE // parts
    features = go_hbm.shape[0]
    near = count // 2
    wide = near * frames
    me = lax.axis_index("tm")
    side, here = me // near, lax.rem(me, near)
    partner = lax.rem(me + near, count)
    row, col = iota((frames, frames), 0), iota((frames, frames), 1)
    lane_low = iota((frames, PAIR), 1) < HEAD_SIZE
    own = [lane_low, jnp.logical_not(lane_low)]
    low2 = jnp.concatenate([lane_low, lane_low], 1)
    own2 = [jnp.concatenate([m, m], 0) for m in own]
    pack_low = iota((HEAD_SIZE, PAIR), 1) < HEAD_SIZE
    prow, pcol = iota((PAIR, PAIR), 0), iota((PAIR, PAIR), 1)
    diagonal = (prow // HEAD_SIZE) == (pcol // HEAD_SIZE)
    ones = jnp.where(diagonal, 1.0, 0.0).astype(BF16)
    tri = jnp.where(row >= col, 1.0, 0.0).astype(BF16)
    strict, lax_tri = row > col, row >= col
    zero = jnp.zeros((), BF16)

    begin = pl.ds(pl.multiple_of(lax.rem(here, parts) * rows_each, rows_each), rows_each)
    moves = [(go_hbm, go_ref)]
    moves += zip((log_hbm, kap_hbm, rem_hbm, key_hbm, rec_hbm, val_hbm), (log_ref, kap_ref, rem_ref, key_ref, rec_ref, val_ref))
    moves += [(start_hbm.at[here // parts * 2 + h, begin], start_ref.at[h]) for h in range(2)]
    moves += [(w_hbm, w_ref)]
    loads = [pltpu.make_async_copy(a, b, copy_sem.at[1 + n]) for n, (a, b) in enumerate(moves)]
    for load in loads:
        load.start()

    barrier = pltpu.get_barrier_semaphore()

    def greet(i):
        pl.semaphore_signal(barrier, inc=1, device_id={"tm": i}, device_id_type=pl.DeviceIdType.MESH)

    def others(f):
        def step(i, carried):
            @pl.when(i != here)
            def _():
                f(i)

            return carried

        lax.fori_loop(0, near, step, 0)

    others(lambda i: greet(side * near + i))
    greet(partner)
    pl.semaphore_wait(barrier, near)

    def lanes(i):
        return pl.ds(pl.multiple_of(i * PAIR, PAIR), PAIR)

    def rows(i, n):
        return pl.ds(pl.multiple_of(i * n, n), n)

    sources = (
        lambda i: go_ref.at[:, rows(side * near + i, frames)],
        lambda i: half_go.at[1 - side, here, :, rows(i, frames)],
        lambda i: pay_out.at[i],
        lambda i: pull_out.at[i],
        lambda i: held.at[0, i],
        lambda i: held.at[1, i],
        lambda i: ylow.at[0, i],
        lambda i: ylow.at[1, i],
    )
    places = (
        lambda i: gath.at[rows(side * near + i, features)],
        lambda i: gath.at[rows((1 - side) * near + i, features)],
        lambda i: pay_in.at[i],
        lambda i: pull_in.at[i],
        lambda i: landed.at[0, rows(i, rows_each)],
        lambda i: landed.at[1, rows(i, rows_each)],
        lambda i: mine.at[0, :, rows(i, frames)],
        lambda i: mine.at[1, :, rows(i, frames)],
    )
    ways = len(sources)

    def remote(way, i, origin):
        return pltpu.make_async_remote_copy(
            src_ref=sources[way](i),
            dst_ref=places[way](origin),
            send_sem=send_sem.at[way, i],
            recv_sem=recv_sem.at[way, origin],
            device_id={"tm": side * near + i},
            device_id_type=pl.DeviceIdType.MESH,
        )

    def local(way):
        return pltpu.make_async_copy(sources[way](here), places[way](here), local_sem.at[way])

    def send(way, i):
        @pl.when(i != here)
        def _():
            remote(way, i, here).start()

        @pl.when(i == here)
        def _():
            local(way).start()

    def send_all(way, begin, many):
        def step(i, carried):
            send(way, begin + lax.rem(here + many // 2 + i, many))
            return carried

        lax.fori_loop(0, many, step, 0)

    def arrive(way):
        others(lambda i: remote(way, i, i).wait_recv())
        local(way).wait()

    def across(source, place, n):
        return pltpu.make_async_remote_copy(
            src_ref=source,
            dst_ref=place,
            send_sem=cross_send.at[n],
            recv_sem=cross_recv.at[n],
            device_id={"tm": partner},
            device_id_type=pl.DeviceIdType.MESH,
        )

    cross_frames = across(go_ref.at[:, rows(1 - side, wide)], half_go.at[side, here], 0)
    cross_state = across(cross_out, cross_in, 1)
    chunks = part_out.shape[0]

    def cross_part(n):
        return across(part_out.at[n], part_in.at[n], 2 + n)

    chips = near // 2
    hops = chips // 2
    core = lax.rem(here, 2)
    chip = here // 2
    spot = jnp.where(lax.rem(chip, 2) == 0, chip // 2, chips - 1 - chip // 2)

    def place_at(spot):
        spot = lax.rem(spot + 2 * chips, chips)
        return 2 * jnp.where(spot < hops, 2 * spot, 2 * (chips - 1 - spot) + 1) + core

    def ring(of, way, step, part):
        toward = 1 - 2 * way
        block = half_go.at[lax.rem(side + of, 2), place_at(spot - toward * (step - 1))]
        if part:
            block = block.at[:, pl.ds(way * (wide // 2), wide // 2)]
        return pltpu.make_async_remote_copy(
            src_ref=block,
            dst_ref=block,
            send_sem=ring_send.at[of, way, step - 1],
            recv_sem=ring_recv.at[of, way, step - 1],
            device_id={"tm": side * near + place_at(spot + toward)},
            device_id_type=pl.DeviceIdType.MESH,
        )

    def twin(of, way, step):
        block = half_go.at[lax.rem(side + of, 2), place_at(spot - (1 - 2 * way) * step)]
        return pltpu.make_async_remote_copy(
            src_ref=block,
            dst_ref=block,
            send_sem=twin_send.at[of, way, step],
            recv_sem=twin_recv.at[of, way, step],
            device_id={"tm": me + 1 - 2 * core},
            device_id_type=pl.DeviceIdType.MESH,
        )

    def ring_begin(of):
        for way in range(2):
            ring(of, way, 1, False).start()
        twin(of, 0, 0).start()

    def ring_steps(of):
        def body(step, carried):
            for way in range(2):
                ring(of, way, step, False).wait_recv()
            for way in range(2):
                ring(of, way, step + 1, False).start()
            for way in range(2):
                twin(of, way, step).start()
            return carried

        lax.fori_loop(1, hops - 1, body, 0)
        for way in range(2):
            ring(of, way, hops - 1, False).wait_recv()
        for way in range(2):
            ring(of, way, hops, True).start()
        for way in range(2):
            twin(of, way, hops - 1).start()

    def ring_end(of):
        for way in range(2):
            ring(of, way, hops, True).wait_recv()
        twin(of, 0, hops).start()

    def ring_done(of):
        def body(step, carried):
            for way in range(2):
                ring(of, way, step, False).wait_send()
                twin(of, way, step).wait()
            return carried

        lax.fori_loop(1, hops, body, 0)
        for way in range(2):
            ring(of, way, hops, True).wait_send()
        twin(of, 0, 0).wait()
        twin(of, 0, hops).wait()

    loads[0].wait()
    cross_frames.start()
    send_all(0, 0, near)
    own_half = pltpu.make_async_copy(go_ref.at[:, rows(side, wide)], half_go.at[side, here], copy_sem.at[0])
    own_half.start()
    own_half.wait()
    ring_begin(0)

    group = GROUP
    groups = PAIRS // group
    per_group = group * parts

    def far_first(n):
        return lax.rem(n + 1 + here * groups // near, groups)

    def first(n, carried):
        g = far_first(n)
        pairs = [g * group + m for m in range(group)]
        m_ab = []
        for pair in pairs:
            at = lanes(pair)
            log_low = log_ref[:, at]
            log_part = log_low.astype(F32)
            total = dot1(tri, log_low, NN)
            middle, last = row_scales(total)
            key_scale = jnp.sqrt(one_less_exp(log_part))
            raw = kap_ref[:, at].astype(F32)
            norm = product(raw * raw, ones, NN)
            a = raw / jnp.sqrt(norm + 1e-06)
            e_neg = jnp.exp(middle - total)
            a_mid = a * jnp.exp(total - log_part - middle)
            b_mid = rem_ref[:, at].astype(F32) * a * e_neg
            k_mid = key_ref[:, at].astype(F32) * key_scale * e_neg
            r_mid = rec_ref[:, at].astype(F32) * jnp.exp(total - middle)
            for ref, value in zip((tot_ref, ks_ref, a_ref, b_ref, k_ref), (total, key_scale, a_mid, b_mid, k_mid)):
                ref[pair] = value
            upper = split(jnp.concatenate([a_mid, r_mid], 0))
            rights = split(jnp.concatenate([b_mid, k_mid], 0))
            for h, m in enumerate(own2):
                gram = product(upper, tuple(jnp.where(m, x, zero) for x in rights), NT)
                m_ab.append(jnp.where(strict, gram[:frames, :frames], 0.0))
                kept = (
                    (ak_ref, jnp.where(strict, gram[:frames, frames:], 0.0)),
                    (rb_ref, jnp.where(lax_tri, gram[frames:, :frames], 0.0)),
                    (rk_ref, jnp.where(lax_tri, gram[frames:, frames:], 0.0)),
                )
                for ref, value in kept:
                    ref[0, pair * 2 + h], ref[1, pair * 2 + h] = split(value)
        inverted = inverses(m_ab, row, col)
        for m, pair in enumerate(pairs):
            at = lanes(pair)
            v = val_ref[:, at]
            total = tot_ref[pair]
            middle, last = row_scales(total)
            a_abs = a_ref[pair] * jnp.exp(middle)
            scale = jnp.exp(last - middle)
            t_inv = [split(inverted[m * 2 + h]) for h in range(2)]
            for h in range(2):
                t_ref[0, pair * 2 + h], t_ref[1, pair * 2 + h] = t_inv[h]
            on_v = both(lambda h: product((ak_ref[0, pair * 2 + h], ak_ref[1, pair * 2 + h]), v, NN), lane_low)
            given = split(jnp.concatenate([on_v, a_abs], 1))
            inner = both(lambda h: product(t_inv[h], given, NN), low2)
            u_ref[pair], x_ref[pair] = inner[:, :PAIR], inner[:, PAIR:]
            ended = product(inner, b_ref[pair] * scale, TN)
            through = pack(jnp.where(prow == pcol, jnp.exp(last), 0.0) - ended[PAIR:], pack_low)
            offset = pack(product(v, k_ref[pair] * scale, TN) - ended[:PAIR], pack_low)
            for part in range(parts):
                pay_out[pair * parts + part, :HEAD_SIZE] = through
                pay_out[pair * parts + part, HEAD_SIZE:] = offset[part * rows_each : (part + 1) * rows_each]
        send_all(2, g * per_group, per_group)

        @pl.when(n == 0)
        def _():
            cross_frames.wait_recv()
            send_all(1, 0, near)
            ring_steps(0)

        return carried

    for load in loads[1:9]:
        load.wait()
    lax.fori_loop(0, groups, first, 0)

    arrive(0)
    arrive(1)
    loads[9].wait()
    some_pairs = 2

    def project(n, carried):
        wide = some_pairs * PAIR
        weight = w_ref[rows(n, wide), :]
        out = dot1(gath[...], weight, (((0,), (1,)), ((), ())))
        for m in range(some_pairs):
            gy_ref[n * some_pairs + m] = out[:, m * PAIR : (m + 1) * PAIR]
        return carried

    lax.fori_loop(0, PAIRS // some_pairs, project, 0)

    def second(n, carried):
        g = far_first(n)
        for pair in [g * group + m for m in range(group)]:
            total = tot_ref[pair]
            middle, last = row_scales(total)
            scale = jnp.exp(last - middle)
            q = split(gy_ref[pair])
            r = rec_ref[:, lanes(pair)].astype(F32)
            back = both(lambda h: product((rb_ref[0, pair * 2 + h], rb_ref[1, pair * 2 + h]), q, TN), lane_low)
            given = split(jnp.concatenate([back, b_ref[pair] * scale], 1))
            pulled = both(lambda h: product((t_ref[0, pair * 2 + h], t_ref[1, pair * 2 + h]), given, TN), low2)
            p0 = pulled[:, :PAIR]
            p_ref[pair], tb_ref[pair] = p0, pulled[:, PAIR:]
            pull = product(q, r * jnp.exp(total), TN) - product(p0, a_ref[pair] * jnp.exp(middle), TN)
            pull = pack(pull, pack_low)
            for part in range(parts):
                pull_out[pair * parts + part] = pull[part * rows_each : (part + 1) * rows_each]
        send_all(3, g * per_group, per_group)
        return carried

    lax.fori_loop(0, PAIRS // group, second, 0)

    def third(g, carried):
        for pair in [g * group + n for n in range(group)]:
            v = val_ref[:, lanes(pair)]
            total = tot_ref[pair]
            middle, last = row_scales(total)
            q = split(gy_ref[pair])
            inner = split(jnp.concatenate([u_ref[pair], x_ref[pair]], 1))
            minus = both(lambda h: product((rb_ref[0, pair * 2 + h], rb_ref[1, pair * 2 + h]), inner, NN), low2)
            m_rk = [(rk_ref[0, pair * 2 + h], rk_ref[1, pair * 2 + h]) for h in range(2)]
            y_ref[pair] = both(lambda h: product(m_rk[h], v, NN), lane_low) - minus[:, :PAIR]
            yr_ref[pair] = rec_ref[:, lanes(pair)].astype(F32) * jnp.exp(total) - minus[:, PAIR:]
            pulled = split(jnp.concatenate([p_ref[pair], tb_ref[pair]], 1))
            minus = both(lambda h: product((ak_ref[0, pair * 2 + h], ak_ref[1, pair * 2 + h]), pulled, TN), low2)
            gv_ref[pair] = both(lambda h: product(m_rk[h], q, TN), lane_low) - minus[:, :PAIR]
            gvk_ref[pair] = k_ref[pair] * jnp.exp(last - middle) - minus[:, PAIR:]
        return carried

    lax.fori_loop(0, PAIRS // group, third, 0)
    ring_end(0)

    arrive(2)
    arrive(3)
    ring_begin(1)

    def ready(i, carried):
        link = split(unpack(pay_in[i, :HEAD_SIZE], diagonal))
        down, across = jnp.concatenate(link, 0), jnp.concatenate(link, 1)
        link_row[i] = jnp.concatenate([across, across], 0)
        link_col[i] = jnp.concatenate([down, down], 1)
        return carried

    lax.fori_loop(0, near, ready, 0)

    def carry_over(x, link, dims):
        out = dot1(jnp.concatenate(split(x), 1), link, dims)
        return out[:, :PAIR] + out[:, PAIR:]

    def ahead(i, state):
        held[0, i] = state
        return pay_in[i, HEAD_SIZE:] + carry_over(state, link_row[i], NN)

    def astern(i, grad):
        j = near - 1 - i
        held[1, j] = grad
        return pull_in[j] + carry_over(grad, link_col[j], NT)

    @pl.when(side == 0)
    def _():
        cross_out[...] = lax.fori_loop(
            0, near, ahead, jnp.concatenate([start_ref[0], start_ref[1]], 1), unroll=near <= 8
        )

    @pl.when(side == 1)
    def _():
        cross_out[...] = lax.fori_loop(0, near, astern, jnp.zeros((rows_each, PAIR), F32), unroll=near <= 8)

    cross_state.start()

    @pl.when(side == 0)
    def _():
        send_all(4, 0, near)

    @pl.when(side == 1)
    def _():
        send_all(5, 0, near)

    def fourth(g, carried):
        for pair in [g * group + n for n in range(group)]:
            v = val_ref[:, lanes(pair)]
            total = tot_ref[pair]
            middle, last = row_scales(total)
            e_pos, e_neg = jnp.exp(total - middle), jnp.exp(middle - total)
            q = split(gy_ref[pair])
            v_own = [jnp.where(m, v, zero) for m in own]
            q_own = [tuple(jnp.where(m, x, zero) for x in q) for m in own]
            k_mid, r_mid = split(k_ref[pair]), split(rec_ref[:, lanes(pair)].astype(F32) * e_pos)
            gra_ref[pair] = e_pos * both(
                lambda h: product(jnp.where(lax_tri, product(q, v_own[h], NT), 0.0), k_mid, NN), lane_low
            )
            gka_ref[pair] = ks_ref[pair] * e_neg * both(
                lambda h: product(jnp.where(row <= col, product(v, q_own[h], NT), 0.0), r_mid, NN), lane_low
            )
        return carried

    lax.fori_loop(0, groups // 2, fourth, 0)
    cross_state.wait_recv()

    @pl.when(side == 0)
    def _():
        lax.fori_loop(0, near, astern, cross_in[...], unroll=near <= 8)
        send_all(5, 0, near)

    @pl.when(side == 1)
    def _():
        lax.fori_loop(0, near, ahead, cross_in[...], unroll=near <= 8)
        send_all(4, 0, near)

    ring_steps(1)
    lax.fori_loop(groups // 2, groups, fourth, 0)
    arrive(4)

    def state_of(pair):
        return unpack(landed[0, rows(pair, HEAD_SIZE)], diagonal)

    def grad_of(pair):
        return unpack(landed[1, rows(pair, HEAD_SIZE)], diagonal)

    def fifth(g, carried):
        for pair in [g * group + n for n in range(group)]:
            y = y_ref[pair] + product(yr_ref[pair], state_of(pair), NT)
            y = y.T.astype(BF16)
            for m in range(PAIR // features):
                block = pair * (PAIR // features) + m
                ylow[block // near, lax.rem(block, near)] = y[m * features : (m + 1) * features]
        return carried

    for g in range(groups):
        fifth(g, 0)
        send_all(6 + g, 0, near)
    arrive(5)

    def sixth(g, carried):
        for pair in [g * group + n for n in range(group)]:
            at = lanes(pair)
            state, grad = split(state_of(pair)), split(grad_of(pair))
            q, v = split(gy_ref[pair]), val_ref[:, at]
            u = split(u_ref[pair] + product(x_ref[pair], state, NT))
            behind = product(jnp.concatenate([tb_ref[pair], gvk_ref[pair]], 0), grad, NT)
            p = split(p_ref[pair] + behind[:frames])
            all_out[2, :, at] = (gv_ref[pair] + behind[frames:]).astype(BF16)
            b_mid, a_mid = split(b_ref[pair]), split(a_ref[pair])
            total = tot_ref[pair]
            middle, last = row_scales(total)

            def removed(h):
                gram = product(q, tuple(jnp.where(own[h], x, zero) for x in u), NT)
                return product(jnp.where(lax_tri, gram, 0.0), b_mid, NN)

            def removed_back(h):
                gram = product(v, tuple(jnp.where(own[h], x, zero) for x in p), NT)
                return product(jnp.where(row < col, gram, 0.0), a_mid, NN)

            gr = jnp.exp(total) * product(q, state, NN) + gra_ref[pair]
            gr = gr - jnp.exp(total - middle) * both(removed, lane_low)
            all_out[0, :, at] = gr.astype(BF16)
            gk = jnp.exp(last - total) * product(v, grad, NN) - jnp.exp(middle - total) * both(
                removed_back, lane_low
            )
            all_out[1, :, at] = (gk * ks_ref[pair] + gka_ref[pair]).astype(BF16)
        return carried

    lax.fori_loop(0, groups // 2, sixth, 0)
    ring_end(1)
    ring_done(0)
    ring_done(1)
    arrive(6)
    arrive(7)
    per = 2 * PAIR // features
    loss_scale = 1.0 / math.sqrt(frames * count)

    def weigh(n, carried):
        blocks = half_go[n * per // near, pl.ds(lax.rem(n * per, near), per)].reshape(per * features, wide)
        out = dot1(mine[...].reshape(2 * features, wide), blocks, NT) * loss_scale
        part_ref[0, n] = out[:features]
        part_ref[1, n] = out[features:]
        part_out[n] = part_ref[1 - side, n].astype(BF16)
        cross_part(n).start()
        return carried

    lax.fori_loop(0, chunks, weigh, 0)
    lax.fori_loop(groups // 2, groups, sixth, 0)
    for n in range(chunks):
        cross_part(n).wait_recv()
        gw_out[:, rows(n, 2 * PAIR)] = part_ref[side, n] + part_in[n].astype(F32)
    for way in range(ways):
        others(lambda i: remote(way, i, here).wait_send())
    cross_frames.wait_send()
    cross_state.wait_send()
    for n in range(chunks):
        cross_part(n).wait_send()


def local(receptance, key_input, values, log_decay, kappa_raw, removal, initial_state, out_weight, grad_output):
    size = lax.axis_size("tm")
    frames, width = receptance.shape
    near = size // 2
    parts = near // PAIRS
    rows_each = HEAD_SIZE // parts
    features = grad_output.shape[0]
    chunks = width // (2 * PAIR)
    whole = pl.BlockSpec(memory_space=pltpu.VMEM)
    anywhere = pl.BlockSpec(memory_space=pl.ANY)
    flat = pltpu.VMEM((PAIRS, frames, PAIR), F32)
    matrix = pltpu.VMEM((2, HEAD_COUNT, frames, frames), BF16)
    vectors, grad_weight = pl.pallas_call(
        functools.partial(stream_kernel, size, parts),
        in_specs=[anywhere] * 9,
        out_specs=[whole] * 2,
        out_shape=[jax.ShapeDtypeStruct((3, frames, width), BF16)] + [jax.ShapeDtypeStruct((features, width), F32)],
        scratch_shapes=[
            pltpu.VMEM((frames, width), BF16),
            pltpu.VMEM((frames, width), BF16),
            pltpu.VMEM((frames, width), BF16),
            pltpu.VMEM((frames, width), BF16),
            pltpu.VMEM((frames, width), BF16),
            pltpu.VMEM((frames, width), BF16),
            pltpu.VMEM((2, rows_each, HEAD_SIZE), F32),
            pltpu.VMEM(grad_output.shape, BF16),
            pltpu.VMEM((width, width), BF16),
            pltpu.VMEM((width, frames), BF16),
        ]
        + [flat] * 16
        + [matrix] * 4
        + [
            pltpu.VMEM((near, HEAD_SIZE + rows_each, PAIR), F32),
            pltpu.VMEM((near, HEAD_SIZE + rows_each, PAIR), F32),
            pltpu.VMEM((near, rows_each, PAIR), F32),
            pltpu.VMEM((near, rows_each, PAIR), F32),
            pltpu.VMEM((near, 2 * PAIR, 2 * PAIR), BF16),
            pltpu.VMEM((near, 2 * PAIR, 2 * PAIR), BF16),
            pltpu.VMEM((2, near, rows_each, PAIR), F32),
            pltpu.VMEM((2, PAIRS * HEAD_SIZE, PAIR), F32),
            pltpu.VMEM((2, near, features, frames), BF16),
            pltpu.VMEM((2, features, near * frames), BF16),
            pltpu.VMEM((2, near, features, near * frames), BF16),
            pltpu.VMEM((rows_each, PAIR), F32),
            pltpu.VMEM((rows_each, PAIR), F32),
            pltpu.VMEM((2, chunks, features, 2 * PAIR), F32),
            pltpu.VMEM((chunks, features, 2 * PAIR), BF16),
            pltpu.VMEM((chunks, features, 2 * PAIR), BF16),
            pltpu.SemaphoreType.DMA((11,)),
            pltpu.SemaphoreType.DMA((8,)),
            pltpu.SemaphoreType.DMA((8, near)),
            pltpu.SemaphoreType.DMA((8, near)),
            pltpu.SemaphoreType.DMA((2 + chunks,)),
            pltpu.SemaphoreType.DMA((2 + chunks,)),
            pltpu.SemaphoreType.DMA((2, 2, near // 4)),
            pltpu.SemaphoreType.DMA((2, 2, near // 4)),
            pltpu.SemaphoreType.DMA((2, 2, near // 4 + 1)),
            pltpu.SemaphoreType.DMA((2, 2, near // 4 + 1)),
        ],
        compiler_params=pltpu.CompilerParams(
            collective_id=0, has_side_effects=True, vmem_limit_bytes=56 << 20
        ),
        name="stream",
    )(receptance, key_input, values, log_decay, kappa_raw, removal, initial_state, grad_output, out_weight)
    return vectors[0], vectors[1], vectors[2], grad_weight


def solution(mesh):
    rows = P(("groups", "tm"), None)
    return jax.shard_map(
        local,
        mesh=mesh,
        in_specs=(rows,) * 6 + (P("groups", None, None), P(), P("tm", "groups")),
        out_specs=(rows,) * 4,
        check_vma=False,
    )
```

```python
import functools
import math

import jax
import jax.numpy as jnp
from jax import lax
from jax.experimental import pallas as pl
from jax.experimental.pallas import tpu as pltpu
from jax.sharding import PartitionSpec as P

HEAD_COUNT = 16
HEAD_SIZE = 64
PAIR = 2 * HEAD_SIZE
PAIRS = HEAD_COUNT // 2
GROUP = 4
F32 = jnp.float32
BF16 = jnp.bfloat16

NN = (((1,), (0,)), ((), ()))
NT = (((1,), (1,)), ((), ()))
TN = (((0,), (0,)), ((), ()))


def split(x):
    high = x.astype(BF16)
    return high, (x - high.astype(F32)).astype(BF16)


def dot1(a, b, dims):
    return lax.dot_general(a, b, dims, preferred_element_type=F32)


def dot3(a, b, dims):
    a = (a,) if not isinstance(a, tuple) and a.dtype == BF16 else a if isinstance(a, tuple) else split(a)
    b = (b,) if not isinstance(b, tuple) and b.dtype == BF16 else b if isinstance(b, tuple) else split(b)
    out = dot1(a[0], b[0], dims)
    if len(b) > 1:
        out = out + dot1(a[0], b[1], dims)
    if len(a) > 1:
        out = out + dot1(a[1], b[0], dims)
    return out


def iota(shape, dim):
    return lax.broadcasted_iota(jnp.int32, shape, dim)


def both(f, lane_low):
    return jnp.where(lane_low, f(0), f(1))


def pack(full, lane_low):
    return jnp.where(lane_low, full[:HEAD_SIZE], full[HEAD_SIZE:])


def unpack(packed, diagonal):
    return jnp.where(diagonal, jnp.concatenate([packed, packed], 0), 0.0)


def product(a, b, dims):
    a = a if isinstance(a, tuple) else (a,) if a.dtype == BF16 else split(a)
    b = b if isinstance(b, tuple) else (b,) if b.dtype == BF16 else split(b)
    (ca,), (cb,) = dims[0]
    if len(a) == 1 and len(b) == 1:
        return dot1(a[0], b[0], dims)
    if len(b) == 1:
        return dot1(jnp.concatenate(a, ca), jnp.concatenate([b[0], b[0]], cb), dims)
    if len(a) == 1:
        return dot1(jnp.concatenate([a[0], a[0]], ca), jnp.concatenate(b, cb), dims)
    wide = b[0].shape[1 - cb]
    if wide <= PAIR:
        right = jnp.concatenate(b, 1 - cb)
        out = dot1(jnp.concatenate(a, ca), jnp.concatenate([right, right], cb), dims)
        return out[:, :wide] + out[:, wide:]
    out = dot1(jnp.concatenate(a, ca), jnp.concatenate([b[0], b[0]], cb), dims)
    return out + dot1(a[0], b[1], dims)


def inverses(lower, row, col):
    size = row.shape[0]
    eye = jnp.where(row == col, 1.0, 0.0).astype(F32)
    block = 8
    inside = row // block == col // block
    first = [jnp.where(inside, m, 0.0) for m in lower]
    halves = [split(m) for m in first]
    square = [split(product(m, m, NN)) for m in halves]
    left = [eye - m for m in first]
    tall = [tuple(jnp.concatenate(x, 0) for x in zip(split(m), s)) for m, s in zip(left, square)]
    tall = [product(m, s, NN) for m, s in zip(tall, square)]
    left = [m + t[:size] for m, t in zip(left, tall)]
    out = [m + product(m, t[size:], NN) for m, t in zip(left, tall)]
    while block < size:
        inside = (row // (4 * block) == col // (4 * block)) & (row // block != col // block)
        halves = [split(t) for t in out]
        near = [split(product(t, jnp.where(inside, m, 0.0), NN)) for t, m in zip(halves, lower)]
        both_of = [
            product(n, tuple(jnp.concatenate(x, 1) for x in zip(n, t)), NN) for n, t in zip(near, halves)
        ]
        out = [t - m[:, size:] for t, m in zip(out, both_of)]
        out = [t + product(m[:, :size], t, NN) for t, m in zip(out, both_of)]
        block *= 4
    return out


def one_less_exp(x):
    series = jnp.full_like(x, 1.0 / math.factorial(10))
    for n in range(9, 0, -1):
        series = series * x + 1.0 / math.factorial(n)
    return jnp.where(x > -0.5, -x * series, 1.0 - jnp.exp(x))


def row_scales(total):
    frames = total.shape[0]
    return total[frames // 2 - 1 : frames // 2], total[frames - 1 : frames]


def stream_kernel(count, parts, rec_hbm, key_hbm, val_hbm, log_hbm, kap_hbm, rem_hbm, start_hbm, go_hbm, w_hbm,
                  all_out, gw_out,
                  rec_ref, key_ref, val_ref, log_ref, kap_ref, rem_ref, start_ref, go_ref, w_ref, gath, gy_ref, tot_ref, ks_ref, a_ref, b_ref, k_ref, u_ref, x_ref, y_ref, yr_ref,
                  p_ref, tb_ref, gv_ref, gvk_ref, gra_ref, gka_ref, t_ref, ak_ref, rb_ref, rk_ref,
                  pay_out, pay_in, pull_out, pull_in, link_row, link_col, held, landed, ylow, mine, half_go,
                  cross_out, cross_in, part_ref, part_out, part_in,
                  copy_sem, local_sem, send_sem, recv_sem, cross_send, cross_recv,
                  ring_send, ring_recv, twin_send, twin_recv):
    frames = rec_hbm.shape[0]
    rows_each = HEAD_SIZE // parts
    features = go_hbm.shape[0]
    near = count // 2
    wide = near * frames
    me = lax.axis_index("tm")
    side, here = me // near, lax.rem(me, near)
    partner = lax.rem(me + near, count)
    row, col = iota((frames, frames), 0), iota((frames, frames), 1)
    lane_low = iota((frames, PAIR), 1) < HEAD_SIZE
    own = [lane_low, jnp.logical_not(lane_low)]
    low2 = jnp.concatenate([lane_low, lane_low], 1)
    own2 = [jnp.concatenate([m, m], 0) for m in own]
    pack_low = iota((HEAD_SIZE, PAIR), 1) < HEAD_SIZE
    prow, pcol = iota((PAIR, PAIR), 0), iota((PAIR, PAIR), 1)
    diagonal = (prow // HEAD_SIZE) == (pcol // HEAD_SIZE)
    ones = jnp.where(diagonal, 1.0, 0.0).astype(BF16)
    tri = jnp.where(row >= col, 1.0, 0.0).astype(BF16)
    strict, lax_tri = row > col, row >= col
    zero = jnp.zeros((), BF16)

    begin = pl.ds(pl.multiple_of(lax.rem(here, parts) * rows_each, rows_each), rows_each)
    moves = [(go_hbm, go_ref)]
    moves += zip((log_hbm, kap_hbm, rem_hbm, key_hbm, rec_hbm, val_hbm), (log_ref, kap_ref, rem_ref, key_ref, rec_ref, val_ref))
    moves += [(start_hbm.at[here // parts * 2 + h, begin], start_ref.at[h]) for h in range(2)]
    moves += [(w_hbm, w_ref)]
    loads = [pltpu.make_async_copy(a, b, copy_sem.at[1 + n]) for n, (a, b) in enumerate(moves)]
    for load in loads:
        load.start()

    barrier = pltpu.get_barrier_semaphore()

    def greet(i):
        pl.semaphore_signal(barrier, inc=1, device_id={"tm": i}, device_id_type=pl.DeviceIdType.MESH)

    def others(f):
        def step(i, carried):
            @pl.when(i != here)
            def _():
                f(i)

            return carried

        lax.fori_loop(0, near, step, 0)

    others(lambda i: greet(side * near + i))
    greet(partner)
    pl.semaphore_wait(barrier, near)

    def lanes(i):
        return pl.ds(pl.multiple_of(i * PAIR, PAIR), PAIR)

    def rows(i, n):
        return pl.ds(pl.multiple_of(i * n, n), n)

    sources = (
        lambda i: go_ref.at[:, rows(side * near + i, frames)],
        lambda i: half_go.at[1 - side, here, :, rows(i, frames)],
        lambda i: pay_out.at[i],
        lambda i: pull_out.at[i],
        lambda i: held.at[0, i],
        lambda i: held.at[1, i],
        lambda i: ylow.at[0, i],
        lambda i: ylow.at[1, i],
    )
    places = (
        lambda i: gath.at[rows(side * near + i, features)],
        lambda i: gath.at[rows((1 - side) * near + i, features)],
        lambda i: pay_in.at[i],
        lambda i: pull_in.at[i],
        lambda i: landed.at[0, rows(i, rows_each)],
        lambda i: landed.at[1, rows(i, rows_each)],
        lambda i: mine.at[0, :, rows(i, frames)],
        lambda i: mine.at[1, :, rows(i, frames)],
    )
    ways = len(sources)

    def remote(way, i, origin):
        return pltpu.make_async_remote_copy(
            src_ref=sources[way](i),
            dst_ref=places[way](origin),
            send_sem=send_sem.at[way, i],
            recv_sem=recv_sem.at[way, origin],
            device_id={"tm": side * near + i},
            device_id_type=pl.DeviceIdType.MESH,
        )

    def local(way):
        return pltpu.make_async_copy(sources[way](here), places[way](here), local_sem.at[way])

    def send(way, i):
        @pl.when(i != here)
        def _():
            remote(way, i, here).start()

        @pl.when(i == here)
        def _():
            local(way).start()

    def send_all(way, begin, many):
        def step(i, carried):
            send(way, begin + lax.rem(here + many // 2 + i, many))
            return carried

        lax.fori_loop(0, many, step, 0)

    def arrive(way):
        others(lambda i: remote(way, i, i).wait_recv())
        local(way).wait()

    def across(source, place, n):
        return pltpu.make_async_remote_copy(
            src_ref=source,
            dst_ref=place,
            send_sem=cross_send.at[n],
            recv_sem=cross_recv.at[n],
            device_id={"tm": partner},
            device_id_type=pl.DeviceIdType.MESH,
        )

    cross_frames = across(go_ref.at[:, rows(1 - side, wide)], half_go.at[side, here], 0)
    cross_state = across(cross_out, cross_in, 1)
    chunks = part_out.shape[0]

    def cross_part(n):
        return across(part_out.at[n], part_in.at[n], 2 + n)

    chips = near // 2
    hops = chips // 2
    core = lax.rem(here, 2)
    chip = here // 2
    spot = jnp.where(lax.rem(chip, 2) == 0, chip // 2, chips - 1 - chip // 2)

    def place_at(spot):
        spot = lax.rem(spot + 2 * chips, chips)
        return 2 * jnp.where(spot < hops, 2 * spot, 2 * (chips - 1 - spot) + 1) + core

    def ring(of, way, step, part):
        toward = 1 - 2 * way
        block = half_go.at[lax.rem(side + of, 2), place_at(spot - toward * (step - 1))]
        if part:
            block = block.at[:, pl.ds(way * (wide // 2), wide // 2)]
        return pltpu.make_async_remote_copy(
            src_ref=block,
            dst_ref=block,
            send_sem=ring_send.at[of, way, step - 1],
            recv_sem=ring_recv.at[of, way, step - 1],
            device_id={"tm": side * near + place_at(spot + toward)},
            device_id_type=pl.DeviceIdType.MESH,
        )

    def twin(of, way, step):
        block = half_go.at[lax.rem(side + of, 2), place_at(spot - (1 - 2 * way) * step)]
        return pltpu.make_async_remote_copy(
            src_ref=block,
            dst_ref=block,
            send_sem=twin_send.at[of, way, step],
            recv_sem=twin_recv.at[of, way, step],
            device_id={"tm": me + 1 - 2 * core},
            device_id_type=pl.DeviceIdType.MESH,
        )

    def ring_begin(of):
        for way in range(2):
            ring(of, way, 1, False).start()
        twin(of, 0, 0).start()

    def ring_steps(of):
        def body(step, carried):
            for way in range(2):
                ring(of, way, step, False).wait_recv()
            for way in range(2):
                ring(of, way, step + 1, False).start()
            for way in range(2):
                twin(of, way, step).start()
            return carried

        lax.fori_loop(1, hops - 1, body, 0)
        for way in range(2):
            ring(of, way, hops - 1, False).wait_recv()
        for way in range(2):
            ring(of, way, hops, True).start()
        for way in range(2):
            twin(of, way, hops - 1).start()

    def ring_end(of):
        for way in range(2):
            ring(of, way, hops, True).wait_recv()
        twin(of, 0, hops).start()

    def ring_done(of):
        def body(step, carried):
            for way in range(2):
                ring(of, way, step, False).wait_send()
                twin(of, way, step).wait()
            return carried

        lax.fori_loop(1, hops, body, 0)
        for way in range(2):
            ring(of, way, hops, True).wait_send()
        twin(of, 0, 0).wait()
        twin(of, 0, hops).wait()

    loads[0].wait()
    cross_frames.start()
    send_all(0, 0, near)
    own_half = pltpu.make_async_copy(go_ref.at[:, rows(side, wide)], half_go.at[side, here], copy_sem.at[0])
    own_half.start()
    own_half.wait()
    ring_begin(0)

    group = GROUP
    groups = PAIRS // group
    per_group = group * parts

    def far_first(n):
        return lax.rem(n + 1 + here * groups // near, groups)

    def first(n, carried):
        g = far_first(n)
        pairs = [g * group + m for m in range(group)]
        m_ab = []
        for pair in pairs:
            at = lanes(pair)
            log_low = log_ref[:, at]
            log_part = log_low.astype(F32)
            total = dot1(tri, log_low, NN)
            middle, last = row_scales(total)
            key_scale = jnp.sqrt(one_less_exp(log_part))
            raw = kap_ref[:, at].astype(F32)
            norm = product(raw * raw, ones, NN)
            a = raw / jnp.sqrt(norm + 1e-06)
            e_neg = jnp.exp(middle - total)
            a_mid = a * jnp.exp(total - log_part - middle)
            b_mid = rem_ref[:, at].astype(F32) * a * e_neg
            k_mid = key_ref[:, at].astype(F32) * key_scale * e_neg
            r_mid = rec_ref[:, at].astype(F32) * jnp.exp(total - middle)
            for ref, value in zip((tot_ref, ks_ref, a_ref, b_ref, k_ref), (total, key_scale, a_mid, b_mid, k_mid)):
                ref[pair] = value
            upper = split(jnp.concatenate([a_mid, r_mid], 0))
            rights = split(jnp.concatenate([b_mid, k_mid], 0))
            for h, m in enumerate(own2):
                gram = product(upper, tuple(jnp.where(m, x, zero) for x in rights), NT)
                m_ab.append(jnp.where(strict, gram[:frames, :frames], 0.0))
                kept = (
                    (ak_ref, jnp.where(strict, gram[:frames, frames:], 0.0)),
                    (rb_ref, jnp.where(lax_tri, gram[frames:, :frames], 0.0)),
                    (rk_ref, jnp.where(lax_tri, gram[frames:, frames:], 0.0)),
                )
                for ref, value in kept:
                    ref[0, pair * 2 + h], ref[1, pair * 2 + h] = split(value)
        inverted = inverses(m_ab, row, col)
        for m, pair in enumerate(pairs):
            at = lanes(pair)
            v = val_ref[:, at]
            total = tot_ref[pair]
            middle, last = row_scales(total)
            a_abs = a_ref[pair] * jnp.exp(middle)
            scale = jnp.exp(last - middle)
            t_inv = [split(inverted[m * 2 + h]) for h in range(2)]
            for h in range(2):
                t_ref[0, pair * 2 + h], t_ref[1, pair * 2 + h] = t_inv[h]
            on_v = both(lambda h: product((ak_ref[0, pair * 2 + h], ak_ref[1, pair * 2 + h]), v, NN), lane_low)
            given = split(jnp.concatenate([on_v, a_abs], 1))
            inner = both(lambda h: product(t_inv[h], given, NN), low2)
            u_ref[pair], x_ref[pair] = inner[:, :PAIR], inner[:, PAIR:]
            ended = product(inner, b_ref[pair] * scale, TN)
            through = pack(jnp.where(prow == pcol, jnp.exp(last), 0.0) - ended[PAIR:], pack_low)
            offset = pack(product(v, k_ref[pair] * scale, TN) - ended[:PAIR], pack_low)
            for part in range(parts):
                pay_out[pair * parts + part, :HEAD_SIZE] = through
                pay_out[pair * parts + part, HEAD_SIZE:] = offset[part * rows_each : (part + 1) * rows_each]
        send_all(2, g * per_group, per_group)

        @pl.when(n == 0)
        def _():
            cross_frames.wait_recv()
            send_all(1, 0, near)
            ring_steps(0)

        return carried

    for load in loads[1:9]:
        load.wait()
    lax.fori_loop(0, groups, first, 0)

    arrive(0)
    arrive(1)
    ring_begin(1)
    loads[9].wait()
    some_pairs = 2

    def project(n, carried):
        wide = some_pairs * PAIR
        weight = w_ref[rows(n, wide), :]
        out = dot1(gath[...], weight, (((0,), (1,)), ((), ())))
        for m in range(some_pairs):
            gy_ref[n * some_pairs + m] = out[:, m * PAIR : (m + 1) * PAIR]
        return carried

    lax.fori_loop(0, PAIRS // some_pairs, project, 0)

    def second(n, carried):
        g = far_first(n)
        for pair in [g * group + m for m in range(group)]:
            total = tot_ref[pair]
            middle, last = row_scales(total)
            scale = jnp.exp(last - middle)
            q = split(gy_ref[pair])
            r = rec_ref[:, lanes(pair)].astype(F32)
            back = both(lambda h: product((rb_ref[0, pair * 2 + h], rb_ref[1, pair * 2 + h]), q, TN), lane_low)
            given = split(jnp.concatenate([back, b_ref[pair] * scale], 1))
            pulled = both(lambda h: product((t_ref[0, pair * 2 + h], t_ref[1, pair * 2 + h]), given, TN), low2)
            p0 = pulled[:, :PAIR]
            p_ref[pair], tb_ref[pair] = p0, pulled[:, PAIR:]
            pull = product(q, r * jnp.exp(total), TN) - product(p0, a_ref[pair] * jnp.exp(middle), TN)
            pull = pack(pull, pack_low)
            for part in range(parts):
                pull_out[pair * parts + part] = pull[part * rows_each : (part + 1) * rows_each]
        send_all(3, g * per_group, per_group)
        return carried

    lax.fori_loop(0, PAIRS // group, second, 0)

    def third(g, carried):
        for pair in [g * group + n for n in range(group)]:
            v = val_ref[:, lanes(pair)]
            total = tot_ref[pair]
            middle, last = row_scales(total)
            q = split(gy_ref[pair])
            inner = split(jnp.concatenate([u_ref[pair], x_ref[pair]], 1))
            minus = both(lambda h: product((rb_ref[0, pair * 2 + h], rb_ref[1, pair * 2 + h]), inner, NN), low2)
            m_rk = [(rk_ref[0, pair * 2 + h], rk_ref[1, pair * 2 + h]) for h in range(2)]
            y_ref[pair] = both(lambda h: product(m_rk[h], v, NN), lane_low) - minus[:, :PAIR]
            yr_ref[pair] = rec_ref[:, lanes(pair)].astype(F32) * jnp.exp(total) - minus[:, PAIR:]
            pulled = split(jnp.concatenate([p_ref[pair], tb_ref[pair]], 1))
            minus = both(lambda h: product((ak_ref[0, pair * 2 + h], ak_ref[1, pair * 2 + h]), pulled, TN), low2)
            gv_ref[pair] = both(lambda h: product(m_rk[h], q, TN), lane_low) - minus[:, :PAIR]
            gvk_ref[pair] = k_ref[pair] * jnp.exp(last - middle) - minus[:, PAIR:]
        return carried

    lax.fori_loop(0, PAIRS // group, third, 0)
    ring_steps(1)
    ring_end(0)

    arrive(2)
    arrive(3)

    def ready(i, carried):
        link = split(unpack(pay_in[i, :HEAD_SIZE], diagonal))
        down, across = jnp.concatenate(link, 0), jnp.concatenate(link, 1)
        link_row[i] = jnp.concatenate([across, across], 0)
        link_col[i] = jnp.concatenate([down, down], 1)
        return carried

    lax.fori_loop(0, near, ready, 0)

    def carry_over(x, link, dims):
        out = dot1(jnp.concatenate(split(x), 1), link, dims)
        return out[:, :PAIR] + out[:, PAIR:]

    def ahead(i, state):
        held[0, i] = state
        return pay_in[i, HEAD_SIZE:] + carry_over(state, link_row[i], NN)

    def astern(i, grad):
        j = near - 1 - i
        held[1, j] = grad
        return pull_in[j] + carry_over(grad, link_col[j], NT)

    @pl.when(side == 0)
    def _():
        cross_out[...] = lax.fori_loop(
            0, near, ahead, jnp.concatenate([start_ref[0], start_ref[1]], 1), unroll=near <= 8
        )

    @pl.when(side == 1)
    def _():
        cross_out[...] = lax.fori_loop(0, near, astern, jnp.zeros((rows_each, PAIR), F32), unroll=near <= 8)

    cross_state.start()

    @pl.when(side == 0)
    def _():
        send_all(4, 0, near)

    @pl.when(side == 1)
    def _():
        send_all(5, 0, near)

    def fourth(g, carried):
        for pair in [g * group + n for n in range(group)]:
            v = val_ref[:, lanes(pair)]
            total = tot_ref[pair]
            middle, last = row_scales(total)
            e_pos, e_neg = jnp.exp(total - middle), jnp.exp(middle - total)
            q = split(gy_ref[pair])
            v_own = [jnp.where(m, v, zero) for m in own]
            q_own = [tuple(jnp.where(m, x, zero) for x in q) for m in own]
            k_mid, r_mid = split(k_ref[pair]), split(rec_ref[:, lanes(pair)].astype(F32) * e_pos)
            gra_ref[pair] = e_pos * both(
                lambda h: product(jnp.where(lax_tri, product(q, v_own[h], NT), 0.0), k_mid, NN), lane_low
            )
            gka_ref[pair] = ks_ref[pair] * e_neg * both(
                lambda h: product(jnp.where(row <= col, product(v, q_own[h], NT), 0.0), r_mid, NN), lane_low
            )
        return carried

    lax.fori_loop(0, groups // 2, fourth, 0)
    cross_state.wait_recv()

    @pl.when(side == 0)
    def _():
        lax.fori_loop(0, near, astern, cross_in[...], unroll=near <= 8)
        send_all(5, 0, near)

    @pl.when(side == 1)
    def _():
        lax.fori_loop(0, near, ahead, cross_in[...], unroll=near <= 8)
        send_all(4, 0, near)

    lax.fori_loop(groups // 2, groups, fourth, 0)
    arrive(4)

    def state_of(pair):
        return unpack(landed[0, rows(pair, HEAD_SIZE)], diagonal)

    def grad_of(pair):
        return unpack(landed[1, rows(pair, HEAD_SIZE)], diagonal)

    def fifth(g, carried):
        for pair in [g * group + n for n in range(group)]:
            y = y_ref[pair] + product(yr_ref[pair], state_of(pair), NT)
            y = y.T.astype(BF16)
            for m in range(PAIR // features):
                block = pair * (PAIR // features) + m
                ylow[block // near, lax.rem(block, near)] = y[m * features : (m + 1) * features]
        return carried

    for g in range(groups):
        fifth(g, 0)
        send_all(6 + g, 0, near)
    arrive(5)

    def sixth(g, carried):
        for pair in [g * group + n for n in range(group)]:
            at = lanes(pair)
            state, grad = split(state_of(pair)), split(grad_of(pair))
            q, v = split(gy_ref[pair]), val_ref[:, at]
            u = split(u_ref[pair] + product(x_ref[pair], state, NT))
            behind = product(jnp.concatenate([tb_ref[pair], gvk_ref[pair]], 0), grad, NT)
            p = split(p_ref[pair] + behind[:frames])
            all_out[2, :, at] = (gv_ref[pair] + behind[frames:]).astype(BF16)
            b_mid, a_mid = split(b_ref[pair]), split(a_ref[pair])
            total = tot_ref[pair]
            middle, last = row_scales(total)

            def removed(h):
                gram = product(q, tuple(jnp.where(own[h], x, zero) for x in u), NT)
                return product(jnp.where(lax_tri, gram, 0.0), b_mid, NN)

            def removed_back(h):
                gram = product(v, tuple(jnp.where(own[h], x, zero) for x in p), NT)
                return product(jnp.where(row < col, gram, 0.0), a_mid, NN)

            gr = jnp.exp(total) * product(q, state, NN) + gra_ref[pair]
            gr = gr - jnp.exp(total - middle) * both(removed, lane_low)
            all_out[0, :, at] = gr.astype(BF16)
            gk = jnp.exp(last - total) * product(v, grad, NN) - jnp.exp(middle - total) * both(
                removed_back, lane_low
            )
            all_out[1, :, at] = (gk * ks_ref[pair] + gka_ref[pair]).astype(BF16)
        return carried

    lax.fori_loop(0, groups // 2, sixth, 0)
    ring_end(1)
    ring_done(0)
    ring_done(1)
    arrive(6)
    arrive(7)
    per = 2 * PAIR // features
    loss_scale = 1.0 / math.sqrt(frames * count)

    def weigh(n, carried):
        blocks = half_go[n * per // near, pl.ds(lax.rem(n * per, near), per)].reshape(per * features, wide)
        out = dot1(mine[...].reshape(2 * features, wide), blocks, NT) * loss_scale
        part_ref[0, n] = out[:features]
        part_ref[1, n] = out[features:]
        part_out[n] = part_ref[1 - side, n].astype(BF16)
        cross_part(n).start()
        return carried

    lax.fori_loop(0, chunks, weigh, 0)
    lax.fori_loop(groups // 2, groups, sixth, 0)
    for n in range(chunks):
        cross_part(n).wait_recv()
        gw_out[:, rows(n, 2 * PAIR)] = part_ref[side, n] + part_in[n].astype(F32)
    for way in range(ways):
        others(lambda i: remote(way, i, here).wait_send())
    cross_frames.wait_send()
    cross_state.wait_send()
    for n in range(chunks):
        cross_part(n).wait_send()


def local(receptance, key_input, values, log_decay, kappa_raw, removal, initial_state, out_weight, grad_output):
    size = lax.axis_size("tm")
    frames, width = receptance.shape
    near = size // 2
    parts = near // PAIRS
    rows_each = HEAD_SIZE // parts
    features = grad_output.shape[0]
    chunks = width // (2 * PAIR)
    whole = pl.BlockSpec(memory_space=pltpu.VMEM)
    anywhere = pl.BlockSpec(memory_space=pl.ANY)
    flat = pltpu.VMEM((PAIRS, frames, PAIR), F32)
    matrix = pltpu.VMEM((2, HEAD_COUNT, frames, frames), BF16)
    vectors, grad_weight = pl.pallas_call(
        functools.partial(stream_kernel, size, parts),
        in_specs=[anywhere] * 9,
        out_specs=[whole] * 2,
        out_shape=[jax.ShapeDtypeStruct((3, frames, width), BF16)] + [jax.ShapeDtypeStruct((features, width), F32)],
        scratch_shapes=[
            pltpu.VMEM((frames, width), BF16),
            pltpu.VMEM((frames, width), BF16),
            pltpu.VMEM((frames, width), BF16),
            pltpu.VMEM((frames, width), BF16),
            pltpu.VMEM((frames, width), BF16),
            pltpu.VMEM((frames, width), BF16),
            pltpu.VMEM((2, rows_each, HEAD_SIZE), F32),
            pltpu.VMEM(grad_output.shape, BF16),
            pltpu.VMEM((width, width), BF16),
            pltpu.VMEM((width, frames), BF16),
        ]
        + [flat] * 16
        + [matrix] * 4
        + [
            pltpu.VMEM((near, HEAD_SIZE + rows_each, PAIR), F32),
            pltpu.VMEM((near, HEAD_SIZE + rows_each, PAIR), F32),
            pltpu.VMEM((near, rows_each, PAIR), F32),
            pltpu.VMEM((near, rows_each, PAIR), F32),
            pltpu.VMEM((near, 2 * PAIR, 2 * PAIR), BF16),
            pltpu.VMEM((near, 2 * PAIR, 2 * PAIR), BF16),
            pltpu.VMEM((2, near, rows_each, PAIR), F32),
            pltpu.VMEM((2, PAIRS * HEAD_SIZE, PAIR), F32),
            pltpu.VMEM((2, near, features, frames), BF16),
            pltpu.VMEM((2, features, near * frames), BF16),
            pltpu.VMEM((2, near, features, near * frames), BF16),
            pltpu.VMEM((rows_each, PAIR), F32),
            pltpu.VMEM((rows_each, PAIR), F32),
            pltpu.VMEM((2, chunks, features, 2 * PAIR), F32),
            pltpu.VMEM((chunks, features, 2 * PAIR), BF16),
            pltpu.VMEM((chunks, features, 2 * PAIR), BF16),
            pltpu.SemaphoreType.DMA((11,)),
            pltpu.SemaphoreType.DMA((8,)),
            pltpu.SemaphoreType.DMA((8, near)),
            pltpu.SemaphoreType.DMA((8, near)),
            pltpu.SemaphoreType.DMA((2 + chunks,)),
            pltpu.SemaphoreType.DMA((2 + chunks,)),
            pltpu.SemaphoreType.DMA((2, 2, near // 4)),
            pltpu.SemaphoreType.DMA((2, 2, near // 4)),
            pltpu.SemaphoreType.DMA((2, 2, near // 4 + 1)),
            pltpu.SemaphoreType.DMA((2, 2, near // 4 + 1)),
        ],
        compiler_params=pltpu.CompilerParams(
            collective_id=0, has_side_effects=True, vmem_limit_bytes=56 << 20
        ),
        name="stream",
    )(receptance, key_input, values, log_decay, kappa_raw, removal, initial_state, grad_output, out_weight)
    return vectors[0], vectors[1], vectors[2], grad_weight


def solution(mesh):
    rows = P(("groups", "tm"), None)
    return jax.shard_map(
        local,
        mesh=mesh,
        in_specs=(rows,) * 6 + (P("groups", None, None), P(), P("tm", "groups")),
        out_specs=(rows,) * 4,
        check_vma=False,
    )
```

```python
import functools
import math

import jax
import jax.numpy as jnp
from jax import lax
from jax.experimental import pallas as pl
from jax.experimental.pallas import tpu as pltpu
from jax.sharding import PartitionSpec as P

HEAD_COUNT = 16
HEAD_SIZE = 64
PAIR = 2 * HEAD_SIZE
PAIRS = HEAD_COUNT // 2
GROUP = 4
F32 = jnp.float32
BF16 = jnp.bfloat16

NN = (((1,), (0,)), ((), ()))
NT = (((1,), (1,)), ((), ()))
TN = (((0,), (0,)), ((), ()))


def split(x):
    high = x.astype(BF16)
    return high, (x - high.astype(F32)).astype(BF16)


def dot1(a, b, dims):
    return lax.dot_general(a, b, dims, preferred_element_type=F32)


def dot3(a, b, dims):
    a = (a,) if not isinstance(a, tuple) and a.dtype == BF16 else a if isinstance(a, tuple) else split(a)
    b = (b,) if not isinstance(b, tuple) and b.dtype == BF16 else b if isinstance(b, tuple) else split(b)
    out = dot1(a[0], b[0], dims)
    if len(b) > 1:
        out = out + dot1(a[0], b[1], dims)
    if len(a) > 1:
        out = out + dot1(a[1], b[0], dims)
    return out


def iota(shape, dim):
    return lax.broadcasted_iota(jnp.int32, shape, dim)


def both(f, lane_low):
    return jnp.where(lane_low, f(0), f(1))


def pack(full, lane_low):
    return jnp.where(lane_low, full[:HEAD_SIZE], full[HEAD_SIZE:])


def unpack(packed, diagonal):
    return jnp.where(diagonal, jnp.concatenate([packed, packed], 0), 0.0)


def product(a, b, dims):
    a = a if isinstance(a, tuple) else (a,) if a.dtype == BF16 else split(a)
    b = b if isinstance(b, tuple) else (b,) if b.dtype == BF16 else split(b)
    (ca,), (cb,) = dims[0]
    if len(a) == 1 and len(b) == 1:
        return dot1(a[0], b[0], dims)
    if len(b) == 1:
        return dot1(jnp.concatenate(a, ca), jnp.concatenate([b[0], b[0]], cb), dims)
    if len(a) == 1:
        return dot1(jnp.concatenate([a[0], a[0]], ca), jnp.concatenate(b, cb), dims)
    wide = b[0].shape[1 - cb]
    if wide <= PAIR:
        right = jnp.concatenate(b, 1 - cb)
        out = dot1(jnp.concatenate(a, ca), jnp.concatenate([right, right], cb), dims)
        return out[:, :wide] + out[:, wide:]
    out = dot1(jnp.concatenate(a, ca), jnp.concatenate([b[0], b[0]], cb), dims)
    return out + dot1(a[0], b[1], dims)


def inverses(lower, row, col):
    size = row.shape[0]
    eye = jnp.where(row == col, 1.0, 0.0).astype(F32)
    block = 8
    inside = row // block == col // block
    first = [jnp.where(inside, m, 0.0) for m in lower]
    halves = [split(m) for m in first]
    square = [split(product(m, m, NN)) for m in halves]
    left = [eye - m for m in first]
    tall = [tuple(jnp.concatenate(x, 0) for x in zip(split(m), s)) for m, s in zip(left, square)]
    tall = [product(m, s, NN) for m, s in zip(tall, square)]
    left = [m + t[:size] for m, t in zip(left, tall)]
    out = [m + product(m, t[size:], NN) for m, t in zip(left, tall)]
    while block < size:
        inside = (row // (4 * block) == col // (4 * block)) & (row // block != col // block)
        halves = [split(t) for t in out]
        near = [split(product(t, jnp.where(inside, m, 0.0), NN)) for t, m in zip(halves, lower)]
        both_of = [
            product(n, tuple(jnp.concatenate(x, 1) for x in zip(n, t)), NN) for n, t in zip(near, halves)
        ]
        out = [t - m[:, size:] for t, m in zip(out, both_of)]
        out = [t + product(m[:, :size], t, NN) for t, m in zip(out, both_of)]
        block *= 4
    return out


def one_less_exp(x):
    series = jnp.full_like(x, 1.0 / math.factorial(10))
    for n in range(9, 0, -1):
        series = series * x + 1.0 / math.factorial(n)
    return jnp.where(x > -0.5, -x * series, 1.0 - jnp.exp(x))


def row_scales(total):
    frames = total.shape[0]
    return total[frames // 2 - 1 : frames // 2], total[frames - 1 : frames]


def stream_kernel(count, parts, rec_hbm, key_hbm, val_hbm, log_hbm, kap_hbm, rem_hbm, start_hbm, go_hbm, w_hbm,
                  all_out, gw_out,
                  rec_ref, key_ref, val_ref, log_ref, kap_ref, rem_ref, start_ref, go_ref, w_ref, gath, gy_ref, tot_ref, ks_ref, a_ref, b_ref, k_ref, u_ref, x_ref, y_ref, yr_ref,
                  p_ref, tb_ref, gv_ref, gvk_ref, gra_ref, gka_ref, t_ref, ak_ref, rb_ref, rk_ref,
                  pay_out, pay_in, pull_out, pull_in, link_row, link_col, held, landed, ylow, mine, half_go,
                  cross_out, cross_in, part_ref, part_out, part_in,
                  copy_sem, local_sem, send_sem, recv_sem, cross_send, cross_recv,
                  ring_send, ring_recv, twin_send, twin_recv):
    frames = rec_hbm.shape[0]
    rows_each = HEAD_SIZE // parts
    features = go_hbm.shape[0]
    near = count // 2
    wide = near * frames
    me = lax.axis_index("tm")
    side, here = me // near, lax.rem(me, near)
    partner = lax.rem(me + near, count)
    row, col = iota((frames, frames), 0), iota((frames, frames), 1)
    lane_low = iota((frames, PAIR), 1) < HEAD_SIZE
    own = [lane_low, jnp.logical_not(lane_low)]
    low2 = jnp.concatenate([lane_low, lane_low], 1)
    own2 = [jnp.concatenate([m, m], 0) for m in own]
    pack_low = iota((HEAD_SIZE, PAIR), 1) < HEAD_SIZE
    prow, pcol = iota((PAIR, PAIR), 0), iota((PAIR, PAIR), 1)
    diagonal = (prow // HEAD_SIZE) == (pcol // HEAD_SIZE)
    ones = jnp.where(diagonal, 1.0, 0.0).astype(BF16)
    tri = jnp.where(row >= col, 1.0, 0.0).astype(BF16)
    strict, lax_tri = row > col, row >= col
    zero = jnp.zeros((), BF16)

    begin = pl.ds(pl.multiple_of(lax.rem(here, parts) * rows_each, rows_each), rows_each)
    moves = [(go_hbm, go_ref)]
    moves += zip((log_hbm, kap_hbm, rem_hbm, key_hbm, rec_hbm, val_hbm), (log_ref, kap_ref, rem_ref, key_ref, rec_ref, val_ref))
    moves += [(start_hbm.at[here // parts * 2 + h, begin], start_ref.at[h]) for h in range(2)]
    moves += [(w_hbm, w_ref)]
    loads = [pltpu.make_async_copy(a, b, copy_sem.at[1 + n]) for n, (a, b) in enumerate(moves)]
    for load in loads:
        load.start()

    barrier = pltpu.get_barrier_semaphore()

    def greet(i):
        pl.semaphore_signal(barrier, inc=1, device_id={"tm": i}, device_id_type=pl.DeviceIdType.MESH)

    def others(f):
        def step(i, carried):
            @pl.when(i != here)
            def _():
                f(i)

            return carried

        lax.fori_loop(0, near, step, 0)

    others(lambda i: greet(side * near + i))
    greet(partner)
    pl.semaphore_wait(barrier, near)

    def lanes(i):
        return pl.ds(pl.multiple_of(i * PAIR, PAIR), PAIR)

    def rows(i, n):
        return pl.ds(pl.multiple_of(i * n, n), n)

    sources = (
        lambda i: go_ref.at[:, rows(side * near + i, frames)],
        lambda i: half_go.at[1 - side, here, :, rows(i, frames)],
        lambda i: pay_out.at[i],
        lambda i: pull_out.at[i],
        lambda i: held.at[0, i],
        lambda i: held.at[1, i],
        lambda i: ylow.at[0, i],
        lambda i: ylow.at[1, i],
    )
    places = (
        lambda i: gath.at[rows(side * near + i, features)],
        lambda i: gath.at[rows((1 - side) * near + i, features)],
        lambda i: pay_in.at[i],
        lambda i: pull_in.at[i],
        lambda i: landed.at[0, rows(i, rows_each)],
        lambda i: landed.at[1, rows(i, rows_each)],
        lambda i: mine.at[0, :, rows(i, frames)],
        lambda i: mine.at[1, :, rows(i, frames)],
    )
    ways = len(sources)

    def remote(way, i, origin):
        return pltpu.make_async_remote_copy(
            src_ref=sources[way](i),
            dst_ref=places[way](origin),
            send_sem=send_sem.at[way, i],
            recv_sem=recv_sem.at[way, origin],
            device_id={"tm": side * near + i},
            device_id_type=pl.DeviceIdType.MESH,
        )

    def local(way):
        return pltpu.make_async_copy(sources[way](here), places[way](here), local_sem.at[way])

    def send(way, i):
        @pl.when(i != here)
        def _():
            remote(way, i, here).start()

        @pl.when(i == here)
        def _():
            local(way).start()

    def send_all(way, begin, many):
        def step(i, carried):
            send(way, begin + lax.rem(here + many // 2 + i, many))
            return carried

        lax.fori_loop(0, many, step, 0)

    def arrive(way):
        others(lambda i: remote(way, i, i).wait_recv())
        local(way).wait()

    def across(source, place, n):
        return pltpu.make_async_remote_copy(
            src_ref=source,
            dst_ref=place,
            send_sem=cross_send.at[n],
            recv_sem=cross_recv.at[n],
            device_id={"tm": partner},
            device_id_type=pl.DeviceIdType.MESH,
        )

    cross_frames = across(go_ref.at[:, rows(1 - side, wide)], half_go.at[side, here], 0)
    cross_state = across(cross_out, cross_in, 1)
    chunks = part_out.shape[0]

    def cross_part(n):
        return across(part_out.at[n], part_in.at[n], 2 + n)

    chips = near // 2
    hops = chips // 2
    core = lax.rem(here, 2)
    chip = here // 2
    spot = jnp.where(lax.rem(chip, 2) == 0, chip // 2, chips - 1 - chip // 2)

    def place_at(spot):
        spot = lax.rem(spot + 2 * chips, chips)
        return 2 * jnp.where(spot < hops, 2 * spot, 2 * (chips - 1 - spot) + 1) + core

    def ring(of, way, step, part):
        toward = 1 - 2 * way
        block = half_go.at[lax.rem(side + of, 2), place_at(spot - toward * (step - 1))]
        if part:
            block = block.at[:, pl.ds(way * (wide // 2), wide // 2)]
        return pltpu.make_async_remote_copy(
            src_ref=block,
            dst_ref=block,
            send_sem=ring_send.at[of, way, step - 1],
            recv_sem=ring_recv.at[of, way, step - 1],
            device_id={"tm": side * near + place_at(spot + toward)},
            device_id_type=pl.DeviceIdType.MESH,
        )

    def twin(of, way, step):
        block = half_go.at[lax.rem(side + of, 2), place_at(spot - (1 - 2 * way) * step)]
        return pltpu.make_async_remote_copy(
            src_ref=block,
            dst_ref=block,
            send_sem=twin_send.at[of, way, step],
            recv_sem=twin_recv.at[of, way, step],
            device_id={"tm": me + 1 - 2 * core},
            device_id_type=pl.DeviceIdType.MESH,
        )

    def ring_begin(of):
        for way in range(2):
            ring(of, way, 1, False).start()
        twin(of, 0, 0).start()

    def ring_steps(of):
        def body(step, carried):
            for way in range(2):
                ring(of, way, step, False).wait_recv()
            for way in range(2):
                ring(of, way, step + 1, False).start()
            for way in range(2):
                twin(of, way, step).start()
            return carried

        lax.fori_loop(1, hops - 1, body, 0)
        for way in range(2):
            ring(of, way, hops - 1, False).wait_recv()
        for way in range(2):
            ring(of, way, hops, True).start()
        for way in range(2):
            twin(of, way, hops - 1).start()

    def ring_end(of):
        for way in range(2):
            ring(of, way, hops, True).wait_recv()
        twin(of, 0, hops).start()

    def ring_done(of):
        def body(step, carried):
            for way in range(2):
                ring(of, way, step, False).wait_send()
                twin(of, way, step).wait()
            return carried

        lax.fori_loop(1, hops, body, 0)
        for way in range(2):
            ring(of, way, hops, True).wait_send()
        twin(of, 0, 0).wait()
        twin(of, 0, hops).wait()

    loads[0].wait()
    cross_frames.start()
    send_all(0, 0, near)
    own_half = pltpu.make_async_copy(go_ref.at[:, rows(side, wide)], half_go.at[side, here], copy_sem.at[0])
    own_half.start()
    own_half.wait()
    ring_begin(0)

    group = GROUP
    groups = PAIRS // group
    per_group = group * parts

    def far_first(n):
        return lax.rem(n + 1 + here * groups // near, groups)

    def first(n, carried):
        g = far_first(n)
        pairs = [g * group + m for m in range(group)]
        m_ab = []
        for pair in pairs:
            at = lanes(pair)
            log_low = log_ref[:, at]
            log_part = log_low.astype(F32)
            total = dot1(tri, log_low, NN)
            middle, last = row_scales(total)
            key_scale = jnp.sqrt(one_less_exp(log_part))
            raw = kap_ref[:, at].astype(F32)
            norm = product(raw * raw, ones, NN)
            a = raw / jnp.sqrt(norm + 1e-06)
            e_neg = jnp.exp(middle - total)
            a_mid = a * jnp.exp(total - log_part - middle)
            b_mid = rem_ref[:, at].astype(F32) * a * e_neg
            k_mid = key_ref[:, at].astype(F32) * key_scale * e_neg
            r_mid = rec_ref[:, at].astype(F32) * jnp.exp(total - middle)
            for ref, value in zip((tot_ref, ks_ref, a_ref, b_ref, k_ref), (total, key_scale, a_mid, b_mid, k_mid)):
                ref[pair] = value
            upper = split(jnp.concatenate([a_mid, r_mid], 0))
            rights = split(jnp.concatenate([b_mid, k_mid], 0))
            for h, m in enumerate(own2):
                gram = product(upper, tuple(jnp.where(m, x, zero) for x in rights), NT)
                m_ab.append(jnp.where(strict, gram[:frames, :frames], 0.0))
                kept = (
                    (ak_ref, jnp.where(strict, gram[:frames, frames:], 0.0)),
                    (rb_ref, jnp.where(lax_tri, gram[frames:, :frames], 0.0)),
                    (rk_ref, jnp.where(lax_tri, gram[frames:, frames:], 0.0)),
                )
                for ref, value in kept:
                    ref[0, pair * 2 + h], ref[1, pair * 2 + h] = split(value)
        inverted = inverses(m_ab, row, col)
        for m, pair in enumerate(pairs):
            at = lanes(pair)
            v = val_ref[:, at]
            total = tot_ref[pair]
            middle, last = row_scales(total)
            a_abs = a_ref[pair] * jnp.exp(middle)
            scale = jnp.exp(last - middle)
            t_inv = [split(inverted[m * 2 + h]) for h in range(2)]
            for h in range(2):
                t_ref[0, pair * 2 + h], t_ref[1, pair * 2 + h] = t_inv[h]
            on_v = both(lambda h: product((ak_ref[0, pair * 2 + h], ak_ref[1, pair * 2 + h]), v, NN), lane_low)
            given = split(jnp.concatenate([on_v, a_abs], 1))
            inner = both(lambda h: product(t_inv[h], given, NN), low2)
            u_ref[pair], x_ref[pair] = inner[:, :PAIR], inner[:, PAIR:]
            ended = product(inner, b_ref[pair] * scale, TN)
            through = pack(jnp.where(prow == pcol, jnp.exp(last), 0.0) - ended[PAIR:], pack_low)
            offset = pack(product(v, k_ref[pair] * scale, TN) - ended[:PAIR], pack_low)
            for part in range(parts):
                pay_out[pair * parts + part, :HEAD_SIZE] = through
                pay_out[pair * parts + part, HEAD_SIZE:] = offset[part * rows_each : (part + 1) * rows_each]
        send_all(2, g * per_group, per_group)

        @pl.when(n == 0)
        def _():
            cross_frames.wait_recv()
            send_all(1, 0, near)
            ring_steps(0)

        return carried

    for load in loads[1:9]:
        load.wait()
    lax.fori_loop(0, groups, first, 0)

    arrive(0)
    arrive(1)
    ring_begin(1)
    loads[9].wait()
    some_pairs = 2

    def project(n, carried):
        wide = some_pairs * PAIR
        weight = w_ref[rows(n, wide), :]
        out = dot1(gath[...], weight, (((0,), (1,)), ((), ())))
        for m in range(some_pairs):
            gy_ref[n * some_pairs + m] = out[:, m * PAIR : (m + 1) * PAIR]
        return carried

    lax.fori_loop(0, PAIRS // some_pairs, project, 0)

    def second(n, carried):
        g = far_first(n)
        for pair in [g * group + m for m in range(group)]:
            total = tot_ref[pair]
            middle, last = row_scales(total)
            scale = jnp.exp(last - middle)
            q = split(gy_ref[pair])
            r = rec_ref[:, lanes(pair)].astype(F32)
            back = both(lambda h: product((rb_ref[0, pair * 2 + h], rb_ref[1, pair * 2 + h]), q, TN), lane_low)
            given = split(jnp.concatenate([back, b_ref[pair] * scale], 1))
            pulled = both(lambda h: product((t_ref[0, pair * 2 + h], t_ref[1, pair * 2 + h]), given, TN), low2)
            p0 = pulled[:, :PAIR]
            p_ref[pair], tb_ref[pair] = p0, pulled[:, PAIR:]
            pull = product(q, r * jnp.exp(total), TN) - product(p0, a_ref[pair] * jnp.exp(middle), TN)
            pull = pack(pull, pack_low)
            for part in range(parts):
                pull_out[pair * parts + part] = pull[part * rows_each : (part + 1) * rows_each]
        send_all(3, g * per_group, per_group)
        return carried

    lax.fori_loop(0, PAIRS // group, second, 0)

    def third(g, carried):
        for pair in [g * group + n for n in range(group)]:
            v = val_ref[:, lanes(pair)]
            inner = split(jnp.concatenate([u_ref[pair], x_ref[pair]], 1))
            minus = both(lambda h: product((rb_ref[0, pair * 2 + h], rb_ref[1, pair * 2 + h]), inner, NN), low2)
            m_rk = [(rk_ref[0, pair * 2 + h], rk_ref[1, pair * 2 + h]) for h in range(2)]
            y_ref[pair] = both(lambda h: product(m_rk[h], v, NN), lane_low) - minus[:, :PAIR]
            yr_ref[pair] = rec_ref[:, lanes(pair)].astype(F32) * jnp.exp(tot_ref[pair]) - minus[:, PAIR:]
        return carried

    def third_back(g, carried):
        for pair in [g * group + n for n in range(group)]:
            middle, last = row_scales(tot_ref[pair])
            q = split(gy_ref[pair])
            m_rk = [(rk_ref[0, pair * 2 + h], rk_ref[1, pair * 2 + h]) for h in range(2)]
            pulled = split(jnp.concatenate([p_ref[pair], tb_ref[pair]], 1))
            minus = both(lambda h: product((ak_ref[0, pair * 2 + h], ak_ref[1, pair * 2 + h]), pulled, TN), low2)
            gv_ref[pair] = both(lambda h: product(m_rk[h], q, TN), lane_low) - minus[:, :PAIR]
            gvk_ref[pair] = k_ref[pair] * jnp.exp(last - middle) - minus[:, PAIR:]
        return carried

    def ready(i, carried):
        link = split(unpack(pay_in[i, :HEAD_SIZE], diagonal))
        down, over = jnp.concatenate(link, 0), jnp.concatenate(link, 1)
        link_row[i] = jnp.concatenate([over, over], 0)
        link_col[i] = jnp.concatenate([down, down], 1)
        return carried

    def carry_over(x, link, dims):
        out = dot1(jnp.concatenate(split(x), 1), link, dims)
        return out[:, :PAIR] + out[:, PAIR:]

    def ahead(i, state):
        held[0, i] = state
        return pay_in[i, HEAD_SIZE:] + carry_over(state, link_row[i], NN)

    def astern(i, grad):
        j = near - 1 - i
        held[1, j] = grad
        return pull_in[j] + carry_over(grad, link_col[j], NT)

    def laps(step, begin):
        return lax.fori_loop(0, near, step, begin, unroll=near <= 8)

    arrive(2)
    lax.fori_loop(0, near, ready, 0)

    @pl.when(side == 0)
    def _():
        cross_out[...] = laps(ahead, jnp.concatenate([start_ref[0], start_ref[1]], 1))
        cross_state.start()
        send_all(4, 0, near)

    lax.fori_loop(0, groups, third, 0)
    ring_steps(1)
    ring_end(0)

    @pl.when(side == 1)
    def _():
        cross_state.wait_recv()
        laps(ahead, cross_in[...])
        send_all(4, 0, near)

    arrive(3)

    @pl.when(side == 1)
    def _():
        cross_out[...] = laps(astern, jnp.zeros((rows_each, PAIR), F32))
        cross_state.start()
        send_all(5, 0, near)

    def fourth(g, carried):
        for pair in [g * group + n for n in range(group)]:
            v = val_ref[:, lanes(pair)]
            total = tot_ref[pair]
            middle, last = row_scales(total)
            e_pos, e_neg = jnp.exp(total - middle), jnp.exp(middle - total)
            q = split(gy_ref[pair])
            v_own = [jnp.where(m, v, zero) for m in own]
            q_own = [tuple(jnp.where(m, x, zero) for x in q) for m in own]
            k_mid, r_mid = split(k_ref[pair]), split(rec_ref[:, lanes(pair)].astype(F32) * e_pos)
            gra_ref[pair] = e_pos * both(
                lambda h: product(jnp.where(lax_tri, product(q, v_own[h], NT), 0.0), k_mid, NN), lane_low
            )
            gka_ref[pair] = ks_ref[pair] * e_neg * both(
                lambda h: product(jnp.where(row <= col, product(v, q_own[h], NT), 0.0), r_mid, NN), lane_low
            )
        return carried

    lax.fori_loop(0, groups // 2, fourth, 0)
    arrive(4)

    def state_of(pair):
        return unpack(landed[0, rows(pair, HEAD_SIZE)], diagonal)

    def grad_of(pair):
        return unpack(landed[1, rows(pair, HEAD_SIZE)], diagonal)

    def fifth(g, carried):
        for pair in [g * group + n for n in range(group)]:
            y = y_ref[pair] + product(yr_ref[pair], state_of(pair), NT)
            y = y.T.astype(BF16)
            for m in range(PAIR // features):
                block = pair * (PAIR // features) + m
                ylow[block // near, lax.rem(block, near)] = y[m * features : (m + 1) * features]
        return carried

    for g in range(groups):
        fifth(g, 0)
        send_all(6 + g, 0, near)

    @pl.when(side == 0)
    def _():
        cross_state.wait_recv()
        laps(astern, cross_in[...])
        send_all(5, 0, near)

    lax.fori_loop(0, groups, third_back, 0)
    lax.fori_loop(groups // 2, groups, fourth, 0)
    ring_end(1)

    def sixth(g, carried):
        for pair in [g * group + n for n in range(group)]:
            at = lanes(pair)
            state, grad = split(state_of(pair)), split(grad_of(pair))
            q, v = split(gy_ref[pair]), val_ref[:, at]
            u = split(u_ref[pair] + product(x_ref[pair], state, NT))
            behind = product(jnp.concatenate([tb_ref[pair], gvk_ref[pair]], 0), grad, NT)
            p = split(p_ref[pair] + behind[:frames])
            all_out[2, :, at] = (gv_ref[pair] + behind[frames:]).astype(BF16)
            b_mid, a_mid = split(b_ref[pair]), split(a_ref[pair])
            total = tot_ref[pair]
            middle, last = row_scales(total)

            def removed(h):
                gram = product(q, tuple(jnp.where(own[h], x, zero) for x in u), NT)
                return product(jnp.where(lax_tri, gram, 0.0), b_mid, NN)

            def removed_back(h):
                gram = product(v, tuple(jnp.where(own[h], x, zero) for x in p), NT)
                return product(jnp.where(row < col, gram, 0.0), a_mid, NN)

            gr = jnp.exp(total) * product(q, state, NN) + gra_ref[pair]
            gr = gr - jnp.exp(total - middle) * both(removed, lane_low)
            all_out[0, :, at] = gr.astype(BF16)
            gk = jnp.exp(last - total) * product(v, grad, NN) - jnp.exp(middle - total) * both(
                removed_back, lane_low
            )
            all_out[1, :, at] = (gk * ks_ref[pair] + gka_ref[pair]).astype(BF16)
        return carried

    ring_done(0)
    ring_done(1)
    arrive(6)
    arrive(7)
    per = 2 * PAIR // features
    loss_scale = 1.0 / math.sqrt(frames * count)

    def weigh(n, carried):
        blocks = half_go[n * per // near, pl.ds(lax.rem(n * per, near), per)].reshape(per * features, wide)
        out = dot1(mine[...].reshape(2 * features, wide), blocks, NT) * loss_scale
        part_ref[0, n] = out[:features]
        part_ref[1, n] = out[features:]
        part_out[n] = part_ref[1 - side, n].astype(BF16)
        cross_part(n).start()
        return carried

    lax.fori_loop(0, chunks, weigh, 0)
    arrive(5)
    lax.fori_loop(0, groups, sixth, 0)
    for n in range(chunks):
        cross_part(n).wait_recv()
        gw_out[:, rows(n, 2 * PAIR)] = part_ref[side, n] + part_in[n].astype(F32)
    for way in range(ways):
        others(lambda i: remote(way, i, here).wait_send())
    cross_frames.wait_send()
    cross_state.wait_send()
    for n in range(chunks):
        cross_part(n).wait_send()


def local(receptance, key_input, values, log_decay, kappa_raw, removal, initial_state, out_weight, grad_output):
    size = lax.axis_size("tm")
    frames, width = receptance.shape
    near = size // 2
    parts = near // PAIRS
    rows_each = HEAD_SIZE // parts
    features = grad_output.shape[0]
    chunks = width // (2 * PAIR)
    whole = pl.BlockSpec(memory_space=pltpu.VMEM)
    anywhere = pl.BlockSpec(memory_space=pl.ANY)
    flat = pltpu.VMEM((PAIRS, frames, PAIR), F32)
    matrix = pltpu.VMEM((2, HEAD_COUNT, frames, frames), BF16)
    vectors, grad_weight = pl.pallas_call(
        functools.partial(stream_kernel, size, parts),
        in_specs=[anywhere] * 9,
        out_specs=[whole] * 2,
        out_shape=[jax.ShapeDtypeStruct((3, frames, width), BF16)] + [jax.ShapeDtypeStruct((features, width), F32)],
        scratch_shapes=[
            pltpu.VMEM((frames, width), BF16),
            pltpu.VMEM((frames, width), BF16),
            pltpu.VMEM((frames, width), BF16),
            pltpu.VMEM((frames, width), BF16),
            pltpu.VMEM((frames, width), BF16),
            pltpu.VMEM((frames, width), BF16),
            pltpu.VMEM((2, rows_each, HEAD_SIZE), F32),
            pltpu.VMEM(grad_output.shape, BF16),
            pltpu.VMEM((width, width), BF16),
            pltpu.VMEM((width, frames), BF16),
        ]
        + [flat] * 16
        + [matrix] * 4
        + [
            pltpu.VMEM((near, HEAD_SIZE + rows_each, PAIR), F32),
            pltpu.VMEM((near, HEAD_SIZE + rows_each, PAIR), F32),
            pltpu.VMEM((near, rows_each, PAIR), F32),
            pltpu.VMEM((near, rows_each, PAIR), F32),
            pltpu.VMEM((near, 2 * PAIR, 2 * PAIR), BF16),
            pltpu.VMEM((near, 2 * PAIR, 2 * PAIR), BF16),
            pltpu.VMEM((2, near, rows_each, PAIR), F32),
            pltpu.VMEM((2, PAIRS * HEAD_SIZE, PAIR), F32),
            pltpu.VMEM((2, near, features, frames), BF16),
            pltpu.VMEM((2, features, near * frames), BF16),
            pltpu.VMEM((2, near, features, near * frames), BF16),
            pltpu.VMEM((rows_each, PAIR), F32),
            pltpu.VMEM((rows_each, PAIR), F32),
            pltpu.VMEM((2, chunks, features, 2 * PAIR), F32),
            pltpu.VMEM((chunks, features, 2 * PAIR), BF16),
            pltpu.VMEM((chunks, features, 2 * PAIR), BF16),
            pltpu.SemaphoreType.DMA((11,)),
            pltpu.SemaphoreType.DMA((8,)),
            pltpu.SemaphoreType.DMA((8, near)),
            pltpu.SemaphoreType.DMA((8, near)),
            pltpu.SemaphoreType.DMA((2 + chunks,)),
            pltpu.SemaphoreType.DMA((2 + chunks,)),
            pltpu.SemaphoreType.DMA((2, 2, near // 4)),
            pltpu.SemaphoreType.DMA((2, 2, near // 4)),
            pltpu.SemaphoreType.DMA((2, 2, near // 4 + 1)),
            pltpu.SemaphoreType.DMA((2, 2, near // 4 + 1)),
        ],
        compiler_params=pltpu.CompilerParams(
            collective_id=0, has_side_effects=True, vmem_limit_bytes=56 << 20
        ),
        name="stream",
    )(receptance, key_input, values, log_decay, kappa_raw, removal, initial_state, grad_output, out_weight)
    return vectors[0], vectors[1], vectors[2], grad_weight


def solution(mesh):
    rows = P(("groups", "tm"), None)
    return jax.shard_map(
        local,
        mesh=mesh,
        in_specs=(rows,) * 6 + (P("groups", None, None), P(), P("tm", "groups")),
        out_specs=(rows,) * 4,
        check_vma=False,
    )
```

```python
import functools
import math

import jax
import jax.numpy as jnp
from jax import lax
from jax.experimental import pallas as pl
from jax.experimental.pallas import tpu as pltpu
from jax.sharding import PartitionSpec as P

HEAD_COUNT = 16
HEAD_SIZE = 64
PAIR = 2 * HEAD_SIZE
PAIRS = HEAD_COUNT // 2
GROUP = 4
F32 = jnp.float32
BF16 = jnp.bfloat16

NN = (((1,), (0,)), ((), ()))
NT = (((1,), (1,)), ((), ()))
TN = (((0,), (0,)), ((), ()))


def split(x):
    high = x.astype(BF16)
    return high, (x - high.astype(F32)).astype(BF16)


def dot1(a, b, dims):
    return lax.dot_general(a, b, dims, preferred_element_type=F32)


def dot3(a, b, dims):
    a = (a,) if not isinstance(a, tuple) and a.dtype == BF16 else a if isinstance(a, tuple) else split(a)
    b = (b,) if not isinstance(b, tuple) and b.dtype == BF16 else b if isinstance(b, tuple) else split(b)
    out = dot1(a[0], b[0], dims)
    if len(b) > 1:
        out = out + dot1(a[0], b[1], dims)
    if len(a) > 1:
        out = out + dot1(a[1], b[0], dims)
    return out


def iota(shape, dim):
    return lax.broadcasted_iota(jnp.int32, shape, dim)


def both(f, lane_low):
    return jnp.where(lane_low, f(0), f(1))


def pack(full, lane_low):
    return jnp.where(lane_low, full[:HEAD_SIZE], full[HEAD_SIZE:])


def unpack(packed, diagonal):
    return jnp.where(diagonal, jnp.concatenate([packed, packed], 0), 0.0)


def product(a, b, dims):
    a = a if isinstance(a, tuple) else (a,) if a.dtype == BF16 else split(a)
    b = b if isinstance(b, tuple) else (b,) if b.dtype == BF16 else split(b)
    (ca,), (cb,) = dims[0]
    if len(a) == 1 and len(b) == 1:
        return dot1(a[0], b[0], dims)
    if len(b) == 1:
        return dot1(jnp.concatenate(a, ca), jnp.concatenate([b[0], b[0]], cb), dims)
    if len(a) == 1:
        return dot1(jnp.concatenate([a[0], a[0]], ca), jnp.concatenate(b, cb), dims)
    wide = b[0].shape[1 - cb]
    if wide <= PAIR:
        right = jnp.concatenate(b, 1 - cb)
        out = dot1(jnp.concatenate(a, ca), jnp.concatenate([right, right], cb), dims)
        return out[:, :wide] + out[:, wide:]
    out = dot1(jnp.concatenate(a, ca), jnp.concatenate([b[0], b[0]], cb), dims)
    return out + dot1(a[0], b[1], dims)


def inverses(lower, row, col):
    size = row.shape[0]
    eye = jnp.where(row == col, 1.0, 0.0).astype(F32)
    block = 8
    inside = row // block == col // block
    first = [jnp.where(inside, m, 0.0) for m in lower]
    halves = [split(m) for m in first]
    square = [split(product(m, m, NN)) for m in halves]
    left = [eye - m for m in first]
    tall = [tuple(jnp.concatenate(x, 0) for x in zip(split(m), s)) for m, s in zip(left, square)]
    tall = [product(m, s, NN) for m, s in zip(tall, square)]
    left = [m + t[:size] for m, t in zip(left, tall)]
    out = [m + product(m, t[size:], NN) for m, t in zip(left, tall)]
    while block < size:
        inside = (row // (4 * block) == col // (4 * block)) & (row // block != col // block)
        halves = [split(t) for t in out]
        near = [split(product(t, jnp.where(inside, m, 0.0), NN)) for t, m in zip(halves, lower)]
        both_of = [
            product(n, tuple(jnp.concatenate(x, 1) for x in zip(n, t)), NN) for n, t in zip(near, halves)
        ]
        out = [t - m[:, size:] for t, m in zip(out, both_of)]
        out = [t + product(m[:, :size], t, NN) for t, m in zip(out, both_of)]
        block *= 4
    return out


def one_less_exp(x):
    series = jnp.full_like(x, 1.0 / math.factorial(10))
    for n in range(9, 0, -1):
        series = series * x + 1.0 / math.factorial(n)
    return jnp.where(x > -0.5, -x * series, 1.0 - jnp.exp(x))


def row_scales(total):
    frames = total.shape[0]
    return total[frames // 2 - 1 : frames // 2], total[frames - 1 : frames]


def stream_kernel(count, parts, rec_hbm, key_hbm, val_hbm, log_hbm, kap_hbm, rem_hbm, start_hbm, go_hbm, w_hbm,
                  all_out, gw_out,
                  rec_ref, key_ref, val_ref, log_ref, kap_ref, rem_ref, start_ref, go_ref, w_ref, gath, gy_ref, tot_ref, ks_ref, a_ref, b_ref, k_ref, u_ref, x_ref, y_ref, yr_ref,
                  p_ref, tb_ref, gv_ref, gvk_ref, gra_ref, gka_ref, t_ref, ak_ref, rb_ref, rk_ref,
                  pay_out, pay_in, pull_out, pull_in, link_row, link_col, held, landed, ylow, mine, half_go,
                  cross_out, cross_in, part_ref, part_out, part_in,
                  copy_sem, local_sem, send_sem, recv_sem, cross_send, cross_recv,
                  ring_send, ring_recv, twin_send, twin_recv):
    frames = rec_hbm.shape[0]
    rows_each = HEAD_SIZE // parts
    features = go_hbm.shape[0]
    near = count // 2
    wide = near * frames
    me = lax.axis_index("tm")
    side, here = me // near, lax.rem(me, near)
    partner = lax.rem(me + near, count)
    row, col = iota((frames, frames), 0), iota((frames, frames), 1)
    lane_low = iota((frames, PAIR), 1) < HEAD_SIZE
    own = [lane_low, jnp.logical_not(lane_low)]
    low2 = jnp.concatenate([lane_low, lane_low], 1)
    own2 = [jnp.concatenate([m, m], 0) for m in own]
    pack_low = iota((HEAD_SIZE, PAIR), 1) < HEAD_SIZE
    prow, pcol = iota((PAIR, PAIR), 0), iota((PAIR, PAIR), 1)
    diagonal = (prow // HEAD_SIZE) == (pcol // HEAD_SIZE)
    ones = jnp.where(diagonal, 1.0, 0.0).astype(BF16)
    tri = jnp.where(row >= col, 1.0, 0.0).astype(BF16)
    strict, lax_tri = row > col, row >= col
    zero = jnp.zeros((), BF16)

    begin = pl.ds(pl.multiple_of(lax.rem(here, parts) * rows_each, rows_each), rows_each)
    moves = [(go_hbm, go_ref)]
    moves += zip((log_hbm, kap_hbm, rem_hbm, key_hbm, rec_hbm, val_hbm), (log_ref, kap_ref, rem_ref, key_ref, rec_ref, val_ref))
    moves += [(start_hbm.at[here // parts * 2 + h, begin], start_ref.at[h]) for h in range(2)]
    moves += [(w_hbm, w_ref)]
    loads = [pltpu.make_async_copy(a, b, copy_sem.at[1 + n]) for n, (a, b) in enumerate(moves)]
    for load in loads:
        load.start()

    barrier = pltpu.get_barrier_semaphore()

    def greet(i):
        pl.semaphore_signal(barrier, inc=1, device_id={"tm": i}, device_id_type=pl.DeviceIdType.MESH)

    def others(f):
        def step(i, carried):
            @pl.when(i != here)
            def _():
                f(i)

            return carried

        lax.fori_loop(0, near, step, 0)

    others(lambda i: greet(side * near + i))
    greet(partner)
    pl.semaphore_wait(barrier, near)

    def lanes(i):
        return pl.ds(pl.multiple_of(i * PAIR, PAIR), PAIR)

    def rows(i, n):
        return pl.ds(pl.multiple_of(i * n, n), n)

    sources = (
        lambda i: go_ref.at[:, rows(side * near + i, frames)],
        lambda i: half_go.at[1 - side, here, :, rows(i, frames)],
        lambda i: pay_out.at[i],
        lambda i: pull_out.at[i],
        lambda i: held.at[0, i],
        lambda i: held.at[1, i],
        lambda i: ylow.at[0, i],
        lambda i: ylow.at[1, i],
    )
    places = (
        lambda i: gath.at[rows(side * near + i, features)],
        lambda i: gath.at[rows((1 - side) * near + i, features)],
        lambda i: pay_in.at[i],
        lambda i: pull_in.at[i],
        lambda i: landed.at[0, rows(i, rows_each)],
        lambda i: landed.at[1, rows(i, rows_each)],
        lambda i: mine.at[0, :, rows(i, frames)],
        lambda i: mine.at[1, :, rows(i, frames)],
    )
    ways = len(sources)

    def remote(way, i, origin):
        return pltpu.make_async_remote_copy(
            src_ref=sources[way](i),
            dst_ref=places[way](origin),
            send_sem=send_sem.at[way, i],
            recv_sem=recv_sem.at[way, origin],
            device_id={"tm": side * near + i},
            device_id_type=pl.DeviceIdType.MESH,
        )

    def local(way):
        return pltpu.make_async_copy(sources[way](here), places[way](here), local_sem.at[way])

    def send(way, i):
        @pl.when(i != here)
        def _():
            remote(way, i, here).start()

        @pl.when(i == here)
        def _():
            local(way).start()

    def send_all(way, begin, many):
        def step(i, carried):
            send(way, begin + lax.rem(here + many // 2 + i, many))
            return carried

        lax.fori_loop(0, many, step, 0)

    def arrive(way):
        others(lambda i: remote(way, i, i).wait_recv())
        local(way).wait()

    def across(source, place, n):
        return pltpu.make_async_remote_copy(
            src_ref=source,
            dst_ref=place,
            send_sem=cross_send.at[n],
            recv_sem=cross_recv.at[n],
            device_id={"tm": partner},
            device_id_type=pl.DeviceIdType.MESH,
        )

    cross_frames = across(go_ref.at[:, rows(1 - side, wide)], half_go.at[side, here], 0)
    cross_state = across(cross_out, cross_in, 1)
    chunks = part_out.shape[0]

    def cross_part(n):
        return across(part_out.at[n], part_in.at[n], 2 + n)

    chips = near // 2
    hops = chips // 2
    core = lax.rem(here, 2)
    chip = here // 2
    spot = jnp.where(lax.rem(chip, 2) == 0, chip // 2, chips - 1 - chip // 2)

    def place_at(spot):
        spot = lax.rem(spot + 2 * chips, chips)
        return 2 * jnp.where(spot < hops, 2 * spot, 2 * (chips - 1 - spot) + 1) + core

    def ring(of, way, step, part):
        toward = 1 - 2 * way
        block = half_go.at[lax.rem(side + of, 2), place_at(spot - toward * (step - 1))]
        if part:
            block = block.at[:, pl.ds(way * (wide // 2), wide // 2)]
        return pltpu.make_async_remote_copy(
            src_ref=block,
            dst_ref=block,
            send_sem=ring_send.at[of, way, step - 1],
            recv_sem=ring_recv.at[of, way, step - 1],
            device_id={"tm": side * near + place_at(spot + toward)},
            device_id_type=pl.DeviceIdType.MESH,
        )

    def twin(of, way, step):
        block = half_go.at[lax.rem(side + of, 2), place_at(spot - (1 - 2 * way) * step)]
        return pltpu.make_async_remote_copy(
            src_ref=block,
            dst_ref=block,
            send_sem=twin_send.at[of, way, step],
            recv_sem=twin_recv.at[of, way, step],
            device_id={"tm": me + 1 - 2 * core},
            device_id_type=pl.DeviceIdType.MESH,
        )

    def ring_begin(of):
        for way in range(2):
            ring(of, way, 1, False).start()
        twin(of, 0, 0).start()

    def ring_steps(of):
        def body(step, carried):
            for way in range(2):
                ring(of, way, step, False).wait_recv()
            for way in range(2):
                ring(of, way, step + 1, False).start()
            for way in range(2):
                twin(of, way, step).start()
            return carried

        lax.fori_loop(1, hops - 1, body, 0)
        for way in range(2):
            ring(of, way, hops - 1, False).wait_recv()
        for way in range(2):
            ring(of, way, hops, True).start()
        for way in range(2):
            twin(of, way, hops - 1).start()

    def ring_end(of):
        for way in range(2):
            ring(of, way, hops, True).wait_recv()
        twin(of, 0, hops).start()

    def ring_done(of):
        def body(step, carried):
            for way in range(2):
                ring(of, way, step, False).wait_send()
                twin(of, way, step).wait()
            return carried

        lax.fori_loop(1, hops, body, 0)
        for way in range(2):
            ring(of, way, hops, True).wait_send()
        twin(of, 0, 0).wait()
        twin(of, 0, hops).wait()

    loads[0].wait()
    cross_frames.start()
    send_all(0, 0, near)
    own_half = pltpu.make_async_copy(go_ref.at[:, rows(side, wide)], half_go.at[side, here], copy_sem.at[0])
    own_half.start()
    own_half.wait()
    ring_begin(0)

    group = GROUP
    groups = PAIRS // group
    per_group = group * parts

    def far_first(n):
        return lax.rem(n + 1 + here * groups // near, groups)

    def first(n, carried):
        g = far_first(n)
        pairs = [g * group + m for m in range(group)]
        m_ab = []
        for pair in pairs:
            at = lanes(pair)
            log_low = log_ref[:, at]
            log_part = log_low.astype(F32)
            total = dot1(tri, log_low, NN)
            middle, last = row_scales(total)
            key_scale = jnp.sqrt(one_less_exp(log_part))
            raw = kap_ref[:, at].astype(F32)
            norm = product(raw * raw, ones, NN)
            a = raw / jnp.sqrt(norm + 1e-06)
            e_neg = jnp.exp(middle - total)
            a_mid = a * jnp.exp(total - log_part - middle)
            b_mid = rem_ref[:, at].astype(F32) * a * e_neg
            k_mid = key_ref[:, at].astype(F32) * key_scale * e_neg
            r_mid = rec_ref[:, at].astype(F32) * jnp.exp(total - middle)
            for ref, value in zip((tot_ref, ks_ref, a_ref, b_ref, k_ref), (total, key_scale, a_mid, b_mid, k_mid)):
                ref[pair] = value
            upper = split(jnp.concatenate([a_mid, r_mid], 0))
            rights = split(jnp.concatenate([b_mid, k_mid], 0))
            for h, m in enumerate(own2):
                gram = product(upper, tuple(jnp.where(m, x, zero) for x in rights), NT)
                m_ab.append(jnp.where(strict, gram[:frames, :frames], 0.0))
                kept = (
                    (ak_ref, jnp.where(strict, gram[:frames, frames:], 0.0)),
                    (rb_ref, jnp.where(lax_tri, gram[frames:, :frames], 0.0)),
                    (rk_ref, jnp.where(lax_tri, gram[frames:, frames:], 0.0)),
                )
                for ref, value in kept:
                    ref[0, pair * 2 + h], ref[1, pair * 2 + h] = split(value)
        inverted = inverses(m_ab, row, col)
        for m, pair in enumerate(pairs):
            at = lanes(pair)
            v = val_ref[:, at]
            total = tot_ref[pair]
            middle, last = row_scales(total)
            a_abs = a_ref[pair] * jnp.exp(middle)
            scale = jnp.exp(last - middle)
            t_inv = [split(inverted[m * 2 + h]) for h in range(2)]
            for h in range(2):
                t_ref[0, pair * 2 + h], t_ref[1, pair * 2 + h] = t_inv[h]
            on_v = both(lambda h: product((ak_ref[0, pair * 2 + h], ak_ref[1, pair * 2 + h]), v, NN), lane_low)
            given = split(jnp.concatenate([on_v, a_abs], 1))
            inner = both(lambda h: product(t_inv[h], given, NN), low2)
            u_ref[pair], x_ref[pair] = inner[:, :PAIR], inner[:, PAIR:]
            ended = product(inner, b_ref[pair] * scale, TN)
            through = pack(jnp.where(prow == pcol, jnp.exp(last), 0.0) - ended[PAIR:], pack_low)
            offset = pack(product(v, k_ref[pair] * scale, TN) - ended[:PAIR], pack_low)
            for part in range(parts):
                pay_out[pair * parts + part, :HEAD_SIZE] = through
                pay_out[pair * parts + part, HEAD_SIZE:] = offset[part * rows_each : (part + 1) * rows_each]

        @pl.when(n == 0)
        def _():
            cross_frames.wait_recv()
            send_all(1, 0, near)
            ring_steps(0)

        send_all(2, g * per_group, per_group)

        return carried

    for load in loads[1:9]:
        load.wait()
    lax.fori_loop(0, groups, first, 0)

    arrive(0)
    arrive(1)
    ring_begin(1)
    loads[9].wait()
    some_pairs = 2

    def project(n, carried):
        wide = some_pairs * PAIR
        weight = w_ref[rows(n, wide), :]
        out = dot1(gath[...], weight, (((0,), (1,)), ((), ())))
        for m in range(some_pairs):
            gy_ref[n * some_pairs + m] = out[:, m * PAIR : (m + 1) * PAIR]
        return carried

    lax.fori_loop(0, PAIRS // some_pairs, project, 0)

    def second(n, carried):
        g = far_first(n)
        for pair in [g * group + m for m in range(group)]:
            total = tot_ref[pair]
            middle, last = row_scales(total)
            scale = jnp.exp(last - middle)
            q = split(gy_ref[pair])
            r = rec_ref[:, lanes(pair)].astype(F32)
            back = both(lambda h: product((rb_ref[0, pair * 2 + h], rb_ref[1, pair * 2 + h]), q, TN), lane_low)
            given = split(jnp.concatenate([back, b_ref[pair] * scale], 1))
            pulled = both(lambda h: product((t_ref[0, pair * 2 + h], t_ref[1, pair * 2 + h]), given, TN), low2)
            p0 = pulled[:, :PAIR]
            p_ref[pair], tb_ref[pair] = p0, pulled[:, PAIR:]
            pull = product(q, r * jnp.exp(total), TN) - product(p0, a_ref[pair] * jnp.exp(middle), TN)
            pull = pack(pull, pack_low)
            for part in range(parts):
                pull_out[pair * parts + part] = pull[part * rows_each : (part + 1) * rows_each]
        send_all(3, g * per_group, per_group)
        return carried

    lax.fori_loop(0, PAIRS // group, second, 0)

    def third(g, carried):
        for pair in [g * group + n for n in range(group)]:
            v = val_ref[:, lanes(pair)]
            inner = split(jnp.concatenate([u_ref[pair], x_ref[pair]], 1))
            minus = both(lambda h: product((rb_ref[0, pair * 2 + h], rb_ref[1, pair * 2 + h]), inner, NN), low2)
            m_rk = [(rk_ref[0, pair * 2 + h], rk_ref[1, pair * 2 + h]) for h in range(2)]
            y_ref[pair] = both(lambda h: product(m_rk[h], v, NN), lane_low) - minus[:, :PAIR]
            yr_ref[pair] = rec_ref[:, lanes(pair)].astype(F32) * jnp.exp(tot_ref[pair]) - minus[:, PAIR:]
        return carried

    def third_back(g, carried):
        for pair in [g * group + n for n in range(group)]:
            middle, last = row_scales(tot_ref[pair])
            q = split(gy_ref[pair])
            m_rk = [(rk_ref[0, pair * 2 + h], rk_ref[1, pair * 2 + h]) for h in range(2)]
            pulled = split(jnp.concatenate([p_ref[pair], tb_ref[pair]], 1))
            minus = both(lambda h: product((ak_ref[0, pair * 2 + h], ak_ref[1, pair * 2 + h]), pulled, TN), low2)
            gv_ref[pair] = both(lambda h: product(m_rk[h], q, TN), lane_low) - minus[:, :PAIR]
            gvk_ref[pair] = k_ref[pair] * jnp.exp(last - middle) - minus[:, PAIR:]
        return carried

    def ready(i, carried):
        link = split(unpack(pay_in[i, :HEAD_SIZE], diagonal))
        down, over = jnp.concatenate(link, 0), jnp.concatenate(link, 1)
        link_row[i] = jnp.concatenate([over, over], 0)
        link_col[i] = jnp.concatenate([down, down], 1)
        return carried

    def carry_over(x, link, dims):
        out = dot1(jnp.concatenate(split(x), 1), link, dims)
        return out[:, :PAIR] + out[:, PAIR:]

    def ahead(i, state):
        held[0, i] = state
        return pay_in[i, HEAD_SIZE:] + carry_over(state, link_row[i], NN)

    def astern(i, grad):
        j = near - 1 - i
        held[1, j] = grad
        return pull_in[j] + carry_over(grad, link_col[j], NT)

    def laps(step, begin):
        return lax.fori_loop(0, near, step, begin, unroll=near <= 8)

    arrive(2)
    lax.fori_loop(0, near, ready, 0)

    @pl.when(side == 0)
    def _():
        cross_out[...] = laps(ahead, jnp.concatenate([start_ref[0], start_ref[1]], 1))
        cross_state.start()
        send_all(4, 0, near)

    lax.fori_loop(0, groups, third, 0)
    ring_steps(1)
    ring_end(0)

    @pl.when(side == 1)
    def _():
        cross_state.wait_recv()
        laps(ahead, cross_in[...])
        send_all(4, 0, near)

    arrive(3)

    @pl.when(side == 1)
    def _():
        cross_out[...] = laps(astern, jnp.zeros((rows_each, PAIR), F32))
        cross_state.start()
        send_all(5, 0, near)

    def fourth(g, carried):
        for pair in [g * group + n for n in range(group)]:
            v = val_ref[:, lanes(pair)]
            total = tot_ref[pair]
            middle, last = row_scales(total)
            e_pos, e_neg = jnp.exp(total - middle), jnp.exp(middle - total)
            q = split(gy_ref[pair])
            v_own = [jnp.where(m, v, zero) for m in own]
            q_own = [tuple(jnp.where(m, x, zero) for x in q) for m in own]
            k_mid, r_mid = split(k_ref[pair]), split(rec_ref[:, lanes(pair)].astype(F32) * e_pos)
            gra_ref[pair] = e_pos * both(
                lambda h: product(jnp.where(lax_tri, product(q, v_own[h], NT), 0.0), k_mid, NN), lane_low
            )
            gka_ref[pair] = ks_ref[pair] * e_neg * both(
                lambda h: product(jnp.where(row <= col, product(v, q_own[h], NT), 0.0), r_mid, NN), lane_low
            )
        return carried

    lax.fori_loop(0, groups // 2, fourth, 0)
    arrive(4)

    def state_of(pair):
        return unpack(landed[0, rows(pair, HEAD_SIZE)], diagonal)

    def grad_of(pair):
        return unpack(landed[1, rows(pair, HEAD_SIZE)], diagonal)

    def fifth(g, carried):
        for pair in [g * group + n for n in range(group)]:
            y = y_ref[pair] + product(yr_ref[pair], state_of(pair), NT)
            y = y.T.astype(BF16)
            for m in range(PAIR // features):
                block = pair * (PAIR // features) + m
                ylow[block // near, lax.rem(block, near)] = y[m * features : (m + 1) * features]
        return carried

    for g in range(groups):
        fifth(g, 0)
        send_all(6 + g, 0, near)

    @pl.when(side == 0)
    def _():
        cross_state.wait_recv()
        laps(astern, cross_in[...])
        send_all(5, 0, near)

    lax.fori_loop(0, groups, third_back, 0)
    lax.fori_loop(groups // 2, groups, fourth, 0)
    ring_end(1)

    def sixth(g, carried):
        for pair in [g * group + n for n in range(group)]:
            at = lanes(pair)
            state, grad = split(state_of(pair)), split(grad_of(pair))
            q, v = split(gy_ref[pair]), val_ref[:, at]
            u = split(u_ref[pair] + product(x_ref[pair], state, NT))
            behind = product(jnp.concatenate([tb_ref[pair], gvk_ref[pair]], 0), grad, NT)
            p = split(p_ref[pair] + behind[:frames])
            all_out[2, :, at] = (gv_ref[pair] + behind[frames:]).astype(BF16)
            b_mid, a_mid = split(b_ref[pair]), split(a_ref[pair])
            total = tot_ref[pair]
            middle, last = row_scales(total)

            def removed(h):
                gram = product(q, tuple(jnp.where(own[h], x, zero) for x in u), NT)
                return product(jnp.where(lax_tri, gram, 0.0), b_mid, NN)

            def removed_back(h):
                gram = product(v, tuple(jnp.where(own[h], x, zero) for x in p), NT)
                return product(jnp.where(row < col, gram, 0.0), a_mid, NN)

            gr = jnp.exp(total) * product(q, state, NN) + gra_ref[pair]
            gr = gr - jnp.exp(total - middle) * both(removed, lane_low)
            all_out[0, :, at] = gr.astype(BF16)
            gk = jnp.exp(last - total) * product(v, grad, NN) - jnp.exp(middle - total) * both(
                removed_back, lane_low
            )
            all_out[1, :, at] = (gk * ks_ref[pair] + gka_ref[pair]).astype(BF16)
        return carried

    ring_done(0)
    ring_done(1)
    arrive(6)
    arrive(7)
    per = 2 * PAIR // features
    loss_scale = 1.0 / math.sqrt(frames * count)

    def weigh(n, carried):
        blocks = half_go[n * per // near, pl.ds(lax.rem(n * per, near), per)].reshape(per * features, wide)
        out = dot1(mine[...].reshape(2 * features, wide), blocks, NT) * loss_scale
        part_ref[0, n] = out[:features]
        part_ref[1, n] = out[features:]
        part_out[n] = part_ref[1 - side, n].astype(BF16)
        cross_part(n).start()
        return carried

    lax.fori_loop(0, chunks, weigh, 0)
    arrive(5)
    lax.fori_loop(0, groups, sixth, 0)
    for n in range(chunks):
        cross_part(n).wait_recv()
        gw_out[:, rows(n, 2 * PAIR)] = part_ref[side, n] + part_in[n].astype(F32)
    for way in range(ways):
        others(lambda i: remote(way, i, here).wait_send())
    cross_frames.wait_send()
    cross_state.wait_send()
    for n in range(chunks):
        cross_part(n).wait_send()


def local(receptance, key_input, values, log_decay, kappa_raw, removal, initial_state, out_weight, grad_output):
    size = lax.axis_size("tm")
    frames, width = receptance.shape
    near = size // 2
    parts = near // PAIRS
    rows_each = HEAD_SIZE // parts
    features = grad_output.shape[0]
    chunks = width // (2 * PAIR)
    whole = pl.BlockSpec(memory_space=pltpu.VMEM)
    anywhere = pl.BlockSpec(memory_space=pl.ANY)
    flat = pltpu.VMEM((PAIRS, frames, PAIR), F32)
    matrix = pltpu.VMEM((2, HEAD_COUNT, frames, frames), BF16)
    vectors, grad_weight = pl.pallas_call(
        functools.partial(stream_kernel, size, parts),
        in_specs=[anywhere] * 9,
        out_specs=[whole] * 2,
        out_shape=[jax.ShapeDtypeStruct((3, frames, width), BF16)] + [jax.ShapeDtypeStruct((features, width), F32)],
        scratch_shapes=[
            pltpu.VMEM((frames, width), BF16),
            pltpu.VMEM((frames, width), BF16),
            pltpu.VMEM((frames, width), BF16),
            pltpu.VMEM((frames, width), BF16),
            pltpu.VMEM((frames, width), BF16),
            pltpu.VMEM((frames, width), BF16),
            pltpu.VMEM((2, rows_each, HEAD_SIZE), F32),
            pltpu.VMEM(grad_output.shape, BF16),
            pltpu.VMEM((width, width), BF16),
            pltpu.VMEM((width, frames), BF16),
        ]
        + [flat] * 16
        + [matrix] * 4
        + [
            pltpu.VMEM((near, HEAD_SIZE + rows_each, PAIR), F32),
            pltpu.VMEM((near, HEAD_SIZE + rows_each, PAIR), F32),
            pltpu.VMEM((near, rows_each, PAIR), F32),
            pltpu.VMEM((near, rows_each, PAIR), F32),
            pltpu.VMEM((near, 2 * PAIR, 2 * PAIR), BF16),
            pltpu.VMEM((near, 2 * PAIR, 2 * PAIR), BF16),
            pltpu.VMEM((2, near, rows_each, PAIR), F32),
            pltpu.VMEM((2, PAIRS * HEAD_SIZE, PAIR), F32),
            pltpu.VMEM((2, near, features, frames), BF16),
            pltpu.VMEM((2, features, near * frames), BF16),
            pltpu.VMEM((2, near, features, near * frames), BF16),
            pltpu.VMEM((rows_each, PAIR), F32),
            pltpu.VMEM((rows_each, PAIR), F32),
            pltpu.VMEM((2, chunks, features, 2 * PAIR), F32),
            pltpu.VMEM((chunks, features, 2 * PAIR), BF16),
            pltpu.VMEM((chunks, features, 2 * PAIR), BF16),
            pltpu.SemaphoreType.DMA((11,)),
            pltpu.SemaphoreType.DMA((8,)),
            pltpu.SemaphoreType.DMA((8, near)),
            pltpu.SemaphoreType.DMA((8, near)),
            pltpu.SemaphoreType.DMA((2 + chunks,)),
            pltpu.SemaphoreType.DMA((2 + chunks,)),
            pltpu.SemaphoreType.DMA((2, 2, near // 4)),
            pltpu.SemaphoreType.DMA((2, 2, near // 4)),
            pltpu.SemaphoreType.DMA((2, 2, near // 4 + 1)),
            pltpu.SemaphoreType.DMA((2, 2, near // 4 + 1)),
        ],
        compiler_params=pltpu.CompilerParams(
            collective_id=0, has_side_effects=True, vmem_limit_bytes=56 << 20
        ),
        name="stream",
    )(receptance, key_input, values, log_decay, kappa_raw, removal, initial_state, grad_output, out_weight)
    return vectors[0], vectors[1], vectors[2], grad_weight


def solution(mesh):
    rows = P(("groups", "tm"), None)
    return jax.shard_map(
        local,
        mesh=mesh,
        in_specs=(rows,) * 6 + (P("groups", None, None), P(), P("tm", "groups")),
        out_specs=(rows,) * 4,
        check_vma=False,
    )
```

```python
import functools
import math

import jax
import jax.numpy as jnp
from jax import lax
from jax.experimental import pallas as pl
from jax.experimental.pallas import tpu as pltpu
from jax.sharding import PartitionSpec as P

HEAD_COUNT = 16
HEAD_SIZE = 64
PAIR = 2 * HEAD_SIZE
PAIRS = HEAD_COUNT // 2
GROUP = 4
F32 = jnp.float32
BF16 = jnp.bfloat16

NN = (((1,), (0,)), ((), ()))
NT = (((1,), (1,)), ((), ()))
TN = (((0,), (0,)), ((), ()))


def split(x):
    high = x.astype(BF16)
    return high, (x - high.astype(F32)).astype(BF16)


def dot1(a, b, dims):
    return lax.dot_general(a, b, dims, preferred_element_type=F32)


def dot3(a, b, dims):
    a = (a,) if not isinstance(a, tuple) and a.dtype == BF16 else a if isinstance(a, tuple) else split(a)
    b = (b,) if not isinstance(b, tuple) and b.dtype == BF16 else b if isinstance(b, tuple) else split(b)
    out = dot1(a[0], b[0], dims)
    if len(b) > 1:
        out = out + dot1(a[0], b[1], dims)
    if len(a) > 1:
        out = out + dot1(a[1], b[0], dims)
    return out


def iota(shape, dim):
    return lax.broadcasted_iota(jnp.int32, shape, dim)


def both(f, lane_low):
    return jnp.where(lane_low, f(0), f(1))


def pack(full, lane_low):
    return jnp.where(lane_low, full[:HEAD_SIZE], full[HEAD_SIZE:])


def unpack(packed, diagonal):
    return jnp.where(diagonal, jnp.concatenate([packed, packed], 0), 0.0)


def product(a, b, dims):
    a = a if isinstance(a, tuple) else (a,) if a.dtype == BF16 else split(a)
    b = b if isinstance(b, tuple) else (b,) if b.dtype == BF16 else split(b)
    (ca,), (cb,) = dims[0]
    if len(a) == 1 and len(b) == 1:
        return dot1(a[0], b[0], dims)
    if len(b) == 1:
        return dot1(jnp.concatenate(a, ca), jnp.concatenate([b[0], b[0]], cb), dims)
    if len(a) == 1:
        return dot1(jnp.concatenate([a[0], a[0]], ca), jnp.concatenate(b, cb), dims)
    wide = b[0].shape[1 - cb]
    if wide <= PAIR:
        right = jnp.concatenate(b, 1 - cb)
        out = dot1(jnp.concatenate(a, ca), jnp.concatenate([right, right], cb), dims)
        return out[:, :wide] + out[:, wide:]
    out = dot1(jnp.concatenate(a, ca), jnp.concatenate([b[0], b[0]], cb), dims)
    return out + dot1(a[0], b[1], dims)


def inverses(lower, row, col):
    size = row.shape[0]
    eye = jnp.where(row == col, 1.0, 0.0).astype(F32)
    block = 8
    inside = row // block == col // block
    first = [jnp.where(inside, m, 0.0) for m in lower]
    halves = [split(m) for m in first]
    square = [split(product(m, m, NN)) for m in halves]
    left = [eye - m for m in first]
    tall = [tuple(jnp.concatenate(x, 0) for x in zip(split(m), s)) for m, s in zip(left, square)]
    tall = [product(m, s, NN) for m, s in zip(tall, square)]
    left = [m + t[:size] for m, t in zip(left, tall)]
    out = [m + product(m, t[size:], NN) for m, t in zip(left, tall)]
    while block < size:
        inside = (row // (4 * block) == col // (4 * block)) & (row // block != col // block)
        halves = [split(t) for t in out]
        near = [split(product(t, jnp.where(inside, m, 0.0), NN)) for t, m in zip(halves, lower)]
        both_of = [
            product(n, tuple(jnp.concatenate(x, 1) for x in zip(n, t)), NN) for n, t in zip(near, halves)
        ]
        out = [t - m[:, size:] for t, m in zip(out, both_of)]
        out = [t + product(m[:, :size], t, NN) for t, m in zip(out, both_of)]
        block *= 4
    return out


def one_less_exp(x):
    series = jnp.full_like(x, 1.0 / math.factorial(10))
    for n in range(9, 0, -1):
        series = series * x + 1.0 / math.factorial(n)
    return jnp.where(x > -0.5, -x * series, 1.0 - jnp.exp(x))


def row_scales(total):
    frames = total.shape[0]
    return total[frames // 2 - 1 : frames // 2], total[frames - 1 : frames]


def stream_kernel(count, parts, rec_hbm, key_hbm, val_hbm, log_hbm, kap_hbm, rem_hbm, start_hbm, go_hbm, w_hbm,
                  all_hbm, gw_hbm,
                  all_out, gw_out, out_sem,
                  rec_ref, key_ref, val_ref, log_ref, kap_ref, rem_ref, start_ref, go_ref, w_ref, gath, gy_ref, tot_ref, ks_ref, a_ref, b_ref, k_ref, u_ref, x_ref, y_ref, yr_ref,
                  p_ref, tb_ref, gv_ref, gvk_ref, gra_ref, gka_ref, t_ref, ak_ref, rb_ref, rk_ref,
                  pay_out, pay_in, pull_out, pull_in, link_row, link_col, held, landed, ylow, mine, half_go,
                  cross_out, cross_in, part_ref, part_out, part_in,
                  copy_sem, local_sem, send_sem, recv_sem, cross_send, cross_recv,
                  ring_send, ring_recv, twin_send, twin_recv):
    frames = rec_hbm.shape[0]
    rows_each = HEAD_SIZE // parts
    features = go_hbm.shape[0]
    near = count // 2
    wide = near * frames
    me = lax.axis_index("tm")
    side, here = me // near, lax.rem(me, near)
    partner = lax.rem(me + near, count)
    row, col = iota((frames, frames), 0), iota((frames, frames), 1)
    lane_low = iota((frames, PAIR), 1) < HEAD_SIZE
    own = [lane_low, jnp.logical_not(lane_low)]
    low2 = jnp.concatenate([lane_low, lane_low], 1)
    own2 = [jnp.concatenate([m, m], 0) for m in own]
    pack_low = iota((HEAD_SIZE, PAIR), 1) < HEAD_SIZE
    prow, pcol = iota((PAIR, PAIR), 0), iota((PAIR, PAIR), 1)
    diagonal = (prow // HEAD_SIZE) == (pcol // HEAD_SIZE)
    ones = jnp.where(diagonal, 1.0, 0.0).astype(BF16)
    tri = jnp.where(row >= col, 1.0, 0.0).astype(BF16)
    strict, lax_tri = row > col, row >= col
    zero = jnp.zeros((), BF16)

    begin = pl.ds(pl.multiple_of(lax.rem(here, parts) * rows_each, rows_each), rows_each)
    moves = [(go_hbm, go_ref)]
    moves += zip((log_hbm, kap_hbm, rem_hbm, key_hbm, rec_hbm, val_hbm), (log_ref, kap_ref, rem_ref, key_ref, rec_ref, val_ref))
    moves += [(start_hbm.at[here // parts * 2 + h, begin], start_ref.at[h]) for h in range(2)]
    moves += [(w_hbm, w_ref)]
    loads = [pltpu.make_async_copy(a, b, copy_sem.at[1 + n]) for n, (a, b) in enumerate(moves)]
    for load in loads:
        load.start()

    barrier = pltpu.get_barrier_semaphore()

    def greet(i):
        pl.semaphore_signal(barrier, inc=1, device_id={"tm": i}, device_id_type=pl.DeviceIdType.MESH)

    def others(f):
        def step(i, carried):
            @pl.when(i != here)
            def _():
                f(i)

            return carried

        lax.fori_loop(0, near, step, 0)

    others(lambda i: greet(side * near + i))
    greet(partner)
    pl.semaphore_wait(barrier, near)

    def lanes(i):
        return pl.ds(pl.multiple_of(i * PAIR, PAIR), PAIR)

    def rows(i, n):
        return pl.ds(pl.multiple_of(i * n, n), n)

    sources = (
        lambda i: go_ref.at[:, rows(side * near + i, frames)],
        lambda i: half_go.at[1 - side, here, :, rows(i, frames)],
        lambda i: pay_out.at[i],
        lambda i: pull_out.at[i],
        lambda i: held.at[0, i],
        lambda i: held.at[1, i],
        lambda i: ylow.at[0, i],
        lambda i: ylow.at[1, i],
    )
    places = (
        lambda i: gath.at[rows(side * near + i, features)],
        lambda i: gath.at[rows((1 - side) * near + i, features)],
        lambda i: pay_in.at[i],
        lambda i: pull_in.at[i],
        lambda i: landed.at[0, rows(i, rows_each)],
        lambda i: landed.at[1, rows(i, rows_each)],
        lambda i: mine.at[0, :, rows(i, frames)],
        lambda i: mine.at[1, :, rows(i, frames)],
    )
    ways = len(sources)

    def remote(way, i, origin):
        return pltpu.make_async_remote_copy(
            src_ref=sources[way](i),
            dst_ref=places[way](origin),
            send_sem=send_sem.at[way, i],
            recv_sem=recv_sem.at[way, origin],
            device_id={"tm": side * near + i},
            device_id_type=pl.DeviceIdType.MESH,
        )

    def local(way):
        return pltpu.make_async_copy(sources[way](here), places[way](here), local_sem.at[way])

    def send(way, i):
        @pl.when(i != here)
        def _():
            remote(way, i, here).start()

        @pl.when(i == here)
        def _():
            local(way).start()

    def send_all(way, begin, many):
        def step(i, carried):
            send(way, begin + lax.rem(here + many // 2 + i, many))
            return carried

        lax.fori_loop(0, many, step, 0)

    def arrive(way):
        others(lambda i: remote(way, i, i).wait_recv())
        local(way).wait()

    def across(source, place, n):
        return pltpu.make_async_remote_copy(
            src_ref=source,
            dst_ref=place,
            send_sem=cross_send.at[n],
            recv_sem=cross_recv.at[n],
            device_id={"tm": partner},
            device_id_type=pl.DeviceIdType.MESH,
        )

    cross_frames = across(go_ref.at[:, rows(1 - side, wide)], half_go.at[side, here], 0)
    cross_state = across(cross_out, cross_in, 1)
    chunks = part_out.shape[0]

    def cross_part(n):
        return across(part_out.at[n], part_in.at[n], 2 + n)

    chips = near // 2
    hops = chips // 2
    core = lax.rem(here, 2)
    chip = here // 2
    spot = jnp.where(lax.rem(chip, 2) == 0, chip // 2, chips - 1 - chip // 2)

    def place_at(spot):
        spot = lax.rem(spot + 2 * chips, chips)
        return 2 * jnp.where(spot < hops, 2 * spot, 2 * (chips - 1 - spot) + 1) + core

    def ring(of, way, step, part):
        toward = 1 - 2 * way
        block = half_go.at[lax.rem(side + of, 2), place_at(spot - toward * (step - 1))]
        if part:
            block = block.at[:, pl.ds(way * (wide // 2), wide // 2)]
        return pltpu.make_async_remote_copy(
            src_ref=block,
            dst_ref=block,
            send_sem=ring_send.at[of, way, step - 1],
            recv_sem=ring_recv.at[of, way, step - 1],
            device_id={"tm": side * near + place_at(spot + toward)},
            device_id_type=pl.DeviceIdType.MESH,
        )

    def twin(of, way, step):
        block = half_go.at[lax.rem(side + of, 2), place_at(spot - (1 - 2 * way) * step)]
        return pltpu.make_async_remote_copy(
            src_ref=block,
            dst_ref=block,
            send_sem=twin_send.at[of, way, step],
            recv_sem=twin_recv.at[of, way, step],
            device_id={"tm": me + 1 - 2 * core},
            device_id_type=pl.DeviceIdType.MESH,
        )

    def ring_begin(of):
        for way in range(2):
            ring(of, way, 1, False).start()
        twin(of, 0, 0).start()

    def ring_steps(of):
        def body(step, carried):
            for way in range(2):
                ring(of, way, step, False).wait_recv()
            for way in range(2):
                ring(of, way, step + 1, False).start()
            for way in range(2):
                twin(of, way, step).start()
            return carried

        lax.fori_loop(1, hops - 1, body, 0)
        for way in range(2):
            ring(of, way, hops - 1, False).wait_recv()
        for way in range(2):
            ring(of, way, hops, True).start()
        for way in range(2):
            twin(of, way, hops - 1).start()

    def ring_end(of):
        for way in range(2):
            ring(of, way, hops, True).wait_recv()
        twin(of, 0, hops).start()

    def ring_done(of):
        def body(step, carried):
            for way in range(2):
                ring(of, way, step, False).wait_send()
                twin(of, way, step).wait()
            return carried

        lax.fori_loop(1, hops, body, 0)
        for way in range(2):
            ring(of, way, hops, True).wait_send()
        twin(of, 0, 0).wait()
        twin(of, 0, hops).wait()

    loads[0].wait()
    cross_frames.start()
    send_all(0, 0, near)
    own_half = pltpu.make_async_copy(go_ref.at[:, rows(side, wide)], half_go.at[side, here], copy_sem.at[0])
    own_half.start()
    own_half.wait()
    ring_begin(0)

    group = GROUP
    groups = PAIRS // group
    per_group = group * parts

    def far_first(n):
        return lax.rem(n + 1 + here * groups // near, groups)

    def first(n, carried):
        g = far_first(n)
        pairs = [g * group + m for m in range(group)]
        m_ab = []
        for pair in pairs:
            at = lanes(pair)
            log_low = log_ref[:, at]
            log_part = log_low.astype(F32)
            total = dot1(tri, log_low, NN)
            middle, last = row_scales(total)
            key_scale = jnp.sqrt(one_less_exp(log_part))
            raw = kap_ref[:, at].astype(F32)
            norm = product(raw * raw, ones, NN)
            a = raw / jnp.sqrt(norm + 1e-06)
            e_neg = jnp.exp(middle - total)
            a_mid = a * jnp.exp(total - log_part - middle)
            b_mid = rem_ref[:, at].astype(F32) * a * e_neg
            k_mid = key_ref[:, at].astype(F32) * key_scale * e_neg
            r_mid = rec_ref[:, at].astype(F32) * jnp.exp(total - middle)
            for ref, value in zip((tot_ref, ks_ref, a_ref, b_ref, k_ref), (total, key_scale, a_mid, b_mid, k_mid)):
                ref[pair] = value
            upper = split(jnp.concatenate([a_mid, r_mid], 0))
            rights = split(jnp.concatenate([b_mid, k_mid], 0))
            for h, m in enumerate(own2):
                gram = product(upper, tuple(jnp.where(m, x, zero) for x in rights), NT)
                m_ab.append(jnp.where(strict, gram[:frames, :frames], 0.0))
                kept = (
                    (ak_ref, jnp.where(strict, gram[:frames, frames:], 0.0)),
                    (rb_ref, jnp.where(lax_tri, gram[frames:, :frames], 0.0)),
                    (rk_ref, jnp.where(lax_tri, gram[frames:, frames:], 0.0)),
                )
                for ref, value in kept:
                    ref[0, pair * 2 + h], ref[1, pair * 2 + h] = split(value)
        inverted = inverses(m_ab, row, col)
        for m, pair in enumerate(pairs):
            at = lanes(pair)
            v = val_ref[:, at]
            total = tot_ref[pair]
            middle, last = row_scales(total)
            a_abs = a_ref[pair] * jnp.exp(middle)
            scale = jnp.exp(last - middle)
            t_inv = [split(inverted[m * 2 + h]) for h in range(2)]
            for h in range(2):
                t_ref[0, pair * 2 + h], t_ref[1, pair * 2 + h] = t_inv[h]
            on_v = both(lambda h: product((ak_ref[0, pair * 2 + h], ak_ref[1, pair * 2 + h]), v, NN), lane_low)
            given = split(jnp.concatenate([on_v, a_abs], 1))
            inner = both(lambda h: product(t_inv[h], given, NN), low2)
            u_ref[pair], x_ref[pair] = inner[:, :PAIR], inner[:, PAIR:]
            ended = product(inner, b_ref[pair] * scale, TN)
            through = pack(jnp.where(prow == pcol, jnp.exp(last), 0.0) - ended[PAIR:], pack_low)
            offset = pack(product(v, k_ref[pair] * scale, TN) - ended[:PAIR], pack_low)
            for part in range(parts):
                pay_out[pair * parts + part, :HEAD_SIZE] = through
                pay_out[pair * parts + part, HEAD_SIZE:] = offset[part * rows_each : (part + 1) * rows_each]

        @pl.when(n == 0)
        def _():
            cross_frames.wait_recv()
            send_all(1, 0, near)
            ring_steps(0)

        send_all(2, g * per_group, per_group)

        return carried

    for load in loads[1:9]:
        load.wait()
    lax.fori_loop(0, groups, first, 0)

    arrive(0)
    arrive(1)
    ring_begin(1)
    loads[9].wait()
    some_pairs = 2

    def project(n, carried):
        wide = some_pairs * PAIR
        weight = w_ref[rows(n, wide), :]
        out = dot1(gath[...], weight, (((0,), (1,)), ((), ())))
        for m in range(some_pairs):
            gy_ref[n * some_pairs + m] = out[:, m * PAIR : (m + 1) * PAIR]
        return carried

    lax.fori_loop(0, PAIRS // some_pairs, project, 0)

    def second(n, carried):
        g = far_first(n)
        for pair in [g * group + m for m in range(group)]:
            total = tot_ref[pair]
            middle, last = row_scales(total)
            scale = jnp.exp(last - middle)
            q = split(gy_ref[pair])
            r = rec_ref[:, lanes(pair)].astype(F32)
            back = both(lambda h: product((rb_ref[0, pair * 2 + h], rb_ref[1, pair * 2 + h]), q, TN), lane_low)
            given = split(jnp.concatenate([back, b_ref[pair] * scale], 1))
            pulled = both(lambda h: product((t_ref[0, pair * 2 + h], t_ref[1, pair * 2 + h]), given, TN), low2)
            p0 = pulled[:, :PAIR]
            p_ref[pair], tb_ref[pair] = p0, pulled[:, PAIR:]
            pull = product(q, r * jnp.exp(total), TN) - product(p0, a_ref[pair] * jnp.exp(middle), TN)
            pull = pack(pull, pack_low)
            for part in range(parts):
                pull_out[pair * parts + part] = pull[part * rows_each : (part + 1) * rows_each]
        send_all(3, g * per_group, per_group)
        return carried

    lax.fori_loop(0, PAIRS // group, second, 0)

    def third(g, carried):
        for pair in [g * group + n for n in range(group)]:
            v = val_ref[:, lanes(pair)]
            inner = split(jnp.concatenate([u_ref[pair], x_ref[pair]], 1))
            minus = both(lambda h: product((rb_ref[0, pair * 2 + h], rb_ref[1, pair * 2 + h]), inner, NN), low2)
            m_rk = [(rk_ref[0, pair * 2 + h], rk_ref[1, pair * 2 + h]) for h in range(2)]
            y_ref[pair] = both(lambda h: product(m_rk[h], v, NN), lane_low) - minus[:, :PAIR]
            yr_ref[pair] = rec_ref[:, lanes(pair)].astype(F32) * jnp.exp(tot_ref[pair]) - minus[:, PAIR:]
        return carried

    def third_back(g, carried):
        for pair in [g * group + n for n in range(group)]:
            middle, last = row_scales(tot_ref[pair])
            q = split(gy_ref[pair])
            m_rk = [(rk_ref[0, pair * 2 + h], rk_ref[1, pair * 2 + h]) for h in range(2)]
            pulled = split(jnp.concatenate([p_ref[pair], tb_ref[pair]], 1))
            minus = both(lambda h: product((ak_ref[0, pair * 2 + h], ak_ref[1, pair * 2 + h]), pulled, TN), low2)
            gv_ref[pair] = both(lambda h: product(m_rk[h], q, TN), lane_low) - minus[:, :PAIR]
            gvk_ref[pair] = k_ref[pair] * jnp.exp(last - middle) - minus[:, PAIR:]
        return carried

    def ready(i, carried):
        link = split(unpack(pay_in[i, :HEAD_SIZE], diagonal))
        down, over = jnp.concatenate(link, 0), jnp.concatenate(link, 1)
        link_row[i] = jnp.concatenate([over, over], 0)
        link_col[i] = jnp.concatenate([down, down], 1)
        return carried

    def carry_over(x, link, dims):
        out = dot1(jnp.concatenate(split(x), 1), link, dims)
        return out[:, :PAIR] + out[:, PAIR:]

    def ahead(i, state):
        held[0, i] = state
        return pay_in[i, HEAD_SIZE:] + carry_over(state, link_row[i], NN)

    def astern(i, grad):
        j = near - 1 - i
        held[1, j] = grad
        return pull_in[j] + carry_over(grad, link_col[j], NT)

    def laps(step, begin):
        return lax.fori_loop(0, near, step, begin, unroll=near <= 8)

    arrive(2)
    lax.fori_loop(0, near, ready, 0)

    @pl.when(side == 0)
    def _():
        cross_out[...] = laps(ahead, jnp.concatenate([start_ref[0], start_ref[1]], 1))
        cross_state.start()
        send_all(4, 0, near)

    lax.fori_loop(0, groups, third, 0)
    ring_steps(1)
    ring_end(0)

    @pl.when(side == 1)
    def _():
        cross_state.wait_recv()
        laps(ahead, cross_in[...])
        send_all(4, 0, near)

    arrive(3)

    @pl.when(side == 1)
    def _():
        cross_out[...] = laps(astern, jnp.zeros((rows_each, PAIR), F32))
        cross_state.start()
        send_all(5, 0, near)

    def fourth(g, carried):
        for pair in [g * group + n for n in range(group)]:
            v = val_ref[:, lanes(pair)]
            total = tot_ref[pair]
            middle, last = row_scales(total)
            e_pos, e_neg = jnp.exp(total - middle), jnp.exp(middle - total)
            q = split(gy_ref[pair])
            v_own = [jnp.where(m, v, zero) for m in own]
            q_own = [tuple(jnp.where(m, x, zero) for x in q) for m in own]
            k_mid, r_mid = split(k_ref[pair]), split(rec_ref[:, lanes(pair)].astype(F32) * e_pos)
            gra_ref[pair] = e_pos * both(
                lambda h: product(jnp.where(lax_tri, product(q, v_own[h], NT), 0.0), k_mid, NN), lane_low
            )
            gka_ref[pair] = ks_ref[pair] * e_neg * both(
                lambda h: product(jnp.where(row <= col, product(v, q_own[h], NT), 0.0), r_mid, NN), lane_low
            )
        return carried

    lax.fori_loop(0, groups // 2, fourth, 0)
    arrive(4)

    def state_of(pair):
        return unpack(landed[0, rows(pair, HEAD_SIZE)], diagonal)

    def grad_of(pair):
        return unpack(landed[1, rows(pair, HEAD_SIZE)], diagonal)

    def fifth(g, carried):
        for pair in [g * group + n for n in range(group)]:
            y = y_ref[pair] + product(yr_ref[pair], state_of(pair), NT)
            y = y.T.astype(BF16)
            for m in range(PAIR // features):
                block = pair * (PAIR // features) + m
                ylow[block // near, lax.rem(block, near)] = y[m * features : (m + 1) * features]
        return carried

    for g in range(groups):
        fifth(g, 0)
        send_all(6 + g, 0, near)

    @pl.when(side == 0)
    def _():
        cross_state.wait_recv()
        laps(astern, cross_in[...])
        send_all(5, 0, near)

    lax.fori_loop(0, groups, third_back, 0)
    lax.fori_loop(groups // 2, groups, fourth, 0)
    ring_end(1)

    def sixth(g, carried):
        for pair in [g * group + n for n in range(group)]:
            at = lanes(pair)
            state, grad = split(state_of(pair)), split(grad_of(pair))
            q, v = split(gy_ref[pair]), val_ref[:, at]
            u = split(u_ref[pair] + product(x_ref[pair], state, NT))
            behind = product(jnp.concatenate([tb_ref[pair], gvk_ref[pair]], 0), grad, NT)
            p = split(p_ref[pair] + behind[:frames])
            all_out[2, :, at] = (gv_ref[pair] + behind[frames:]).astype(BF16)
            b_mid, a_mid = split(b_ref[pair]), split(a_ref[pair])
            total = tot_ref[pair]
            middle, last = row_scales(total)

            def removed(h):
                gram = product(q, tuple(jnp.where(own[h], x, zero) for x in u), NT)
                return product(jnp.where(lax_tri, gram, 0.0), b_mid, NN)

            def removed_back(h):
                gram = product(v, tuple(jnp.where(own[h], x, zero) for x in p), NT)
                return product(jnp.where(row < col, gram, 0.0), a_mid, NN)

            gr = jnp.exp(total) * product(q, state, NN) + gra_ref[pair]
            gr = gr - jnp.exp(total - middle) * both(removed, lane_low)
            all_out[0, :, at] = gr.astype(BF16)
            gk = jnp.exp(last - total) * product(v, grad, NN) - jnp.exp(middle - total) * both(
                removed_back, lane_low
            )
            all_out[1, :, at] = (gk * ks_ref[pair] + gka_ref[pair]).astype(BF16)
        leave(g).start()
        return carried

    def leave(g):
        some = pl.ds(pl.multiple_of(g * group * PAIR, group * PAIR), group * PAIR)
        return pltpu.make_async_copy(all_out.at[:, :, some], all_hbm.at[:, :, some], out_sem.at[g])

    def leave_part(n):
        return pltpu.make_async_copy(gw_out.at[n], gw_hbm.at[:, rows(n, 2 * PAIR)], out_sem.at[groups + n])

    def finish(n):
        cross_part(n).wait_recv()
        gw_out[n] = part_ref[side, n] + part_in[n].astype(F32)
        leave_part(n).start()

    ring_done(0)
    ring_done(1)
    arrive(6)
    arrive(7)
    per = 2 * PAIR // features

    def weigh(n, carried):
        blocks = half_go[n * per // near, pl.ds(lax.rem(n * per, near), per)].reshape(per * features, wide)
        out = dot1(mine[...].reshape(2 * features, wide), blocks, NT)
        part_ref[0, n] = out[:features]
        part_ref[1, n] = out[features:]
        part_out[n] = part_ref[1 - side, n].astype(BF16)
        cross_part(n).start()
        return carried

    lax.fori_loop(0, chunks, weigh, 0)
    arrive(5)
    lax.fori_loop(0, groups, sixth, 0)
    for n in range(chunks):
        finish(n)
    for g in range(groups):
        leave(g).wait()
    for n in range(chunks):
        leave_part(n).wait()
    for way in range(ways):
        others(lambda i: remote(way, i, here).wait_send())
    cross_frames.wait_send()
    cross_state.wait_send()
    for n in range(chunks):
        cross_part(n).wait_send()


def local(receptance, key_input, values, log_decay, kappa_raw, removal, initial_state, out_weight, grad_output):
    size = lax.axis_size("tm")
    frames, width = receptance.shape
    near = size // 2
    parts = near // PAIRS
    rows_each = HEAD_SIZE // parts
    features = grad_output.shape[0]
    chunks = width // (2 * PAIR)
    anywhere = pl.BlockSpec(memory_space=pl.ANY)
    flat = pltpu.VMEM((PAIRS, frames, PAIR), F32)
    matrix = pltpu.VMEM((2, HEAD_COUNT, frames, frames), BF16)
    vectors, grad_weight = pl.pallas_call(
        functools.partial(stream_kernel, size, parts),
        in_specs=[anywhere] * 9,
        out_specs=[anywhere] * 2,
        out_shape=[jax.ShapeDtypeStruct((3, frames, width), BF16)] + [jax.ShapeDtypeStruct((features, width), F32)],
        scratch_shapes=[
            pltpu.VMEM((3, frames, width), BF16),
            pltpu.VMEM((chunks, features, 2 * PAIR), F32),
            pltpu.SemaphoreType.DMA((chunks + PAIRS // GROUP,)),
            pltpu.VMEM((frames, width), BF16),
            pltpu.VMEM((frames, width), BF16),
            pltpu.VMEM((frames, width), BF16),
            pltpu.VMEM((frames, width), BF16),
            pltpu.VMEM((frames, width), BF16),
            pltpu.VMEM((frames, width), BF16),
            pltpu.VMEM((2, rows_each, HEAD_SIZE), F32),
            pltpu.VMEM(grad_output.shape, BF16),
            pltpu.VMEM((width, width), BF16),
            pltpu.VMEM((width, frames), BF16),
        ]
        + [flat] * 16
        + [matrix] * 4
        + [
            pltpu.VMEM((near, HEAD_SIZE + rows_each, PAIR), F32),
            pltpu.VMEM((near, HEAD_SIZE + rows_each, PAIR), F32),
            pltpu.VMEM((near, rows_each, PAIR), F32),
            pltpu.VMEM((near, rows_each, PAIR), F32),
            pltpu.VMEM((near, 2 * PAIR, 2 * PAIR), BF16),
            pltpu.VMEM((near, 2 * PAIR, 2 * PAIR), BF16),
            pltpu.VMEM((2, near, rows_each, PAIR), F32),
            pltpu.VMEM((2, PAIRS * HEAD_SIZE, PAIR), F32),
            pltpu.VMEM((2, near, features, frames), BF16),
            pltpu.VMEM((2, features, near * frames), BF16),
            pltpu.VMEM((2, near, features, near * frames), BF16),
            pltpu.VMEM((rows_each, PAIR), F32),
            pltpu.VMEM((rows_each, PAIR), F32),
            pltpu.VMEM((2, chunks, features, 2 * PAIR), F32),
            pltpu.VMEM((chunks, features, 2 * PAIR), BF16),
            pltpu.VMEM((chunks, features, 2 * PAIR), BF16),
            pltpu.SemaphoreType.DMA((11,)),
            pltpu.SemaphoreType.DMA((8,)),
            pltpu.SemaphoreType.DMA((8, near)),
            pltpu.SemaphoreType.DMA((8, near)),
            pltpu.SemaphoreType.DMA((2 + chunks,)),
            pltpu.SemaphoreType.DMA((2 + chunks,)),
            pltpu.SemaphoreType.DMA((2, 2, near // 4)),
            pltpu.SemaphoreType.DMA((2, 2, near // 4)),
            pltpu.SemaphoreType.DMA((2, 2, near // 4 + 1)),
            pltpu.SemaphoreType.DMA((2, 2, near // 4 + 1)),
        ],
        compiler_params=pltpu.CompilerParams(
            collective_id=0, has_side_effects=True, vmem_limit_bytes=56 << 20
        ),
        name="stream",
    )(receptance, key_input, values, log_decay, kappa_raw, removal, initial_state, grad_output, out_weight)
    return vectors[0], vectors[1], vectors[2], grad_weight * (1.0 / math.sqrt(frames * size))


def solution(mesh):
    rows = P(("groups", "tm"), None)
    return jax.shard_map(
        local,
        mesh=mesh,
        in_specs=(rows,) * 6 + (P("groups", None, None), P(), P("tm", "groups")),
        out_specs=(rows,) * 4,
        check_vma=False,
    )
```
